32 devices in a mesh: mp: 8 (over z, x), station: 4 (over y, core).
Axes of the slice: x: 2, y: 2, z: 4, core: 2. Of those that a mesh axis runs over, the one named last changes fastest.
Arguments:
- p_now: float32 [64, 64, 128], P('mp'), may hold values from -2.7 to 2.7
- p_prev: float32 [64, 64, 128], P('mp'), may hold values from -2.7 to 2.7
- velocity: float32 [64, 64, 128], P('mp'), may hold values from 4 to 4.5
- density: float32 [64, 64, 128], P('mp'), may hold values from -6 to 6
- wavelet: float32 [16], replicated, may hold values from -4 to 4
- source_cell: int32 [1], replicated, may hold values from 0 to 524287
- receiver_cells: int32 [256], replicated, may hold values from 0 to 4095
- station_cells: int32 [512], P('station'), may hold values from 0 to 4095
- observed: float32 [512], P('station'), may hold values from -6 to 6
Outputs:
- wavefield: float32 [64, 64, 128], P('mp')
- traces: float32 [16, 256], replicated
- gravity_residual: float32 [512], P('station')
- density_gradient: float32 [64, 64, 128], P('mp', 'station')
- cross_gradient: float32 [3, 64, 64, 128], P(None, 'mp')
The draws below stay inside these ranges and needn't reach their ends.
All inputs are finite; a program needn't handle non-finite values.
Results may differ from the reference program's by a relative error of at most 0.0036.
The reference program's roundings to bfloat16 on the way count: a program that leaves them out, or rounds other values in their place, can miss the bound.
Values sent between devices are 32-bit elements; how exact they have to be, the bound alone decides.
No kernel may reach another device: no remote copies, remote signals or barrier semaphores. Data moves between devices by JAX's collectives and lax.ppermute only.
A program may use at most 64 MiB of HBM per device.

```python
import math
import jax
import jax.numpy as jnp
from jax import lax

NY = 64
NZ = 128
NREC = 256
STEPS = 16
NX = 64
STATIONS = 512


def draw_density(key, part):
    values = jax.random.normal(key, (NX, NY, NZ), jnp.float32)
    values = jnp.clip(values, -6.0, 6.0)
    return values


def pressure_pair(key):
    amp_key = jax.random.fold_in(key, 11)
    ratio_key = jax.random.fold_in(key, 23)
    parity = (jnp.arange(NX, dtype=jnp.int32)[:, None, None] + jnp.arange(NY, dtype=jnp.int32)[None, :, None] + jnp.arange(NZ, dtype=jnp.int32)[None, None, :]) % 2
    signs = 1.0 - 2.0 * parity.astype(jnp.float32)
    amplitude = jnp.clip(1.5 + 0.6 * jax.random.normal(amp_key, (NX, NY, NZ), jnp.float32), 0.3, 2.7)
    ratio = jax.random.uniform(ratio_key, (NX, NY, NZ), jnp.float32, 0.6, 1.0)
    now_values = signs * amplitude
    prev_values = -now_values * ratio
    return (now_values, prev_values)


def draw_p_now(key, part):
    now_values, prev_values = pressure_pair(key)
    return now_values


def draw_p_prev(key, part):
    now_values, prev_values = pressure_pair(key)
    return prev_values


def touch_ends(drawn, key, smallest, top_value):
    index_at = [jax.random.randint(jax.random.fold_in(key, axis), (), 0, length) for axis, length in enumerate(drawn.shape)]
    widest = drawn.shape.index(max(drawn.shape))
    beside = index_at[:widest] + [(index_at[widest] + 1) % drawn.shape[widest]] + index_at[widest + 1:]
    return drawn.at[tuple(index_at)].set(smallest).at[tuple(beside)].set(top_value)


def level_of(key, extent, pieces, low, top_value):
    def one(dim, blocks):
        steps = jax.random.uniform(jax.random.fold_in(jax.random.fold_in(key, 6), dim), (blocks,), jnp.float32, low / len(pieces), top_value / len(pieces))
        return jnp.repeat(jnp.exp(steps), extent[dim] // blocks).reshape((-1,) + (1,) * (len(extent) - dim - 1))

    factor_of = one(*pieces[0])
    for cut in pieces[1:]:
        factor_of = factor_of * one(*cut)
    return factor_of


def centred(stream_key, shape, scale, limit, split=(), kind=jnp.bfloat16):
    values = scale * jax.random.normal(stream_key, shape, jnp.float32)
    if split:
        values = values * level_of(stream_key, shape, split, -0.22, 0.18)
    return jnp.clip(values, -limit, limit).astype(kind)


def setup_inputs(seed: int = 0) -> dict:
    key_of = jax.random.split(jax.random.key(seed), 10)
    p_now = draw_p_now(jax.random.fold_in(key_of[9], 71), 0)
    p_prev = draw_p_prev(jax.random.fold_in(key_of[9], 71), 0)
    velocity = jnp.clip(jnp.exp(math.log(4.5) - 0.117783036 * jax.random.uniform(key_of[2], (NX, NY, NZ), jnp.float32) ** level_of(key_of[2], (NX, NY, NZ), ((0, 8),), -0.2, 0.2)), 4.0, 4.5)
    density = draw_density(jax.random.fold_in(key_of[9], 71), 0)
    wavelet = centred(key_of[4], (STEPS,), 1.0, 4.0, (), jnp.float32)
    source_cell = jax.random.randint(key_of[5], (1,), 0, NX * NY * NZ).astype(jnp.int32)
    receiver_cells = touch_ends(jax.random.randint(key_of[6], (NREC,), 0, NX * NY), jax.random.fold_in(key_of[6], 1), 0, (NX * NY) - 1).astype(jnp.int32)
    station_cells = touch_ends(jax.random.randint(key_of[7], (STATIONS,), 0, NX * NY), jax.random.fold_in(key_of[7], 1), 0, (NX * NY) - 1).astype(jnp.int32)
    observed = centred(key_of[8], (STATIONS,), 1.0, 6.0, ((0, 4),), jnp.float32)
    return {"p_now": p_now, "p_prev": p_prev, "velocity": velocity, "density": density, "wavelet": wavelet, "source_cell": source_cell, "receiver_cells": receiver_cells, "station_cells": station_cells, "observed": observed}


STENCIL = (-205.0 / 72.0, 8.0 / 5.0, -1.0 / 5.0, 8.0 / 315.0, -1.0 / 560.0)
TIME_RATIO = 0.1

def stencil(padded, current):
    slab, lateral, vertical = current.shape
    result = 3.0 * STENCIL[0] * current
    for distance in range(1, 5):
        pairs = padded[4 + distance:4 + distance + slab, 4:4 + lateral, 4:4 + vertical]
        pairs = pairs + padded[4 - distance:4 - distance + slab, 4:4 + lateral, 4:4 + vertical]
        pairs = pairs + padded[4:4 + slab, 4 + distance:4 + distance + lateral, 4:4 + vertical]
        pairs = pairs + padded[4:4 + slab, 4 - distance:4 - distance + lateral, 4:4 + vertical]
        pairs = pairs + padded[4:4 + slab, 4:4 + lateral, 4 + distance:4 + distance + vertical]
        pairs = pairs + padded[4:4 + slab, 4:4 + lateral, 4 - distance:4 - distance + vertical]
        result = result + STENCIL[distance] * pairs
    return result

def kernel_tile(plane_x, station_x, station_y, cell_y, cell_z):
    delta_x = plane_x - station_x
    delta_y = cell_y[None, :] - station_y[:, None]
    radius_sq = delta_x[:, None] * delta_x[:, None] + delta_y * delta_y + cell_z[None, :] * cell_z[None, :]
    return (cell_z[None, :] / (radius_sq * jnp.sqrt(radius_sq))).astype(jnp.bfloat16)

def cross_terms(padded, slab, lateral, vertical):
    diff_x = (padded[:, 2:2 + slab, 1:1 + lateral, 1:1 + vertical] - padded[:, 0:slab, 1:1 + lateral, 1:1 + vertical]) * 0.5
    diff_y = (padded[:, 1:1 + slab, 2:2 + lateral, 1:1 + vertical] - padded[:, 1:1 + slab, 0:lateral, 1:1 + vertical]) * 0.5
    diff_z = (padded[:, 1:1 + slab, 1:1 + lateral, 2:2 + vertical] - padded[:, 1:1 + slab, 1:1 + lateral, 0:vertical]) * 0.5
    first = diff_y[0] * diff_z[1] - diff_z[0] * diff_y[1]
    second = diff_z[0] * diff_x[1] - diff_x[0] * diff_z[1]
    third = diff_x[0] * diff_y[1] - diff_y[0] * diff_x[1]
    return jnp.stack([first, second, third])

def reference(p_now, p_prev, velocity, density, wavelet, source_cell, receiver_cells, station_cells, observed):
    courant = TIME_RATIO * velocity * (TIME_RATIO * velocity)
    flat_index = (jnp.arange(NX, dtype=jnp.int32)[:, None, None] * NY + jnp.arange(NY, dtype=jnp.int32)[None, :, None]) * NZ + jnp.arange(NZ, dtype=jnp.int32)[None, None, :]
    source_mask = (flat_index == source_cell[0]).astype(jnp.float32)

    def advance(carry, pulse):
        current, previous = carry
        padded = jnp.pad(current, 4)
        updated = 2.0 * current - previous + courant * stencil(padded, current) + pulse * source_mask
        surface = updated[:, :, 0].reshape(-1)
        return ((updated, current), surface[receiver_cells])
    (wavefield, unused), traces = lax.scan(advance, (p_now, p_prev), wavelet)
    station_x = (station_cells // NY).astype(jnp.float32)
    station_y = (station_cells % NY).astype(jnp.float32)
    cell_y = (jnp.arange(NY * NZ, dtype=jnp.int32) // NZ).astype(jnp.float32)
    cell_z = (jnp.arange(NY * NZ, dtype=jnp.int32) % NZ).astype(jnp.float32) + 1.0
    planes = density.astype(jnp.bfloat16).reshape(NX, NY * NZ)
    plane_xs = jnp.arange(NX, dtype=jnp.int32).astype(jnp.float32)

    def forward(totals, packed):
        plane_x, plane = packed
        tile = kernel_tile(plane_x, station_x, station_y, cell_y, cell_z)
        return (totals + jnp.dot(tile, plane, preferred_element_type=jnp.float32), None)
    predicted, unused_out = lax.scan(forward, jnp.zeros((STATIONS,), jnp.float32), (plane_xs, planes))
    gravity_residual = predicted - observed
    residual_low = gravity_residual.astype(jnp.bfloat16)

    def adjoint(plane_x):
        tile = kernel_tile(plane_x, station_x, station_y, cell_y, cell_z)
        return jnp.dot(residual_low, tile, preferred_element_type=jnp.float32)
    density_gradient = lax.map(adjoint, plane_xs).reshape(NX, NY, NZ)
    stacked = jnp.stack([velocity, density])
    padded_model = jnp.pad(stacked, ((0, 0), (1, 1), (1, 1), (1, 1)))
    cross_gradient = cross_terms(padded_model, NX, NY, NZ)
    return (wavefield, traces, gravity_residual, density_gradient, cross_gradient)
```

```python
import functools

import jax
import jax.numpy as jnp
from jax import lax
from jax.experimental import pallas as pl
from jax.experimental.pallas import tpu as pltpu
from jax.sharding import PartitionSpec as P

STENCIL = (-205.0 / 72.0, 8.0 / 5.0, -1.0 / 5.0, 8.0 / 315.0, -1.0 / 560.0)
TIME_RATIO = 0.1
REACH = 4
AXES = ("mp", "station")
VMEM = pl.BlockSpec(memory_space=pltpu.VMEM)
SMEM = pl.BlockSpec(memory_space=pltpu.SMEM)
SRC_PLANE, SRC_ROW, SRC_LANE, X_LOW, HALF_LOW, ROW_LOW, LEFT_OK, RIGHT_OK, OUTER_OK, FLIPPED = range(10)
F32 = jnp.float32


def shape(dims):
    return jax.ShapeDtypeStruct(dims, F32)


def pairs_of(count, stations, partner):
    return [
        (m * stations + s, (lambda t: t[0] * stations + t[1])(partner(m, s)))
        for m in range(count)
        for s in range(stations)
    ]


def chain_partner(count):
    def partner(m, s):
        if s % 2 == 0:
            return (m ^ 1, s)
        other = m + 1 if m % 2 else m - 1
        if other < 0 or other >= count:
            return (m, s ^ 2)
        return (other, s)

    return partner


def divmod_static(value, divisor):
    if divisor & (divisor - 1) == 0:
        return value >> (divisor.bit_length() - 1), value & (divisor - 1)
    return value // divisor, value % divisor


def local_kernel(step, meta, wavelet, cur, prev, cour, surf_in, base, surf, pad):
    planes, rows, lanes = cur.shape
    lane = lax.broadcasted_iota(jnp.int32, (rows, lanes), 1)
    weights = {}
    for d in range(1, REACH + 1):
        weights[d] = jnp.where(lane >= d, STENCIL[d], 0.0)
        weights[-d] = jnp.where(lane < lanes - d, STENCIL[d], 0.0)
    for j in range(planes):
        pad[j, 0:8, :] = jnp.zeros((8, lanes), F32)
        pad[j, 8 + rows : 16 + rows, :] = jnp.zeros((8, lanes), F32)
        pad[j, 8 : 8 + rows, :] = cur[j]
    for j in range(planes):
        c = cur[j]
        acc = 3.0 * STENCIL[0] * c
        for d in range(1, REACH + 1):
            acc = acc + weights[d] * pltpu.roll(c, d, 1) + weights[-d] * pltpu.roll(c, lanes - d, 1)
            near = pad[j, 8 + d : 8 + d + rows, :] + pad[j, 8 - d : 8 - d + rows, :]
            for i in (j - d, j + d):
                if 0 <= i < planes:
                    near = near + cur[i]
            acc = acc + STENCIL[d] * near
        base[j] = 2.0 * c - prev[j] + cour[j] * acc
        if step == 0:
            surf[j] = jnp.zeros((rows, lanes), F32)
        else:
            surf[j] = jnp.where(
                lane == step - 1, jnp.broadcast_to(c[:, 0:1], (rows, lanes)), surf_in[j]
            )

    @pl.when(meta[SRC_PLANE] >= 0)
    def _():
        j, row = meta[SRC_PLANE], meta[SRC_ROW]
        hit = lax.broadcasted_iota(jnp.int32, (1, lanes), 1) == meta[SRC_LANE]
        line = base[j, pl.ds(row, 1), :]
        base[j, pl.ds(row, 1), :] = line + jnp.where(hit, wavelet[step], 0.0)


def local_step(step, meta, wavelet, cur, prev, cour, surf):
    planes, rows, lanes = cur.shape
    return pl.pallas_call(
        functools.partial(local_kernel, step),
        out_shape=(shape(cur.shape), shape(cur.shape)),
        in_specs=[SMEM, SMEM, VMEM, VMEM, VMEM, VMEM],
        out_specs=(VMEM, VMEM),
        scratch_shapes=[pltpu.VMEM((planes, rows + 16, lanes), F32)],
        cost_estimate=pl.CostEstimate(
            flops=60 * cur.size, bytes_accessed=24 * cur.size, transcendentals=0
        ),
        name="wave_local",
    )(meta, wavelet, cur, prev, cour, surf)


def halo_kernel(meta, base, cour, outer, inner, out):
    planes = base.shape[0]
    ok = jnp.where(meta[OUTER_OK] > 0, 1.0, 0.0)
    for j in range(planes):
        far = None
        for d in range(j + 1, REACH + 1):
            term = (STENCIL[d] * ok) * outer[d - j - 1]
            far = term if far is None else far + term
        for d in range(planes - j, REACH + 1):
            far = far + STENCIL[d] * inner[2 * planes - 1 - j - d]
        out[j] = base[j] + cour[j] * far


def halo_step(meta, base, cour, outer, inner):
    return pl.pallas_call(
        halo_kernel,
        out_shape=shape(base.shape),
        in_specs=[SMEM, VMEM, VMEM, VMEM, VMEM],
        out_specs=VMEM,
        cost_estimate=pl.CostEstimate(
            flops=12 * base.size, bytes_accessed=20 * base.size, transcendentals=0
        ),
        name="wave_halo",
    )(meta, base, cour, outer, inner)


def trace_kernel(step, place, cur, surf, out):
    planes, rows, lanes = cur.shape
    receivers = place.shape[0]
    steps = out.shape[0]
    lane = lax.broadcasted_iota(jnp.int32, (rows, lanes), 1)
    columns = jnp.concatenate(
        [
            jnp.where(lane == step, jnp.broadcast_to(cur[j, :, 0:1], (rows, lanes)), surf[j])
            for j in range(planes)
        ],
        0,
    )
    where = lax.broadcasted_iota(jnp.int32, (receivers, planes * rows), 1)
    pick = jnp.where(place[...] == where, 1.0, 0.0).astype(jnp.bfloat16)
    total = None
    for _ in range(3):
        part = columns.astype(jnp.bfloat16)
        columns = columns - part.astype(F32)
        term = jnp.dot(pick, part, preferred_element_type=F32)
        total = term if total is None else total + term
    out[...] = total.T[:steps, :]


def table_kernel(low, out):
    spread = out.shape[1]
    lanes = out.shape[2]
    dy = (lax.broadcasted_iota(jnp.int32, (spread, lanes), 0) - (spread // 2 - 1)).astype(F32)
    dz = (lax.broadcasted_iota(jnp.int32, (spread, lanes), 1) + 1).astype(F32)
    side = dy * dy
    deep = dz * dz

    def one(t, carry):
        dx = (t + low[0]).astype(F32)
        square = dx * dx + side + deep
        value = dz / (square * jnp.sqrt(square))
        out[t] = value.astype(jnp.bfloat16).astype(F32)
        return carry

    lax.fori_loop(0, out.shape[0], one, 0)


def gravity_table(low, depth, lateral, vertical):
    size = depth * 2 * lateral * vertical
    return pl.pallas_call(
        table_kernel,
        out_shape=shape((depth, 2 * lateral, vertical)),
        in_specs=[SMEM],
        out_specs=VMEM,
        cost_estimate=pl.CostEstimate(
            flops=20 * size, bytes_accessed=4 * size, transcendentals=2 * size
        ),
        name="gravity_table",
    )(low)


def forward_kernel(first, guard, lateral, low, meta, stations, table, dens, out):
    planes, rows, lanes = dens.shape
    count = out.shape[0]
    spread = 2 * lateral
    if guard:
        out[...] = jnp.zeros_like(out)

    def one(s, carry):
        sx, sy = divmod_static(stations[first + s], lateral)
        shift = meta[X_LOW] - sx - low[0]
        start = (shift + meta[HALF_LOW]) * spread + (lateral - 1 - sy)

        def accumulate():
            acc = None
            for p in range(planes):
                term = table[pl.ds(start + p * spread, rows), :] * dens[p]
                acc = term if acc is None else acc + term
            out[pl.ds(s, 1), :] = jnp.sum(acc, axis=0, keepdims=True)

        if guard:
            pl.when((shift >= 0) & (shift < guard))(accumulate)
        else:
            accumulate()
        return carry

    lax.fori_loop(0, count, one, 0, unroll=4)


def gravity_forward(first, count, guard, lateral, low, meta, stations, table, dens):
    flat = table.reshape(-1, table.shape[2])
    work = count * dens.size
    return pl.pallas_call(
        functools.partial(forward_kernel, first, guard, lateral),
        out_shape=shape((count, dens.shape[2])),
        in_specs=[SMEM, SMEM, SMEM, VMEM, VMEM],
        out_specs=VMEM,
        cost_estimate=pl.CostEstimate(
            flops=4 * work, bytes_accessed=4 * (flat.size + dens.size), transcendentals=0
        ),
        name="gravity_forward",
    )(low, meta, stations, flat, dens)


def adjoint_kernel(guard, lateral, slab, low, meta, stations, weights, table, out):
    rows = out.shape[1]
    spread = 2 * lateral

    def one(s, acc):
        sx, sy = divmod_static(stations[s], lateral)
        shift = meta[X_LOW] - sx - low[0]
        weight = weights[s]
        if guard:
            keep = (shift >= 0) & (shift < guard)
            shift = jnp.where(keep, shift, 0)
            weight = jnp.where(keep, weight, 0.0)
        start = shift * spread + (lateral - 1 - sy + meta[ROW_LOW])
        return tuple(
            acc[x] + weight * table[pl.ds(start + x * spread, rows), :] for x in range(slab)
        )

    zero = jnp.zeros((rows, out.shape[2]), F32)
    acc = lax.fori_loop(0, stations.shape[0], one, (zero,) * slab, unroll=4)
    for x in range(slab):
        out[x] = acc[x]


def gravity_adjoint(guard, lateral, slab, rows, low, meta, stations, weights, table):
    flat = table.reshape(-1, table.shape[2])
    return pl.pallas_call(
        functools.partial(adjoint_kernel, guard, lateral, slab),
        out_shape=shape((slab, rows, table.shape[2])),
        in_specs=[SMEM, SMEM, SMEM, SMEM, VMEM],
        out_specs=VMEM,
        name="gravity_adjoint",
    )(low, meta, stations, weights, flat)


def cross_kernel(meta, velocity, density, outer, inner, out):
    slab, rows, lanes = velocity.shape
    lane = lax.broadcasted_iota(jnp.int32, (rows, lanes), 1)
    row = lax.broadcasted_iota(jnp.int32, (rows, lanes), 0)
    flipped = meta[FLIPPED] > 0
    left_ok = jnp.where(meta[LEFT_OK] > 0, 0.5, 0.0)
    right_ok = jnp.where(meta[RIGHT_OK] > 0, 0.5, 0.0)

    def slopes(field, side, x):
        f = field[x]
        if x > 0:
            below = 0.5 * field[x - 1]
        else:
            below = left_ok * jnp.where(flipped, inner[side], outer[side])
        if x < slab - 1:
            above = 0.5 * field[x + 1]
        else:
            above = right_ok * jnp.where(flipped, outer[side], inner[side])
        up = jnp.where(row < rows - 1, pltpu.roll(f, rows - 1, 0), 0.0)
        down = jnp.where(row > 0, pltpu.roll(f, 1, 0), 0.0)
        ahead = jnp.where(lane < lanes - 1, pltpu.roll(f, lanes - 1, 1), 0.0)
        back = jnp.where(lane > 0, pltpu.roll(f, 1, 1), 0.0)
        return above - below, (up - down) * 0.5, (ahead - back) * 0.5

    for x in range(slab):
        v = slopes(velocity, 0, x)
        q = slopes(density, 1, x)
        out[0, x] = v[1] * q[2] - v[2] * q[1]
        out[1, x] = v[2] * q[0] - v[0] * q[2]
        out[2, x] = v[0] * q[1] - v[1] * q[0]


def cross_gradient_of(meta, velocity, density, outer, inner):
    return pl.pallas_call(
        cross_kernel,
        out_shape=shape((3,) + velocity.shape),
        in_specs=[SMEM, VMEM, VMEM, VMEM, VMEM],
        out_specs=VMEM,
        cost_estimate=pl.CostEstimate(
            flops=60 * velocity.size, bytes_accessed=24 * velocity.size, transcendentals=0
        ),
        name="cross_gradient",
    )(meta, velocity, density, outer, inner)


def per_device(
    p_now, p_prev, velocity, density, wavelet, source_cell, receiver_cells, station_cells, observed
):
    slab, lateral, vertical = p_now.shape
    count = lax.axis_size("mp")
    stations = lax.axis_size("station")
    steps = wavelet.shape[0]
    half = slab // 2
    assert half == REACH and count % 2 == 0 and stations % 4 == 0
    total_x = slab * count
    m = lax.axis_index("mp")
    s = lax.axis_index("station")
    core = s % 2
    x_low = m * slab
    flipped = (m + core) % 2 == 0
    outer_ok = jnp.where(flipped, m < count - 1, m > 0)

    chain = pairs_of(count, stations, chain_partner(count))

    def across(value):
        return lax.ppermute(value, AXES, chain)

    def swap_station(value, bit):
        return lax.ppermute(value, AXES, pairs_of(count, stations, lambda i, k: (i, k ^ bit)))

    def swap_slab(value, bit):
        return lax.ppermute(value, AXES, pairs_of(count, stations, lambda i, k: (i ^ bit, k)))

    def owned(field):
        return jnp.where(flipped, jnp.flip(field[half:], 0), field[:half])

    source_plane, source_lane = divmod_static(source_cell[0], vertical)
    source_x, source_row = divmod_static(source_plane, lateral)
    offset = source_x - x_low
    source_j = jnp.where(flipped, slab - 1 - offset, offset)
    source_j = jnp.where((source_j >= 0) & (source_j < half), source_j, -1)
    block = lateral // stations
    meta = jnp.stack(
        [
            source_j,
            source_row,
            source_lane,
            x_low,
            core * half,
            s * block,
            (m > 0).astype(jnp.int32),
            (m < count - 1).astype(jnp.int32),
            outer_ok.astype(jnp.int32),
            flipped.astype(jnp.int32),
        ]
    ).astype(jnp.int32)

    receiver_x, receiver_y = divmod_static(receiver_cells, lateral)
    receiver_j = receiver_x - x_low
    receiver_j = jnp.where(flipped, slab - 1 - receiver_j, receiver_j)
    inside = (receiver_j >= 0) & (receiver_j < half)
    place = jnp.where(inside, receiver_j * lateral + receiver_y, -1)[:, None]

    known = jnp.stack([station_cells.astype(F32), observed])[:, None, :]
    bit = 1
    while bit < stations:
        other = swap_station(known, bit)
        upper = (s // bit) % 2 == 1
        known = jnp.concatenate(
            [jnp.where(upper, other, known), jnp.where(upper, known, other)], 1
        )
        bit *= 2
    all_stations = known[0].reshape(-1).astype(jnp.int32)
    all_observed = known[1].reshape(-1)
    n_stations = all_stations.shape[0]

    reach = min(total_x, 64)
    chunks = -(-total_x // reach)
    guard = 0 if chunks == 1 else reach
    rounded = density.astype(jnp.bfloat16).astype(F32)
    half_density = jnp.where(core == 0, rounded[:half], rounded[half:])
    span = reach + slab - 1
    base_low = x_low - (total_x - 1)

    def table_at(low):
        return gravity_table(low, span, lateral, vertical)

    if chunks == 1:
        low = base_low[None].astype(jnp.int32)
        table = table_at(low)
        pieces = 4
        part = n_stations // pieces
        sums = jnp.concatenate(
            [
                gravity_forward(i * part, part, 0, lateral, low, meta, all_stations, table, half_density)
                for i in range(pieces)
            ]
        )
    else:

        def add_chunk(i, total):
            low = (base_low + i * reach)[None].astype(jnp.int32)
            return total + gravity_forward(
                0, n_stations, guard, lateral, low, meta, all_stations, table_at(low), half_density
            )

        sums = lax.fori_loop(0, chunks, add_chunk, jnp.zeros((n_stations, vertical), F32))
    predicted = jnp.sum(sums, axis=1)

    cour_full = TIME_RATIO * velocity * (TIME_RATIO * velocity)
    cour = owned(cour_full)
    cur = owned(p_now)
    prev = owned(p_prev)
    surf = cour
    edges = jnp.stack([owned(velocity)[0], owned(density)[0]])
    outer_edges = inner_edges = None
    for step in range(steps):
        if step == 0:
            received = across(jnp.concatenate([cur, edges]))
            outer, outer_edges = received[:half], received[half:]
        else:
            outer = across(cur)
        inner = swap_station(cur, 1)
        base, surf = local_step(step, meta, wavelet, cur, prev, cour, surf)
        if step == 1:
            inner_edges = swap_station(outer_edges, 1)
        cur, prev = halo_step(meta, base, cour, outer, inner), cur

    cross_gradient = cross_gradient_of(meta, velocity, density, outer_edges, inner_edges)

    sibling = swap_station(cur, 1)
    swapped = core == (m % 2)
    left = jnp.where(swapped, sibling, cur)
    right = jnp.where(swapped, cur, sibling)
    wavefield = jnp.concatenate([left, jnp.flip(right, 0)])

    recorded = pl.pallas_call(
        functools.partial(trace_kernel, steps - 1),
        out_shape=shape((steps, receiver_cells.shape[0])),
        in_specs=[VMEM] * 3,
        out_specs=VMEM,
        name="traces",
    )(place, cur, surf)
    packed = jnp.concatenate([recorded.reshape(-1, 128), predicted.reshape(-1, 128)])
    packed = packed + swap_station(packed, 1)
    if count & (count - 1) == 0:
        bit = 1
        while bit < count:
            packed = packed + swap_slab(packed, bit)
            bit *= 2
    else:
        packed = lax.psum(packed, "mp")
    trace_rows = recorded.size // 128
    traces = packed[:trace_rows].reshape(recorded.shape)
    residual = packed[trace_rows:].reshape(-1) - all_observed
    own_stations = station_cells.shape[0]
    gravity_residual = lax.dynamic_slice(residual, (s * own_stations,), (own_stations,))
    weights = residual.astype(jnp.bfloat16).astype(F32)

    if chunks == 1:
        density_gradient = gravity_adjoint(
            0, lateral, slab, block, low, meta, all_stations, weights, table
        )
    else:

        def back_chunk(i, total):
            low = (base_low + i * reach)[None].astype(jnp.int32)
            return total + gravity_adjoint(
                guard, lateral, slab, block, low, meta, all_stations, weights, table_at(low)
            )

        density_gradient = lax.fori_loop(
            0, chunks, back_chunk, jnp.zeros((slab, block, vertical), F32)
        )
    return (wavefield, traces, gravity_residual, density_gradient, cross_gradient)


def solution(mesh):
    in_specs = (
        P("mp", None, None),
        P("mp", None, None),
        P("mp", None, None),
        P("mp", None, None),
        P(),
        P(),
        P(),
        P("station"),
        P("station"),
    )
    out_specs = (
        P("mp", None, None),
        P(),
        P("station"),
        P("mp", "station", None),
        P(None, "mp", None, None),
    )
    return jax.shard_map(
        per_device, mesh=mesh, in_specs=in_specs, out_specs=out_specs, check_vma=False
    )
```

```python
import functools

import jax
import jax.numpy as jnp
from jax import lax
from jax.experimental import pallas as pl
from jax.experimental.pallas import tpu as pltpu
from jax.sharding import PartitionSpec as P

STENCIL = (-205.0 / 72.0, 8.0 / 5.0, -1.0 / 5.0, 8.0 / 315.0, -1.0 / 560.0)
TIME_RATIO = 0.1
REACH = 4
AXES = ("mp", "station")
VMEM = pl.BlockSpec(memory_space=pltpu.VMEM)
SMEM = pl.BlockSpec(memory_space=pltpu.SMEM)
SRC_PLANE, SRC_ROW, SRC_LANE, X_LOW, HALF_LOW, ROW_LOW, LEFT_OK, RIGHT_OK, FLIPPED = range(9)
F32 = jnp.float32
MIB = 1 << 20


def room(mib):
    return pltpu.CompilerParams(vmem_limit_bytes=mib * MIB)


def shape(dims):
    return jax.ShapeDtypeStruct(dims, F32)


def pairs_of(count, stations, partner):
    return [
        (m * stations + s, (lambda t: t[0] * stations + t[1])(partner(m, s)))
        for m in range(count)
        for s in range(stations)
    ]


def chain_partner(count):
    def partner(m, s):
        if s % 2 == 0:
            return (m ^ 1, s)
        other = m + 1 if m % 2 else m - 1
        if other < 0 or other >= count:
            return (m, s ^ 2)
        return (other, s)

    return partner


def divmod_static(value, divisor):
    if divisor & (divisor - 1) == 0:
        return value >> (divisor.bit_length() - 1), value & (divisor - 1)
    return value // divisor, value % divisor


def local_kernel(step, meta, wavelet, cur, prev, cour, surf_in, base, surf, pad):
    planes, rows, lanes = cur.shape
    lane = lax.broadcasted_iota(jnp.int32, (rows, lanes), 1)
    weights = {}
    for d in range(1, REACH + 1):
        weights[d] = jnp.where(lane >= d, STENCIL[d], 0.0)
        weights[-d] = jnp.where(lane < lanes - d, STENCIL[d], 0.0)
    for j in range(planes):
        pad[j, 0:8, :] = jnp.zeros((8, lanes), F32)
        pad[j, 8 + rows : 16 + rows, :] = jnp.zeros((8, lanes), F32)
        pad[j, 8 : 8 + rows, :] = cur[j]
    for j in range(planes):
        c = cur[j]
        acc = 3.0 * STENCIL[0] * c
        for d in range(1, REACH + 1):
            acc = acc + weights[d] * pltpu.roll(c, d, 1) + weights[-d] * pltpu.roll(c, lanes - d, 1)
            near = pad[j, 8 + d : 8 + d + rows, :] + pad[j, 8 - d : 8 - d + rows, :]
            for i in (j - d, j + d):
                if 0 <= i < planes:
                    near = near + cur[i]
            acc = acc + STENCIL[d] * near
        base[j] = 2.0 * c - prev[j] + cour[j] * acc
        if step == 0:
            surf[j] = jnp.zeros((rows, lanes), F32)
        else:
            surf[j] = jnp.where(
                lane == step - 1, jnp.broadcast_to(c[:, 0:1], (rows, lanes)), surf_in[j]
            )

    @pl.when(meta[SRC_PLANE] >= 0)
    def _():
        j, row = meta[SRC_PLANE], meta[SRC_ROW]
        hit = lax.broadcasted_iota(jnp.int32, (1, lanes), 1) == meta[SRC_LANE]
        line = base[j, pl.ds(row, 1), :]
        base[j, pl.ds(row, 1), :] = line + jnp.where(hit, wavelet[step], 0.0)


def local_step(step, meta, wavelet, cur, prev, cour, surf):
    planes, rows, lanes = cur.shape
    return pl.pallas_call(
        functools.partial(local_kernel, step),
        out_shape=(shape(cur.shape), shape(cur.shape)),
        in_specs=[SMEM, SMEM, VMEM, VMEM, VMEM, VMEM],
        out_specs=(VMEM, VMEM),
        scratch_shapes=[pltpu.VMEM((planes, rows + 16, lanes), F32)],
        compiler_params=room(2),
        cost_estimate=pl.CostEstimate(
            flops=60 * cur.size, bytes_accessed=24 * cur.size, transcendentals=0
        ),
        name="wave_local",
    )(meta, wavelet, cur, prev, cour, surf)


def halo_kernel(base, cour, cour_outer, outer, inner, out):
    planes = base.shape[0]
    for j in range(planes):
        far = near = None
        for d in range(j + 1, REACH + 1):
            term = STENCIL[d] * outer[d - j - 1]
            far = term if far is None else far + term
        for d in range(planes - j, REACH + 1):
            term = STENCIL[d] * inner[2 * planes - 1 - j - d]
            near = term if near is None else near + term
        out[j] = base[j] + (cour[j] * near + cour_outer[j] * far)


def halo_step(base, cour, cour_outer, outer, inner):
    return pl.pallas_call(
        halo_kernel,
        out_shape=shape(base.shape),
        in_specs=[VMEM] * 5,
        out_specs=VMEM,
        compiler_params=room(2),
        cost_estimate=pl.CostEstimate(
            flops=12 * base.size, bytes_accessed=20 * base.size, transcendentals=0
        ),
        name="wave_halo",
    )(base, cour, cour_outer, outer, inner)


def trace_kernel(step, place, cur, surf, out):
    planes, rows, lanes = cur.shape
    receivers = place.shape[0]
    steps = out.shape[0]
    lane = lax.broadcasted_iota(jnp.int32, (rows, lanes), 1)
    columns = jnp.concatenate(
        [
            jnp.where(lane == step, jnp.broadcast_to(cur[j, :, 0:1], (rows, lanes)), surf[j])
            for j in range(planes)
        ],
        0,
    )
    where = lax.broadcasted_iota(jnp.int32, (receivers, planes * rows), 1)
    pick = jnp.where(place[...] == where, 1.0, 0.0).astype(jnp.bfloat16)
    total = None
    for _ in range(3):
        part = columns.astype(jnp.bfloat16)
        columns = columns - part.astype(F32)
        term = jnp.dot(pick, part, preferred_element_type=F32)
        total = term if total is None else total + term
    out[...] = total.T[:steps, :]


def table_kernel(low, out):
    spread = out.shape[1]
    lanes = out.shape[2]
    dy = (lax.broadcasted_iota(jnp.int32, (spread, lanes), 0) - (spread // 2 - 1)).astype(F32)
    dz = (lax.broadcasted_iota(jnp.int32, (spread, lanes), 1) + 1).astype(F32)
    side = dy * dy
    deep = dz * dz

    def one(t, carry):
        dx = (t + low[0]).astype(F32)
        square = dx * dx + side + deep
        value = dz / (square * jnp.sqrt(square))
        out[t] = value.astype(jnp.bfloat16).astype(F32)
        return carry

    lax.fori_loop(0, out.shape[0], one, 0)


def gravity_table(low, depth, lateral, vertical):
    size = depth * 2 * lateral * vertical
    return pl.pallas_call(
        table_kernel,
        out_shape=shape((depth, 2 * lateral, vertical)),
        in_specs=[SMEM],
        out_specs=VMEM,
        cost_estimate=pl.CostEstimate(
            flops=20 * size, bytes_accessed=4 * size, transcendentals=2 * size
        ),
        compiler_params=room(8),
        name="gravity_table",
    )(low)


def forward_kernel(first, guard, lateral, low, meta, stations, table, dens, out):
    planes, rows, lanes = dens.shape
    count = out.shape[0]
    spread = 2 * lateral
    if guard:
        out[...] = jnp.zeros_like(out)

    def one(s, carry):
        sx, sy = divmod_static(stations[first + s], lateral)
        shift = meta[X_LOW] - sx - low[0]
        start = (shift + meta[HALF_LOW]) * spread + (lateral - 1 - sy)

        def accumulate():
            acc = None
            for p in range(planes):
                term = table[pl.ds(start + p * spread, rows), :] * dens[p]
                acc = term if acc is None else acc + term
            out[pl.ds(s, 1), :] = jnp.sum(acc, axis=0, keepdims=True)

        if guard:
            pl.when((shift >= 0) & (shift < guard))(accumulate)
        else:
            accumulate()
        return carry

    lax.fori_loop(0, count, one, 0, unroll=4)


def gravity_forward(first, count, guard, lateral, low, meta, stations, table, dens):
    flat = table.reshape(-1, table.shape[2])
    work = count * dens.size
    return pl.pallas_call(
        functools.partial(forward_kernel, first, guard, lateral),
        out_shape=shape((count, dens.shape[2])),
        in_specs=[SMEM, SMEM, SMEM, VMEM, VMEM],
        out_specs=VMEM,
        cost_estimate=pl.CostEstimate(
            flops=4 * work, bytes_accessed=4 * (flat.size + dens.size), transcendentals=0
        ),
        compiler_params=room(8),
        name="gravity_forward",
    )(low, meta, stations, flat, dens)


def adjoint_kernel(guard, lateral, slab, low, meta, stations, weights, table, out):
    rows = out.shape[1]
    spread = 2 * lateral

    def one(s, acc):
        sx, sy = divmod_static(stations[s], lateral)
        shift = meta[X_LOW] - sx - low[0]
        weight = weights[s]
        if guard:
            keep = (shift >= 0) & (shift < guard)
            shift = jnp.where(keep, shift, 0)
            weight = jnp.where(keep, weight, 0.0)
        start = shift * spread + (lateral - 1 - sy + meta[ROW_LOW])
        return tuple(
            acc[x] + weight * table[pl.ds(start + x * spread, rows), :] for x in range(slab)
        )

    zero = jnp.zeros((rows, out.shape[2]), F32)
    acc = lax.fori_loop(0, stations.shape[0], one, (zero,) * slab, unroll=4)
    for x in range(slab):
        out[x] = acc[x]


def gravity_adjoint(guard, lateral, slab, rows, low, meta, stations, weights, table):
    flat = table.reshape(-1, table.shape[2])
    return pl.pallas_call(
        functools.partial(adjoint_kernel, guard, lateral, slab),
        out_shape=shape((slab, rows, table.shape[2])),
        in_specs=[SMEM, SMEM, SMEM, SMEM, VMEM],
        out_specs=VMEM,
        compiler_params=room(8),
        name="gravity_adjoint",
    )(low, meta, stations, weights, flat)


def cross_kernel(meta, velocity, density, outer, inner, out):
    slab, rows, lanes = velocity.shape
    lane = lax.broadcasted_iota(jnp.int32, (rows, lanes), 1)
    row = lax.broadcasted_iota(jnp.int32, (rows, lanes), 0)
    flipped = meta[FLIPPED] > 0
    left_ok = jnp.where(meta[LEFT_OK] > 0, 0.5, 0.0)
    right_ok = jnp.where(meta[RIGHT_OK] > 0, 0.5, 0.0)

    def slopes(field, side, x):
        f = field[x]
        if x > 0:
            below = 0.5 * field[x - 1]
        else:
            below = left_ok * jnp.where(flipped, inner[side], outer[side])
        if x < slab - 1:
            above = 0.5 * field[x + 1]
        else:
            above = right_ok * jnp.where(flipped, outer[side], inner[side])
        up = jnp.where(row < rows - 1, pltpu.roll(f, rows - 1, 0), 0.0)
        down = jnp.where(row > 0, pltpu.roll(f, 1, 0), 0.0)
        ahead = jnp.where(lane < lanes - 1, pltpu.roll(f, lanes - 1, 1), 0.0)
        back = jnp.where(lane > 0, pltpu.roll(f, 1, 1), 0.0)
        return above - below, (up - down) * 0.5, (ahead - back) * 0.5

    for x in range(slab):
        v = slopes(velocity, 0, x)
        q = slopes(density, 1, x)
        out[0, x] = v[1] * q[2] - v[2] * q[1]
        out[1, x] = v[2] * q[0] - v[0] * q[2]
        out[2, x] = v[0] * q[1] - v[1] * q[0]


def cross_gradient_of(meta, velocity, density, outer, inner):
    return pl.pallas_call(
        cross_kernel,
        out_shape=shape((3,) + velocity.shape),
        in_specs=[SMEM, VMEM, VMEM, VMEM, VMEM],
        out_specs=VMEM,
        cost_estimate=pl.CostEstimate(
            flops=60 * velocity.size, bytes_accessed=24 * velocity.size, transcendentals=0
        ),
        compiler_params=room(8),
        name="cross_gradient",
    )(meta, velocity, density, outer, inner)


def per_device(
    p_now, p_prev, velocity, density, wavelet, source_cell, receiver_cells, station_cells, observed
):
    slab, lateral, vertical = p_now.shape
    count = lax.axis_size("mp")
    stations = lax.axis_size("station")
    steps = wavelet.shape[0]
    half = slab // 2
    assert half == REACH and count % 2 == 0 and stations % 4 == 0
    total_x = slab * count
    m = lax.axis_index("mp")
    s = lax.axis_index("station")
    core = s % 2
    x_low = m * slab
    flipped = (m + core) % 2 == 0
    outer_ok = jnp.where(flipped, m < count - 1, m > 0)

    chain = pairs_of(count, stations, chain_partner(count))

    def across(value):
        return lax.ppermute(value, AXES, chain)

    def swap_station(value, bit):
        return lax.ppermute(value, AXES, pairs_of(count, stations, lambda i, k: (i, k ^ bit)))

    def swap_slab(value, bit):
        return lax.ppermute(value, AXES, pairs_of(count, stations, lambda i, k: (i ^ bit, k)))

    def owned(field):
        return jnp.where(flipped, jnp.flip(field[half:], 0), field[:half])

    source_plane, source_lane = divmod_static(source_cell[0], vertical)
    source_x, source_row = divmod_static(source_plane, lateral)
    offset = source_x - x_low
    source_j = jnp.where(flipped, slab - 1 - offset, offset)
    source_j = jnp.where((source_j >= 0) & (source_j < half), source_j, -1)
    block = lateral // stations
    meta = jnp.stack(
        [
            source_j,
            source_row,
            source_lane,
            x_low,
            core * half,
            s * block,
            (m > 0).astype(jnp.int32),
            (m < count - 1).astype(jnp.int32),
            flipped.astype(jnp.int32),
        ]
    ).astype(jnp.int32)

    receiver_x, receiver_y = divmod_static(receiver_cells, lateral)
    receiver_j = receiver_x - x_low
    receiver_j = jnp.where(flipped, slab - 1 - receiver_j, receiver_j)
    inside = (receiver_j >= 0) & (receiver_j < half)
    place = jnp.where(inside, receiver_j * lateral + receiver_y, -1)[:, None]

    known = jnp.stack([station_cells.astype(F32), observed])[:, None, :]
    bit = 1
    while bit < stations:
        other = swap_station(known, bit)
        upper = (s // bit) % 2 == 1
        known = jnp.concatenate(
            [jnp.where(upper, other, known), jnp.where(upper, known, other)], 1
        )
        bit *= 2
    all_stations = known[0].reshape(-1).astype(jnp.int32)
    all_observed = known[1].reshape(-1)
    n_stations = all_stations.shape[0]

    reach = min(total_x, 64)
    chunks = -(-total_x // reach)
    guard = 0 if chunks == 1 else reach
    rounded = density.astype(jnp.bfloat16).astype(F32)
    half_density = jnp.where(core == 0, rounded[:half], rounded[half:])
    span = reach + slab - 1
    base_low = x_low - (total_x - 1)

    def table_at(low):
        return gravity_table(low, span, lateral, vertical)

    if chunks == 1:
        low = base_low[None].astype(jnp.int32)
        table = table_at(low)
        pieces = 4
        part = n_stations // pieces
        sums = jnp.concatenate(
            [
                gravity_forward(i * part, part, 0, lateral, low, meta, all_stations, table, half_density)
                for i in range(pieces)
            ]
        )
    else:

        def add_chunk(i, total):
            low = (base_low + i * reach)[None].astype(jnp.int32)
            return total + gravity_forward(
                0, n_stations, guard, lateral, low, meta, all_stations, table_at(low), half_density
            )

        sums = lax.fori_loop(0, chunks, add_chunk, jnp.zeros((n_stations, vertical), F32))
    predicted = jnp.sum(sums, axis=1)

    cour_full = TIME_RATIO * velocity * (TIME_RATIO * velocity)
    cour = owned(cour_full)
    cour_outer = jnp.where(outer_ok, cour, 0.0)
    cur = owned(p_now)
    prev = owned(p_prev)
    surf = cour
    edges = jnp.stack([owned(velocity)[0], owned(density)[0]])
    outer_edges = inner_edges = None
    for step in range(steps):
        if step == 0:
            received = across(jnp.concatenate([cur, edges]))
            outer, outer_edges = received[:half], received[half:]
        else:
            outer = across(cur)
        inner = swap_station(cur, 1)
        base, surf = local_step(step, meta, wavelet, cur, prev, cour, surf)
        if step == 1:
            inner_edges = swap_station(outer_edges, 1)
        cur, prev = halo_step(base, cour, cour_outer, outer, inner), cur

    cross_gradient = cross_gradient_of(meta, velocity, density, outer_edges, inner_edges)

    sibling = swap_station(cur, 1)
    swapped = core == (m % 2)
    left = jnp.where(swapped, sibling, cur)
    right = jnp.where(swapped, cur, sibling)
    wavefield = jnp.concatenate([left, jnp.flip(right, 0)])

    recorded = pl.pallas_call(
        functools.partial(trace_kernel, steps - 1),
        out_shape=shape((steps, receiver_cells.shape[0])),
        in_specs=[VMEM] * 3,
        out_specs=VMEM,
        compiler_params=room(4),
        name="traces",
    )(place, cur, surf)
    packed = jnp.concatenate([recorded.reshape(-1, 128), predicted.reshape(-1, 128)])
    packed = packed + swap_station(packed, 1)
    if count & (count - 1) == 0:
        bit = 1
        while bit < count:
            packed = packed + swap_slab(packed, bit)
            bit *= 2
    else:
        packed = lax.psum(packed, "mp")
    trace_rows = recorded.size // 128
    traces = packed[:trace_rows].reshape(recorded.shape)
    residual = packed[trace_rows:].reshape(-1) - all_observed
    own_stations = station_cells.shape[0]
    gravity_residual = lax.dynamic_slice(residual, (s * own_stations,), (own_stations,))
    weights = residual.astype(jnp.bfloat16).astype(F32)

    if chunks == 1:
        density_gradient = gravity_adjoint(
            0, lateral, slab, block, low, meta, all_stations, weights, table
        )
    else:

        def back_chunk(i, total):
            low = (base_low + i * reach)[None].astype(jnp.int32)
            return total + gravity_adjoint(
                guard, lateral, slab, block, low, meta, all_stations, weights, table_at(low)
            )

        density_gradient = lax.fori_loop(
            0, chunks, back_chunk, jnp.zeros((slab, block, vertical), F32)
        )
    return (wavefield, traces, gravity_residual, density_gradient, cross_gradient)


def solution(mesh):
    in_specs = (
        P("mp", None, None),
        P("mp", None, None),
        P("mp", None, None),
        P("mp", None, None),
        P(),
        P(),
        P(),
        P("station"),
        P("station"),
    )
    out_specs = (
        P("mp", None, None),
        P(),
        P("station"),
        P("mp", "station", None),
        P(None, "mp", None, None),
    )
    return jax.shard_map(
        per_device, mesh=mesh, in_specs=in_specs, out_specs=out_specs, check_vma=False
    )
```

```python
import functools

import jax
import jax.numpy as jnp
from jax import lax
from jax.experimental import pallas as pl
from jax.experimental.pallas import tpu as pltpu
from jax.sharding import PartitionSpec as P

STENCIL = (-205.0 / 72.0, 8.0 / 5.0, -1.0 / 5.0, 8.0 / 315.0, -1.0 / 560.0)
TIME_RATIO = 0.1
REACH = 4
AXES = ("mp", "station")
VMEM = pl.BlockSpec(memory_space=pltpu.VMEM)
SMEM = pl.BlockSpec(memory_space=pltpu.SMEM)
ANY = pl.BlockSpec(memory_space=pl.ANY)
F32 = jnp.float32
MIB = 1 << 20


def room(mib):
    return pltpu.CompilerParams(vmem_limit_bytes=mib * MIB)


def shape(dims):
    return jax.ShapeDtypeStruct(dims, F32)


def pairs_of(count, stations, partner):
    return [
        (m * stations + s, (lambda t: t[0] * stations + t[1])(partner(m, s)))
        for m in range(count)
        for s in range(stations)
    ]


def chain_partner(count):
    def partner(m, s):
        other = m + 1 if s % 2 == 0 else m - 1
        if other < 0 or other >= count:
            return (m, s ^ 2)
        return (other, s ^ 1)

    return partner


def position():
    return lax.axis_index("mp"), lax.axis_index("station") % 2


def divmod_static(value, divisor):
    if divisor & (divisor - 1) == 0:
        return value >> (divisor.bit_length() - 1), value & (divisor - 1)
    return value // divisor, value % divisor


def run_copies(pairs, sems):
    copies = [pltpu.make_async_copy(a, b, sems.at[i]) for i, (a, b) in enumerate(pairs)]
    for copy in copies:
        copy.start()
    for copy in copies:
        copy.wait()


def plane_of(core, j, slab):
    return jnp.where(core == 0, slab - 1 - j, j)


def first_kernel(now, velocity, density, cur, message, sems):
    slab = now.shape[0]
    half = slab // 2
    _, core = position()
    pairs = []
    for j in range(half):
        plane = plane_of(core, j, slab)
        pairs += [(now.at[plane], cur.at[j]), (now.at[plane], message.at[j])]
    edge = plane_of(core, 0, slab)
    pairs += [(velocity.at[edge], message.at[half]), (density.at[edge], message.at[half + 1])]
    run_copies(pairs, sems)


def first_message(p_now, velocity, density):
    slab, rows, lanes = p_now.shape
    half = slab // 2
    return pl.pallas_call(
        first_kernel,
        out_shape=(shape((half, rows, lanes)), shape((half + 2, rows, lanes))),
        in_specs=[ANY] * 3,
        out_specs=(VMEM, VMEM),
        scratch_shapes=[pltpu.SemaphoreType.DMA((2 * half + 2,))],
        compiler_params=room(2),
        name="first_message",
    )(p_now, velocity, density)


def setup_kernel(count, source, p_prev, velocity, density, prev, cour, cour_outer, mask, dens, vel, raw, sems):
    slab = p_prev.shape[0]
    half, rows, lanes = prev.shape
    m, core = position()
    pairs = []
    for j in range(half):
        plane = plane_of(core, j, slab)
        pairs += [(p_prev.at[plane], prev.at[j]), (velocity.at[plane], vel.at[j])]
    pairs += [(density.at[pl.ds(core * half, half)], raw)]
    run_copies(pairs, sems)
    outer_ok = jnp.where(jnp.where(core == 0, m < count - 1, m > 0), 1.0, 0.0)
    column, source_lane = divmod_static(source[0], lanes)
    source_x, source_row = divmod_static(column, rows)
    row = lax.broadcasted_iota(jnp.int32, (rows, lanes), 0)
    lane = lax.broadcasted_iota(jnp.int32, (rows, lanes), 1)
    spot = jnp.where((row == source_row) & (lane == source_lane), 1.0, 0.0)
    for j in range(half):
        scaled = TIME_RATIO * vel[j]
        square = scaled * scaled
        cour[j] = square
        cour_outer[j] = square * outer_ok
        here = m * slab + plane_of(core, j, slab) == source_x
        mask[j] = spot * jnp.where(here, 1.0, 0.0)
        dens[j] = raw[j].astype(jnp.bfloat16).astype(F32)


def setup(count, source_cell, p_prev, velocity, density):
    slab, rows, lanes = p_prev.shape
    half = slab // 2
    part = shape((half, rows, lanes))
    held = pltpu.VMEM((half, rows, lanes), F32)
    return pl.pallas_call(
        functools.partial(setup_kernel, count),
        out_shape=(part,) * 5,
        in_specs=[SMEM] + [ANY] * 3,
        out_specs=(VMEM,) * 5,
        scratch_shapes=[held, held, pltpu.SemaphoreType.DMA((2 * half + 1,))],
        compiler_params=room(4),
        cost_estimate=pl.CostEstimate(
            flops=20 * half * rows * lanes, bytes_accessed=32 * half * rows * lanes, transcendentals=0
        ),
        name="setup",
    )(source_cell, p_prev, velocity, density)


def local_kernel(step, pulses, mask, cur, prev, cour, surf_in, base, surf, pad):
    planes, rows, lanes = prev.shape
    lane = lax.broadcasted_iota(jnp.int32, (rows, lanes), 1)
    weights = {}
    for d in range(1, REACH + 1):
        weights[d] = jnp.where(lane >= d, STENCIL[d], 0.0)
        weights[-d] = jnp.where(lane < lanes - d, STENCIL[d], 0.0)
    pulse = pulses[step : step + 1, :]
    for j in range(planes):
        pad[j, 0:8, :] = jnp.zeros((8, lanes), F32)
        pad[j, 8 + rows : 16 + rows, :] = jnp.zeros((8, lanes), F32)
        pad[j, 8 : 8 + rows, :] = cur[j]
    for j in range(planes):
        c = cur[j]
        acc = 3.0 * STENCIL[0] * c
        for d in range(1, REACH + 1):
            acc = acc + weights[d] * pltpu.roll(c, d, 1) + weights[-d] * pltpu.roll(c, lanes - d, 1)
            near = pad[j, 8 + d : 8 + d + rows, :] + pad[j, 8 - d : 8 - d + rows, :]
            for i in (j - d, j + d):
                if 0 <= i < planes:
                    near = near + cur[i]
            acc = acc + STENCIL[d] * near
        base[j] = 2.0 * c - prev[j] + cour[j] * acc + pulse * mask[j]
        if step == 0:
            surf[j] = jnp.zeros((rows, lanes), F32)
        else:
            surf[j] = jnp.where(
                lane == step - 1, jnp.broadcast_to(c[:, 0:1], (rows, lanes)), surf_in[j]
            )


def local_step(step, pulses, mask, cur, prev, cour, surf):
    planes, rows, lanes = cur.shape
    return pl.pallas_call(
        functools.partial(local_kernel, step),
        out_shape=(shape(cur.shape), shape(cur.shape)),
        in_specs=[VMEM] * 6,
        out_specs=(VMEM, VMEM),
        scratch_shapes=[pltpu.VMEM((planes, rows + 16, lanes), F32)],
        compiler_params=room(2),
        cost_estimate=pl.CostEstimate(
            flops=60 * cur.size, bytes_accessed=24 * cur.size, transcendentals=0
        ),
        name="wave_local",
    )(pulses, mask, cur, prev, cour, surf)


def halo_kernel(base, cour, cour_outer, outer, inner, out):
    planes = base.shape[0]
    for j in range(planes):
        far = near = None
        for d in range(j + 1, REACH + 1):
            term = STENCIL[d] * outer[d - j - 1]
            far = term if far is None else far + term
        for d in range(planes - j, REACH + 1):
            term = STENCIL[d] * inner[2 * planes - 1 - j - d]
            near = term if near is None else near + term
        out[j] = base[j] + (cour[j] * near + cour_outer[j] * far)


def halo_step(base, cour, cour_outer, outer, inner):
    return pl.pallas_call(
        halo_kernel,
        out_shape=shape(base.shape),
        in_specs=[VMEM] * 5,
        out_specs=VMEM,
        compiler_params=room(2),
        cost_estimate=pl.CostEstimate(
            flops=12 * base.size, bytes_accessed=20 * base.size, transcendentals=0
        ),
        name="wave_halo",
    )(base, cour, cour_outer, outer, inner)


def trace_kernel(step, place, cur, surf, predicted, out):
    planes, rows, lanes = cur.shape
    receivers = place.shape[0]
    steps = step + 1
    lane = lax.broadcasted_iota(jnp.int32, (rows, lanes), 1)
    columns = jnp.concatenate(
        [
            jnp.where(lane == step, jnp.broadcast_to(cur[j, :, 0:1], (rows, lanes)), surf[j])
            for j in range(planes)
        ],
        0,
    )
    where = lax.broadcasted_iota(jnp.int32, (receivers, planes * rows), 1)
    pick = jnp.where(place[...] == where, 1.0, 0.0).astype(jnp.bfloat16)
    total = None
    for _ in range(3):
        part = columns.astype(jnp.bfloat16)
        columns = columns - part.astype(F32)
        term = jnp.dot(pick, part, preferred_element_type=F32)
        total = term if total is None else total + term
    total = total.T
    for b in range(receivers // 128):
        out[b * steps : (b + 1) * steps, :] = total[:steps, b * 128 : (b + 1) * 128]
    out[steps * (receivers // 128) :, :] = predicted[...]


def recorded_traces(step, place, cur, surf, predicted):
    rows = (step + 1) * (place.shape[0] // 128) + predicted.shape[0]
    return pl.pallas_call(
        functools.partial(trace_kernel, step),
        out_shape=shape((rows, 128)),
        in_specs=[VMEM] * 4,
        out_specs=VMEM,
        compiler_params=room(4),
        name="traces",
    )(place, cur, surf, predicted)


def join_kernel(own, sibling, out, sems):
    slab = out.shape[0]
    _, core = position()
    pairs = []
    for j in range(slab // 2):
        pairs += [
            (own.at[j], out.at[plane_of(core, j, slab)]),
            (sibling.at[j], out.at[plane_of(1 - core, j, slab)]),
        ]
    run_copies(pairs, sems)


def join(own, sibling):
    half, rows, lanes = own.shape
    return pl.pallas_call(
        join_kernel,
        out_shape=shape((2 * half, rows, lanes)),
        in_specs=[VMEM, VMEM],
        out_specs=ANY,
        scratch_shapes=[pltpu.SemaphoreType.DMA((2 * half,))],
        compiler_params=room(2),
        name="join",
    )(own, sibling)


def table_low(total_x, slab, offset):
    m, _ = position()
    return m * slab - (total_x - 1) + offset


def table_kernel(total_x, slab, head, out):
    spread, lanes = out.shape[1:]
    low = table_low(total_x, slab, head[0])
    dy = (lax.broadcasted_iota(jnp.int32, (spread, lanes), 0) - (spread // 2 - 1)).astype(F32)
    dz = (lax.broadcasted_iota(jnp.int32, (spread, lanes), 1) + 1).astype(F32)
    side = dy * dy
    deep = dz * dz

    def one(t, carry):
        dx = (t + low).astype(F32)
        square = dx * dx + side + deep
        value = dz / (square * jnp.sqrt(square))
        out[t] = value.astype(jnp.bfloat16).astype(F32)
        return carry

    lax.fori_loop(0, out.shape[0], one, 0)


def gravity_table(total_x, slab, depth, lateral, vertical, head):
    size = depth * 2 * lateral * vertical
    return pl.pallas_call(
        functools.partial(table_kernel, total_x, slab),
        out_shape=shape((depth, 2 * lateral, vertical)),
        in_specs=[SMEM],
        out_specs=VMEM,
        cost_estimate=pl.CostEstimate(
            flops=20 * size, bytes_accessed=4 * size, transcendentals=2 * size
        ),
        compiler_params=room(8),
        name="gravity_table",
    )(head)


def forward_kernel(first, guard, total_x, slab, lateral, head, table, dens, out):
    planes, rows, lanes = dens.shape
    count = out.shape[0]
    spread = 2 * lateral
    m, core = position()
    lead = total_x - 1 - head[0]
    if guard:
        out[...] = jnp.zeros_like(out)

    def one(s, carry):
        sx, sy = divmod_static(head[1 + first + s], lateral)
        shift = lead - sx
        start = (shift + core * planes) * spread + (lateral - 1 - sy)

        def accumulate():
            acc = None
            for p in range(planes):
                term = table[pl.ds(start + p * spread, rows), :] * dens[p]
                acc = term if acc is None else acc + term
            out[pl.ds(s, 1), :] = jnp.sum(acc, axis=0, keepdims=True)

        if guard:
            pl.when((shift >= 0) & (shift < guard))(accumulate)
        else:
            accumulate()
        return carry

    lax.fori_loop(0, count, one, 0, unroll=4)


def gravity_forward(first, count, guard, total_x, slab, lateral, head, table, dens):
    flat = table.reshape(-1, table.shape[2])
    work = count * dens.size
    return pl.pallas_call(
        functools.partial(forward_kernel, first, guard, total_x, slab, lateral),
        out_shape=shape((count, dens.shape[2])),
        in_specs=[SMEM, VMEM, VMEM],
        out_specs=VMEM,
        cost_estimate=pl.CostEstimate(
            flops=4 * work, bytes_accessed=4 * dens.size, transcendentals=0
        ),
        compiler_params=room(8),
        name="gravity_forward",
    )(head, flat, dens)


def spread_back(guard, total_x, lateral, row_low, head, weights, table, out):
    slab, rows, lanes = out.shape
    spread = 2 * lateral
    lead = total_x - 1 - head[0]

    def one(s, acc):
        sx, sy = divmod_static(head[1 + s], lateral)
        shift = lead - sx
        weight = weights(s)
        if guard:
            keep = (shift >= 0) & (shift < guard)
            shift = jnp.where(keep, shift, 0)
            weight = jnp.where(keep, weight, 0.0)
        start = shift * spread + (lateral - 1 - sy + row_low)
        return tuple(
            acc[x] + weight * table[pl.ds(start + x * spread, rows), :] for x in range(slab)
        )

    zero = jnp.zeros((rows, lanes), F32)
    acc = lax.fori_loop(0, head.shape[0] - 1, one, (zero,) * slab, unroll=4)
    for x in range(slab):
        out[x] = acc[x]


def adjoint_kernel(guard, total_x, lateral, head, weights, table, out):
    row_low = lax.axis_index("station") * out.shape[1]
    spread_back(guard, total_x, lateral, row_low, head, lambda s: weights[s], table, out)


def gravity_adjoint(guard, total_x, slab, rows, lateral, head, weights, table):
    flat = table.reshape(-1, table.shape[2])
    return pl.pallas_call(
        functools.partial(adjoint_kernel, guard, total_x, lateral),
        out_shape=shape((slab, rows, table.shape[2])),
        in_specs=[SMEM, SMEM, VMEM],
        out_specs=VMEM,
        compiler_params=room(8),
        name="gravity_adjoint",
    )(head, weights, flat)


def last_kernel(total_x, lateral, head, packed, other, observed, table, traces, own, out, held, scalars, sem):
    steps, receivers = traces.shape
    blocks = receivers // 128
    total = packed[...] + other[...]
    residual = total[steps * blocks :, :] - observed[...]
    held[...] = residual.astype(jnp.bfloat16).astype(F32)
    copy = pltpu.make_async_copy(held, scalars, sem)
    copy.start()
    for b in range(blocks):
        traces[:, b * 128 : (b + 1) * 128] = total[b * steps : (b + 1) * steps, :]
    s = lax.axis_index("station")
    mine = own.shape[0]
    for k in range(residual.shape[0] // mine):

        @pl.when(s == k)
        def _(k=k):
            own[...] = residual[k * mine : (k + 1) * mine, :]

    copy.wait()
    spread_back(
        0,
        total_x,
        lateral,
        s * out.shape[1],
        head,
        lambda i: scalars[i // 128, i % 128],
        table,
        out,
    )


def gravity_last(steps, receivers, total_x, slab, rows, lateral, head, packed, other, observed, table):
    flat = table.reshape(-1, table.shape[2])
    count = lax.axis_size("station")
    lines = observed.shape[0]
    return pl.pallas_call(
        functools.partial(last_kernel, total_x, lateral),
        out_shape=(
            shape((steps, receivers)),
            shape((lines // count, 128)),
            shape((slab, rows, table.shape[2])),
        ),
        in_specs=[SMEM] + [VMEM] * 4,
        out_specs=(VMEM,) * 3,
        scratch_shapes=[
            pltpu.VMEM((lines, 128), F32),
            pltpu.SMEM((lines, 128), F32),
            pltpu.SemaphoreType.DMA,
        ],
        compiler_params=room(8),
        name="gravity_last",
    )(head, packed, other, observed, flat)


def cross_kernel(count, velocity, density, outer, inner, out):
    slab, rows, lanes = velocity.shape
    half = slab // 2
    lane = lax.broadcasted_iota(jnp.int32, (rows, lanes), 1)
    row = lax.broadcasted_iota(jnp.int32, (rows, lanes), 0)
    m, core = position()
    flipped = core == 0
    left_ok = jnp.where(m > 0, 0.5, 0.0)
    right_ok = jnp.where(m < count - 1, 0.5, 0.0)

    def slopes(field, side, x):
        f = field[x]
        if x > 0:
            below = 0.5 * field[x - 1]
        else:
            below = left_ok * jnp.where(flipped, inner[side], outer[side])
        if x < slab - 1:
            above = 0.5 * field[x + 1]
        else:
            above = right_ok * jnp.where(flipped, outer[side], inner[side])
        up = jnp.where(row < rows - 1, pltpu.roll(f, rows - 1, 0), 0.0)
        down = jnp.where(row > 0, pltpu.roll(f, 1, 0), 0.0)
        ahead = jnp.where(lane < lanes - 1, pltpu.roll(f, lanes - 1, 1), 0.0)
        back = jnp.where(lane > 0, pltpu.roll(f, 1, 1), 0.0)
        return above - below, (up - down) * 0.5, (ahead - back) * 0.5

    for x in range(slab):
        v = slopes(velocity, half, x)
        q = slopes(density, half + 1, x)
        out[0, x] = v[1] * q[2] - v[2] * q[1]
        out[1, x] = v[2] * q[0] - v[0] * q[2]
        out[2, x] = v[0] * q[1] - v[1] * q[0]


def cross_gradient_of(count, velocity, density, outer, inner):
    return pl.pallas_call(
        functools.partial(cross_kernel, count),
        out_shape=shape((3,) + velocity.shape),
        in_specs=[VMEM] * 4,
        out_specs=VMEM,
        cost_estimate=pl.CostEstimate(
            flops=60 * velocity.size, bytes_accessed=24 * velocity.size, transcendentals=0
        ),
        compiler_params=room(8),
        name="cross_gradient",
    )(velocity, density, outer, inner)


def per_device(
    p_now, p_prev, velocity, density, wavelet, source_cell, receiver_cells, station_cells, observed
):
    slab, lateral, vertical = p_now.shape
    count = lax.axis_size("mp")
    stations = lax.axis_size("station")
    steps = wavelet.shape[0]
    half = slab // 2
    assert half == REACH and count % 2 == 0 and stations % 4 == 0
    total_x = slab * count
    m, core = position()
    s = lax.axis_index("station")
    block = lateral // stations
    chain = pairs_of(count, stations, chain_partner(count))
    together = lax.optimization_barrier

    def across(value):
        return lax.ppermute(value, AXES, chain)

    def swap(value, slab_bit, station_bit):
        pairs = pairs_of(count, stations, lambda i, k: (i ^ slab_bit, k ^ station_bit))
        return lax.ppermute(value, AXES, pairs)

    cur, message = first_message(p_now, velocity, density)
    outer = across(message)
    inner = swap(cur, 0, 1)
    edges = outer
    prev, cour, cour_outer, mask, dens = setup(count, source_cell, p_prev, velocity, density)
    pulses = jnp.broadcast_to(wavelet[:, None], (steps, 128))

    receiver_x, receiver_y = divmod_static(receiver_cells, lateral)
    receiver_j = receiver_x - m * slab
    receiver_j = jnp.where(core == 0, slab - 1 - receiver_j, receiver_j)
    inside = (receiver_j >= 0) & (receiver_j < half)
    place = jnp.where(inside, receiver_j * lateral + receiver_y, -1)[:, None]

    reach = min(total_x, 64)
    chunks = -(-total_x // reach)
    span = reach + slab - 1
    own_stations = station_cells.shape[0]
    n_stations = own_stations * stations

    def head_of(offset, cells):
        return jnp.concatenate([jnp.reshape(offset, (1,)).astype(jnp.int32), cells])

    def table_of(head):
        return gravity_table(total_x, slab, span, lateral, vertical, head)

    state = {"known": jnp.stack([station_cells.astype(F32), observed])[:, None, :]}

    def exchange(bit):
        def work(gate):
            known = gate(state["known"])
            other = swap(known, 0, bit)
            upper = (s // bit) % 2 == 1
            state["known"] = jnp.concatenate(
                [jnp.where(upper, other, known), jnp.where(upper, known, other)], 1
            )
            return "known"

        return work

    def share_edges(gate):
        state["inner"] = swap(gate(edges), 0, 1)
        return "inner"

    def cross(gate):
        state["cross"] = cross_gradient_of(count, velocity, density, edges, gate(state["inner"]))
        return "cross"

    def build_table(gate):
        cells = state["known"][0].reshape(-1).astype(jnp.int32)
        state["head"] = head_of(0, cells)
        state["table"] = table_of(gate(jnp.zeros((1,), jnp.int32)))
        return "table"

    pieces = 8
    part = n_stations // pieces

    def forward(i):
        def work(gate):
            state[i] = gravity_forward(
                i * part, part, 0, total_x, slab, lateral, gate(state["head"]), state["table"], dens
            )
            return i

        return work

    def gather_sums(gate):
        sums = jnp.concatenate([state[i] for i in range(pieces)])
        state["predicted"] = jnp.sum(gate(sums), axis=1).reshape(-1, 128)
        return "predicted"

    jobs = [exchange(1 << b) for b in range(stations.bit_length() - 1)]
    jobs.insert(1, share_edges)
    jobs.append(cross)
    if chunks == 1:
        jobs += [build_table] + [forward(i) for i in range(pieces)] + [gather_sums]

    surf = cour
    for step in range(steps):
        job = jobs.pop(0) if step and jobs else None
        done = None
        if step:
            if job is not None:
                gated = []

                def gate(value):
                    nonlocal cur
                    cur, value = together((cur, value))
                    gated.append(value)
                    return value

                done = job(gate)
            outer = across(cur)
            inner = swap(cur, 0, 1)
        base, surf = local_step(step, pulses, mask, cur, prev, cour, surf)
        cur, prev = halo_step(base, cour, cour_outer, outer, inner), cur
        if done is not None:
            cur, state[done] = together((cur, state[done]))
    assert not jobs

    all_observed = state["known"][1].reshape(-1, 128)
    cells = state["known"][0].reshape(-1).astype(jnp.int32)
    if chunks == 1:
        predicted = state["predicted"]
    else:

        def add_chunk(i, total):
            head = head_of(i * reach, cells)
            return total + gravity_forward(
                0, n_stations, reach, total_x, slab, lateral, head, table_of(head[:1]), dens
            )

        sums = lax.fori_loop(0, chunks, add_chunk, jnp.zeros((n_stations, vertical), F32))
        predicted = jnp.sum(sums, axis=1).reshape(-1, 128)

    sibling = swap(cur, 0, 1)
    packed = recorded_traces(steps - 1, place, cur, surf, predicted)
    other = swap(packed, 0, 1)
    if count & (count - 1) == 0:
        bit = 1
        while bit < count:
            packed = packed + other
            other = swap(packed, bit, 1)
            if bit == 1:
                wavefield = join(cur, sibling)
                other, wavefield = together((other, wavefield))
            bit *= 2
    else:
        wavefield = join(cur, sibling)
        packed = lax.psum(packed + other, "mp")
        other = jnp.zeros_like(packed)

    receivers = receiver_cells.shape[0]
    if chunks == 1:
        traces, own, density_gradient = gravity_last(
            steps,
            receivers,
            total_x,
            slab,
            block,
            lateral,
            state["head"],
            packed,
            other,
            all_observed,
            state["table"],
        )
        gravity_residual = own.reshape(-1)
    else:
        packed = packed + other
        blocks = receivers // 128
        traces = jnp.concatenate(
            [packed[b * steps : (b + 1) * steps] for b in range(blocks)], axis=1
        )
        residual = (packed[steps * blocks :] - all_observed).reshape(-1)
        gravity_residual = lax.dynamic_slice(residual, (s * own_stations,), (own_stations,))
        weights = residual.astype(jnp.bfloat16).astype(F32)

        def back_chunk(i, total):
            head = head_of(i * reach, cells)
            return total + gravity_adjoint(
                reach, total_x, slab, block, lateral, head, weights, table_of(head[:1])
            )

        density_gradient = lax.fori_loop(
            0, chunks, back_chunk, jnp.zeros((slab, block, vertical), F32)
        )
    return (wavefield, traces, gravity_residual, density_gradient, state["cross"])


def solution(mesh):
    in_specs = (
        P("mp", None, None),
        P("mp", None, None),
        P("mp", None, None),
        P("mp", None, None),
        P(),
        P(),
        P(),
        P("station"),
        P("station"),
    )
    out_specs = (
        P("mp", None, None),
        P(),
        P("station"),
        P("mp", "station", None),
        P(None, "mp", None, None),
    )
    return jax.shard_map(
        per_device, mesh=mesh, in_specs=in_specs, out_specs=out_specs, check_vma=False
    )
```

```python
import functools

import jax
import jax.numpy as jnp
from jax import lax
from jax.experimental import pallas as pl
from jax.experimental.pallas import tpu as pltpu
from jax.sharding import PartitionSpec as P

STENCIL = (-205.0 / 72.0, 8.0 / 5.0, -1.0 / 5.0, 8.0 / 315.0, -1.0 / 560.0)
TIME_RATIO = 0.1
REACH = 4
AXES = ("mp", "station")
VMEM = pl.BlockSpec(memory_space=pltpu.VMEM)
SMEM = pl.BlockSpec(memory_space=pltpu.SMEM)
HBM = pl.BlockSpec(memory_space=pltpu.HBM)
F32 = jnp.float32
MIB = 1 << 20


def room(mib):
    return pltpu.CompilerParams(vmem_limit_bytes=mib * MIB)


def shape(dims):
    return jax.ShapeDtypeStruct(dims, F32)


def pairs_of(count, stations, partner):
    return [
        (m * stations + s, (lambda t: t[0] * stations + t[1])(partner(m, s)))
        for m in range(count)
        for s in range(stations)
    ]


def chain_partner(count):
    def partner(m, s):
        if s % 2 == 0:
            return (m ^ 1, s)
        other = m + 1 if m % 2 else m - 1
        if other < 0 or other >= count:
            return (m, s ^ 2)
        return (other, s)

    return partner


def position():
    m = lax.axis_index("mp")
    return m, (m + lax.axis_index("station")) % 2 == 0


def divmod_static(value, divisor):
    if divisor & (divisor - 1) == 0:
        return value >> (divisor.bit_length() - 1), value & (divisor - 1)
    return value // divisor, value % divisor


def in_place(*values):
    return [pltpu.with_memory_space_constraint(value, pltpu.HBM) for value in values]


def run_copies(pairs, sems):
    copies = [pltpu.make_async_copy(a, b, sems.at[i]) for i, (a, b) in enumerate(pairs)]
    for copy in copies:
        copy.start()
    for copy in copies:
        copy.wait()


def plane_of(upper, j, slab):
    return jnp.where(upper, slab - 1 - j, j)


def first_kernel(now, velocity, density, cur, message, sems):
    slab = now.shape[0]
    half = slab // 2
    _, upper = position()
    pairs = []
    for j in range(half):
        plane = plane_of(upper, j, slab)
        pairs += [(now.at[plane], cur.at[j]), (now.at[plane], message.at[j])]
    edge = plane_of(upper, 0, slab)
    pairs += [(velocity.at[edge], message.at[half]), (density.at[edge], message.at[half + 1])]
    run_copies(pairs, sems)


def first_message(p_now, velocity, density):
    slab, rows, lanes = p_now.shape
    half = slab // 2
    return pl.pallas_call(
        first_kernel,
        out_shape=(shape((half, rows, lanes)), shape((half + 2, rows, lanes))),
        in_specs=[HBM] * 3,
        out_specs=(VMEM, VMEM),
        scratch_shapes=[pltpu.SemaphoreType.DMA((2 * half + 2,))],
        compiler_params=room(2),
        name="first_message",
    )(*in_place(p_now, velocity, density))


def setup_kernel(
    count, source, wavelet, p_prev, velocity, density, prev, cour, cour_outer, mask, dens, pulses, vel, raw, sems
):
    slab = p_prev.shape[0]
    half, rows, lanes = prev.shape
    m, upper = position()
    pairs = []
    for j in range(half):
        plane = plane_of(upper, j, slab)
        pairs += [(p_prev.at[plane], prev.at[j]), (velocity.at[plane], vel.at[j])]
    low = half * (lax.axis_index("station") % 2)
    pairs += [(density.at[pl.ds(low, half)], raw)]
    run_copies(pairs, sems)
    for n in range(pulses.shape[0]):
        pulses[n : n + 1, :] = jnp.full((1, lanes), wavelet[n], F32)
    outer_ok = jnp.where(upper, m < count - 1, m > 0)
    outer_ok = jnp.where(outer_ok, 1.0, 0.0)
    column, source_lane = divmod_static(source[0], lanes)
    source_x, source_row = divmod_static(column, rows)
    row = lax.broadcasted_iota(jnp.int32, (rows, lanes), 0)
    lane = lax.broadcasted_iota(jnp.int32, (rows, lanes), 1)
    spot = jnp.where((row == source_row) & (lane == source_lane), 1.0, 0.0)
    for j in range(half):
        scaled = TIME_RATIO * vel[j]
        square = scaled * scaled
        cour[j] = square
        cour_outer[j] = square * outer_ok
        here = m * slab + plane_of(upper, j, slab) == source_x
        mask[j] = spot * jnp.where(here, 1.0, 0.0)
        dens[j] = raw[j].astype(jnp.bfloat16).astype(F32)


def setup(count, source_cell, wavelet, p_prev, velocity, density):
    slab, rows, lanes = p_prev.shape
    half = slab // 2
    part = shape((half, rows, lanes))
    held = pltpu.VMEM((half, rows, lanes), F32)
    return pl.pallas_call(
        functools.partial(setup_kernel, count),
        out_shape=(part,) * 5 + (shape((wavelet.shape[0], lanes)),),
        in_specs=[SMEM, SMEM] + [HBM] * 3,
        out_specs=(VMEM,) * 6,
        scratch_shapes=[held, held, pltpu.SemaphoreType.DMA((2 * half + 1,))],
        compiler_params=room(4),
        cost_estimate=pl.CostEstimate(
            flops=20 * half * rows * lanes, bytes_accessed=32 * half * rows * lanes, transcendentals=0
        ),
        name="setup",
    )(source_cell, wavelet, *in_place(p_prev, velocity, density))


def local_kernel(step, pulses, mask, cur, prev, cour, surf_in, base, surf, pad):
    planes, rows, lanes = prev.shape
    lane = lax.broadcasted_iota(jnp.int32, (rows, lanes), 1)
    weights = {}
    for d in range(1, REACH + 1):
        weights[d] = jnp.where(lane >= d, STENCIL[d], 0.0)
        weights[-d] = jnp.where(lane < lanes - d, STENCIL[d], 0.0)
    pulse = pulses[step : step + 1, :]
    for j in range(planes):
        pad[j, 0:8, :] = jnp.zeros((8, lanes), F32)
        pad[j, 8 + rows : 16 + rows, :] = jnp.zeros((8, lanes), F32)
        pad[j, 8 : 8 + rows, :] = cur[j]
    for j in range(planes):
        c = cur[j]
        acc = 3.0 * STENCIL[0] * c
        for d in range(1, REACH + 1):
            acc = acc + weights[d] * pltpu.roll(c, d, 1) + weights[-d] * pltpu.roll(c, lanes - d, 1)
            near = pad[j, 8 + d : 8 + d + rows, :] + pad[j, 8 - d : 8 - d + rows, :]
            for i in (j - d, j + d):
                if 0 <= i < planes:
                    near = near + cur[i]
            acc = acc + STENCIL[d] * near
        base[j] = 2.0 * c - prev[j] + cour[j] * acc + pulse * mask[j]
        if step == 0:
            surf[j] = jnp.zeros((rows, lanes), F32)
        else:
            surf[j] = jnp.where(
                lane == step - 1, jnp.broadcast_to(c[:, 0:1], (rows, lanes)), surf_in[j]
            )


def local_step(step, pulses, mask, cur, prev, cour, surf):
    planes, rows, lanes = cur.shape
    return pl.pallas_call(
        functools.partial(local_kernel, step),
        out_shape=(shape(cur.shape), shape(cur.shape)),
        in_specs=[VMEM] * 6,
        out_specs=(VMEM, VMEM),
        scratch_shapes=[pltpu.VMEM((planes, rows + 16, lanes), F32)],
        compiler_params=room(2),
        cost_estimate=pl.CostEstimate(
            flops=60 * cur.size, bytes_accessed=24 * cur.size, transcendentals=0
        ),
        name="wave_local",
    )(pulses, mask, cur, prev, cour, surf)


def halo_kernel(base, cour, cour_outer, outer, inner, out):
    planes = base.shape[0]
    for j in range(planes):
        far = near = None
        for d in range(j + 1, REACH + 1):
            term = STENCIL[d] * outer[d - j - 1]
            far = term if far is None else far + term
        for d in range(planes - j, REACH + 1):
            term = STENCIL[d] * inner[2 * planes - 1 - j - d]
            near = term if near is None else near + term
        out[j] = base[j] + (cour[j] * near + cour_outer[j] * far)


def halo_step(base, cour, cour_outer, outer, inner):
    return pl.pallas_call(
        halo_kernel,
        out_shape=shape(base.shape),
        in_specs=[VMEM] * 5,
        out_specs=VMEM,
        compiler_params=room(2),
        cost_estimate=pl.CostEstimate(
            flops=12 * base.size, bytes_accessed=20 * base.size, transcendentals=0
        ),
        name="wave_halo",
    )(base, cour, cour_outer, outer, inner)


def trace_kernel(step, place, cur, surf, predicted, kept, out):
    del kept
    planes, rows, lanes = cur.shape
    receivers = place.shape[0]
    steps = step + 1
    lane = lax.broadcasted_iota(jnp.int32, (rows, lanes), 1)
    columns = jnp.concatenate(
        [
            jnp.where(lane == step, jnp.broadcast_to(cur[j, :, 0:1], (rows, lanes)), surf[j])
            for j in range(planes)
        ],
        0,
    )
    where = lax.broadcasted_iota(jnp.int32, (receivers, planes * rows), 1)
    pick = jnp.where(place[...] == where, 1.0, 0.0).astype(jnp.bfloat16)
    total = None
    for _ in range(3):
        part = columns.astype(jnp.bfloat16)
        columns = columns - part.astype(F32)
        term = jnp.dot(pick, part, preferred_element_type=F32)
        total = term if total is None else total + term
    total = total.T
    for b in range(receivers // 128):
        out[b * steps : (b + 1) * steps, :] = total[:steps, b * 128 : (b + 1) * 128]
    out[steps * (receivers // 128) :, :] = predicted[...]


def recorded_traces(step, place, cur, surf, predicted, kept):
    rows = (step + 1) * (place.shape[0] // 128) + predicted.shape[0]
    return pl.pallas_call(
        functools.partial(trace_kernel, step),
        out_shape=shape((rows, 128)),
        in_specs=[VMEM] * 5,
        out_specs=VMEM,
        compiler_params=room(4),
        name="traces",
    )(place, cur, surf, predicted, kept)


def join_kernel(own, sibling, kept, out, sems):
    del kept
    slab = out.shape[0]
    _, upper = position()
    pairs = []
    for j in range(slab // 2):
        here = plane_of(upper, j, slab)
        pairs += [(own.at[j], out.at[here]), (sibling.at[j], out.at[slab - 1 - here])]
    run_copies(pairs, sems)


def join(own, sibling, kept):
    half, rows, lanes = own.shape
    return pl.pallas_call(
        join_kernel,
        out_shape=shape((2 * half, rows, lanes)),
        in_specs=[VMEM] * 3,
        out_specs=HBM,
        scratch_shapes=[pltpu.SemaphoreType.DMA((2 * half,))],
        compiler_params=room(2),
        name="join",
    )(own, sibling, kept)


def on_chip(value):
    return pltpu.with_memory_space_constraint(value, pltpu.VMEM)


def table_low(total_x, slab, offset):
    m, _ = position()
    return m * slab - (total_x - 1) + offset


def table_kernel(total_x, slab, spread, head, out):
    lanes = out.shape[1]
    low = table_low(total_x, slab, head[0])
    dy = (lax.broadcasted_iota(jnp.int32, (spread, lanes), 0) - (spread // 2 - 1)).astype(F32)
    dz = (lax.broadcasted_iota(jnp.int32, (spread, lanes), 1) + 1).astype(F32)
    side = dy * dy
    deep = dz * dz

    def one(t, carry):
        dx = (t + low).astype(F32)
        square = dx * dx + side + deep
        value = dz / (square * jnp.sqrt(square))
        start = pl.multiple_of(t * spread, spread)
        out[pl.ds(start, spread), :] = value.astype(jnp.bfloat16).astype(F32)
        return carry

    lax.fori_loop(0, out.shape[0] // spread, one, 0)


def gravity_table(total_x, slab, depth, lateral, vertical, head):
    size = depth * 2 * lateral * vertical
    return pl.pallas_call(
        functools.partial(table_kernel, total_x, slab, 2 * lateral),
        out_shape=shape((depth * 2 * lateral, vertical)),
        in_specs=[SMEM],
        out_specs=VMEM,
        cost_estimate=pl.CostEstimate(
            flops=20 * size, bytes_accessed=4 * size, transcendentals=2 * size
        ),
        compiler_params=room(8),
        name="gravity_table",
    )(head)


def forward_kernel(first, guard, total_x, slab, lateral, head, table, dens, out):
    planes, rows, lanes = dens.shape
    count = out.shape[0]
    spread = 2 * lateral
    core = lax.axis_index("station") % 2
    lead = total_x - 1 - head[0]
    if guard:
        out[...] = jnp.zeros_like(out)

    def one(s, carry):
        sx, sy = divmod_static(head[1 + first + s], lateral)
        shift = lead - sx
        start = (shift + core * planes) * spread + (lateral - 1 - sy)

        def accumulate():
            acc = None
            for p in range(planes):
                term = table[pl.ds(start + p * spread, rows), :] * dens[p]
                acc = term if acc is None else acc + term
            out[pl.ds(s, 1), :] = jnp.sum(acc, axis=0, keepdims=True)

        if guard:
            pl.when((shift >= 0) & (shift < guard))(accumulate)
        else:
            accumulate()
        return carry

    lax.fori_loop(0, count, one, 0, unroll=4)


def gravity_forward(first, count, guard, total_x, slab, lateral, head, table, dens):
    work = count * dens.size
    return pl.pallas_call(
        functools.partial(forward_kernel, first, guard, total_x, slab, lateral),
        out_shape=shape((count, dens.shape[2])),
        in_specs=[SMEM, VMEM, VMEM],
        out_specs=VMEM,
        cost_estimate=pl.CostEstimate(
            flops=4 * work, bytes_accessed=4 * dens.size, transcendentals=0
        ),
        compiler_params=room(8),
        name="gravity_forward",
    )(head, on_chip(table), dens)


def spread_back(guard, total_x, lateral, row_low, head, weights, table, out):
    slab, rows, lanes = out.shape
    groups = (head.shape[0] - 1) // 128
    spread = 2 * lateral
    lead = total_x - 1 - head[0]

    def one(k, i, acc):
        sx, sy = divmod_static(head[1 + 128 * k + i], lateral)
        shift = lead - sx
        weight = weights(k, i)
        if guard:
            keep = (shift >= 0) & (shift < guard)
            shift = jnp.where(keep, shift, 0)
            weight = jnp.where(keep, weight, 0.0)
        start = shift * spread + (lateral - 1 - sy + row_low)
        return tuple(
            acc[x] + weight * table[pl.ds(start + x * spread, rows), :] for x in range(slab)
        )

    zero = jnp.zeros((rows, lanes), F32)
    acc = (zero,) * slab
    for k in range(groups):
        acc = lax.fori_loop(0, 128, functools.partial(one, k), acc, unroll=4)
    for x in range(slab):
        out[x] = acc[x]


def adjoint_kernel(guard, total_x, lateral, head, weights, table, out):
    row_low = lax.axis_index("station") * out.shape[1]
    spread_back(guard, total_x, lateral, row_low, head, lambda k, i: weights[128 * k + i], table, out)


def gravity_adjoint(guard, total_x, slab, rows, lateral, head, weights, table):
    return pl.pallas_call(
        functools.partial(adjoint_kernel, guard, total_x, lateral),
        out_shape=shape((slab, rows, table.shape[1])),
        in_specs=[SMEM, SMEM, VMEM],
        out_specs=VMEM,
        compiler_params=room(8),
        name="gravity_adjoint",
    )(head, weights, table)


def last_kernel(total_x, lateral, head, packed, other, observed, table, traces, own, out, held, scalars, sem):
    steps, receivers = traces.shape
    blocks = receivers // 128
    total = packed[...] + other[...]
    residual = total[steps * blocks :, :] - observed[...]
    held[...] = residual.astype(jnp.bfloat16).astype(F32)
    copy = pltpu.make_async_copy(held, scalars, sem)
    copy.start()
    for b in range(blocks):
        traces[:, b * 128 : (b + 1) * 128] = total[b * steps : (b + 1) * steps, :]
    s = lax.axis_index("station")
    mine = own.shape[0]
    for k in range(residual.shape[0] // mine):

        @pl.when(s == k)
        def _(k=k):
            own[...] = residual[k * mine : (k + 1) * mine, :]

    copy.wait()
    spread_back(
        0,
        total_x,
        lateral,
        s * out.shape[1],
        head,
        lambda k, i: scalars[k, i],
        table,
        out,
    )


def gravity_last(steps, receivers, total_x, slab, rows, lateral, head, packed, other, observed, table):
    count = lax.axis_size("station")
    lines = observed.shape[0]
    return pl.pallas_call(
        functools.partial(last_kernel, total_x, lateral),
        out_shape=(
            shape((steps, receivers)),
            shape((lines // count, 128)),
            shape((slab, rows, table.shape[1])),
        ),
        in_specs=[SMEM] + [VMEM] * 4,
        out_specs=(VMEM,) * 3,
        scratch_shapes=[
            pltpu.VMEM((lines, 128), F32),
            pltpu.SMEM((lines, 128), F32),
            pltpu.SemaphoreType.DMA,
        ],
        compiler_params=room(8),
        name="gravity_last",
    )(head, packed, other, observed, on_chip(table))


def cross_kernel(count, velocity, density, outer, inner, out):
    slab, rows, lanes = velocity.shape
    half = slab // 2
    lane = lax.broadcasted_iota(jnp.int32, (rows, lanes), 1)
    row = lax.broadcasted_iota(jnp.int32, (rows, lanes), 0)
    m, flipped = position()
    left_ok = jnp.where(m > 0, 0.5, 0.0)
    right_ok = jnp.where(m < count - 1, 0.5, 0.0)

    def slopes(field, side, x):
        f = field[x]
        if x > 0:
            below = 0.5 * field[x - 1]
        else:
            below = left_ok * jnp.where(flipped, inner[side], outer[side])
        if x < slab - 1:
            above = 0.5 * field[x + 1]
        else:
            above = right_ok * jnp.where(flipped, outer[side], inner[side])
        up = jnp.where(row < rows - 1, pltpu.roll(f, rows - 1, 0), 0.0)
        down = jnp.where(row > 0, pltpu.roll(f, 1, 0), 0.0)
        ahead = jnp.where(lane < lanes - 1, pltpu.roll(f, lanes - 1, 1), 0.0)
        back = jnp.where(lane > 0, pltpu.roll(f, 1, 1), 0.0)
        return above - below, (up - down) * 0.5, (ahead - back) * 0.5

    for x in range(slab):
        v = slopes(velocity, half, x)
        q = slopes(density, half + 1, x)
        out[0, x] = v[1] * q[2] - v[2] * q[1]
        out[1, x] = v[2] * q[0] - v[0] * q[2]
        out[2, x] = v[0] * q[1] - v[1] * q[0]


def cross_gradient_of(count, velocity, density, outer, inner):
    return pl.pallas_call(
        functools.partial(cross_kernel, count),
        out_shape=shape((3,) + velocity.shape),
        in_specs=[VMEM] * 4,
        out_specs=VMEM,
        cost_estimate=pl.CostEstimate(
            flops=60 * velocity.size, bytes_accessed=24 * velocity.size, transcendentals=0
        ),
        compiler_params=room(8),
        name="cross_gradient",
    )(velocity, density, outer, inner)


def per_device(
    p_now, p_prev, velocity, density, wavelet, source_cell, receiver_cells, station_cells, observed
):
    slab, lateral, vertical = p_now.shape
    count = lax.axis_size("mp")
    stations = lax.axis_size("station")
    steps = wavelet.shape[0]
    half = slab // 2
    assert half == REACH and count % 2 == 0 and stations % 4 == 0
    total_x = slab * count
    m, upper = position()
    s = lax.axis_index("station")
    block = lateral // stations
    chain = pairs_of(count, stations, chain_partner(count))
    together = lax.optimization_barrier

    def across(value):
        return lax.ppermute(value, AXES, chain)

    def swap(value, slab_bit, station_bit):
        pairs = pairs_of(count, stations, lambda i, k: (i ^ slab_bit, k ^ station_bit))
        return lax.ppermute(value, AXES, pairs)

    cur, message = first_message(p_now, velocity, density)
    outer = across(message)
    inner = swap(cur, 0, 1)
    edges = outer
    prev, cour, cour_outer, mask, dens, pulses = setup(
        count, source_cell, wavelet, p_prev, velocity, density
    )

    receiver_x, receiver_y = divmod_static(receiver_cells, lateral)
    receiver_j = receiver_x - m * slab
    receiver_j = jnp.where(upper, slab - 1 - receiver_j, receiver_j)
    inside = (receiver_j >= 0) & (receiver_j < half)
    place = jnp.where(inside, receiver_j * lateral + receiver_y, -1)[:, None]

    reach = min(total_x, 64)
    chunks = -(-total_x // reach)
    span = reach + slab - 1
    own_stations = station_cells.shape[0]
    n_stations = own_stations * stations

    def head_of(offset, cells):
        return jnp.concatenate([jnp.reshape(offset, (1,)).astype(jnp.int32), cells])

    def table_of(head):
        return gravity_table(total_x, slab, span, lateral, vertical, head)

    state = {}

    def exchange(bit):
        def work(gate):
            if bit == 1:
                known = jnp.stack([gate(station_cells).astype(F32), observed])[:, None, :]
            else:
                known = gate(state["known"])
            other = swap(known, 0, bit)
            upper = (s // bit) % 2 == 1
            state["known"] = jnp.concatenate(
                [jnp.where(upper, other, known), jnp.where(upper, known, other)], 1
            )
            return "known"

        return work

    def share_edges(gate):
        state["inner"] = swap(gate(edges), 0, 1)
        return "inner"

    def cross(gate):
        state["cross"] = cross_gradient_of(count, velocity, density, edges, gate(state["inner"]))
        return "cross"

    def build_table(gate):
        cells = state["known"][0].reshape(-1).astype(jnp.int32)
        state["head"] = head_of(0, cells)
        state["table"] = table_of(gate(jnp.zeros((1,), jnp.int32)))
        return "table"

    pieces = 8
    part = n_stations // pieces

    def forward(i):
        def work(gate):
            state[i] = gravity_forward(
                i * part, part, 0, total_x, slab, lateral, gate(state["head"]), state["table"], dens
            )
            return i

        return work

    def gather_sums(gate):
        sums = jnp.concatenate([state[i] for i in range(pieces)])
        state["predicted"] = jnp.sum(gate(sums), axis=1).reshape(-1, 128)
        return "predicted"

    jobs = [exchange(1 << b) for b in range(stations.bit_length() - 1)]
    jobs.insert(1, share_edges)
    jobs += [cross, None]
    if chunks == 1:
        jobs += [build_table] + [forward(i) for i in range(pieces)] + [gather_sums]

    surf = cour
    for step in range(steps):
        job = jobs.pop(0) if step and jobs else None
        done = None
        if step:
            if job is not None:
                gated = []

                def gate(value):
                    nonlocal cur
                    cur, value = together((cur, value))
                    gated.append(value)
                    return value

                done = job(gate)
            outer = across(cur)
            inner = swap(cur, 0, 1)
        base, surf = local_step(step, pulses, mask, cur, prev, cour, surf)
        cur, prev = halo_step(base, cour, cour_outer, outer, inner), cur
        if done is not None:
            cur, state[done] = together((cur, state[done]))
    assert not any(jobs)

    all_observed = state["known"][1].reshape(-1, 128)
    cells = state["known"][0].reshape(-1).astype(jnp.int32)
    if chunks == 1:
        predicted = state["predicted"]
    else:

        def add_chunk(i, total):
            head = head_of(i * reach, cells)
            return total + gravity_forward(
                0, n_stations, reach, total_x, slab, lateral, head, table_of(head[:1]), dens
            )

        sums = lax.fori_loop(0, chunks, add_chunk, jnp.zeros((n_stations, vertical), F32))
        predicted = jnp.sum(sums, axis=1).reshape(-1, 128)

    kept = state["table"] if chunks == 1 else predicted
    sibling = swap(cur, 0, 1)
    packed = recorded_traces(steps - 1, place, cur, surf, predicted, kept)
    other = swap(packed, 0, 1)
    if count & (count - 1) == 0:
        bit = 1
        while bit < count:
            packed = packed + other
            other = swap(packed, bit, 1)
            if bit == 1:
                wavefield = join(cur, sibling, kept)
                other, wavefield = together((other, wavefield))
            bit *= 2
    else:
        wavefield = join(cur, sibling, kept)
        packed = lax.psum(packed + other, "mp")
        other = jnp.zeros_like(packed)

    receivers = receiver_cells.shape[0]
    if chunks == 1:
        traces, own, density_gradient = gravity_last(
            steps,
            receivers,
            total_x,
            slab,
            block,
            lateral,
            state["head"],
            packed,
            other,
            all_observed,
            state["table"],
        )
        gravity_residual = own.reshape(-1)
    else:
        packed = packed + other
        blocks = receivers // 128
        traces = jnp.concatenate(
            [packed[b * steps : (b + 1) * steps] for b in range(blocks)], axis=1
        )
        residual = (packed[steps * blocks :] - all_observed).reshape(-1)
        gravity_residual = lax.dynamic_slice(residual, (s * own_stations,), (own_stations,))
        weights = residual.astype(jnp.bfloat16).astype(F32)

        def back_chunk(i, total):
            head = head_of(i * reach, cells)
            return total + gravity_adjoint(
                reach, total_x, slab, block, lateral, head, weights, table_of(head[:1])
            )

        density_gradient = lax.fori_loop(
            0, chunks, back_chunk, jnp.zeros((slab, block, vertical), F32)
        )
    return (wavefield, traces, gravity_residual, density_gradient, state["cross"])


def solution(mesh):
    in_specs = (
        P("mp", None, None),
        P("mp", None, None),
        P("mp", None, None),
        P("mp", None, None),
        P(),
        P(),
        P(),
        P("station"),
        P("station"),
    )
    out_specs = (
        P("mp", None, None),
        P(),
        P("station"),
        P("mp", "station", None),
        P(None, "mp", None, None),
    )
    return jax.shard_map(
        per_device, mesh=mesh, in_specs=in_specs, out_specs=out_specs, check_vma=False
    )
```

```python
import functools

import jax
import jax.numpy as jnp
from jax import lax
from jax.experimental import pallas as pl
from jax.experimental.pallas import tpu as pltpu
from jax.sharding import PartitionSpec as P

STENCIL = (-205.0 / 72.0, 8.0 / 5.0, -1.0 / 5.0, 8.0 / 315.0, -1.0 / 560.0)
TIME_RATIO = 0.1
REACH = 4
AXES = ("mp", "station")
VMEM = pl.BlockSpec(memory_space=pltpu.VMEM)
SMEM = pl.BlockSpec(memory_space=pltpu.SMEM)
HBM = pl.BlockSpec(memory_space=pltpu.HBM)
F32 = jnp.float32
MIB = 1 << 20


def room(mib):
    return pltpu.CompilerParams(vmem_limit_bytes=mib * MIB)


def shape(dims):
    return jax.ShapeDtypeStruct(dims, F32)


def pairs_of(count, stations, partner):
    return [
        (m * stations + s, (lambda t: t[0] * stations + t[1])(partner(m, s)))
        for m in range(count)
        for s in range(stations)
    ]


def chain_partner(count):
    def partner(m, s):
        if s % 2 == 0:
            return (m ^ 1, s)
        other = m + 1 if m % 2 else m - 1
        if other < 0 or other >= count:
            return (m, s ^ 2)
        return (other, s)

    return partner


def position():
    m = lax.axis_index("mp")
    return m, (m + lax.axis_index("station")) % 2 == 0


def divmod_static(value, divisor):
    if divisor & (divisor - 1) == 0:
        return value >> (divisor.bit_length() - 1), value & (divisor - 1)
    return value // divisor, value % divisor


def in_place(*values):
    return [pltpu.with_memory_space_constraint(value, pltpu.HBM) for value in values]


def run_copies(pairs, sems):
    copies = [pltpu.make_async_copy(a, b, sems.at[i]) for i, (a, b) in enumerate(pairs)]
    for copy in copies:
        copy.start()
    for copy in copies:
        copy.wait()


def plane_of(upper, j, slab):
    return jnp.where(upper, slab - 1 - j, j)


def first_kernel(now, velocity, density, cur, message, sems):
    slab = now.shape[0]
    half = slab // 2
    _, upper = position()
    pairs = []
    for j in range(half):
        plane = plane_of(upper, j, slab)
        pairs += [(now.at[plane], cur.at[j]), (now.at[plane], message.at[j])]
    edge = plane_of(upper, 0, slab)
    pairs += [(velocity.at[edge], message.at[half]), (density.at[edge], message.at[half + 1])]
    run_copies(pairs, sems)


def first_message(p_now, velocity, density):
    slab, rows, lanes = p_now.shape
    half = slab // 2
    return pl.pallas_call(
        first_kernel,
        out_shape=(shape((half, rows, lanes)), shape((half + 2, rows, lanes))),
        in_specs=[HBM] * 3,
        out_specs=(VMEM, VMEM),
        scratch_shapes=[pltpu.SemaphoreType.DMA((2 * half + 2,))],
        compiler_params=room(2),
        name="first_message",
    )(*in_place(p_now, velocity, density))


def setup_kernel(
    count, source, wavelet, p_prev, velocity, density, prev, cour, cour_outer, mask, dens, pulses, vel, raw, sems
):
    slab = p_prev.shape[0]
    half, rows, lanes = prev.shape
    m, upper = position()
    pairs = []
    for j in range(half):
        plane = plane_of(upper, j, slab)
        pairs += [(p_prev.at[plane], prev.at[j]), (velocity.at[plane], vel.at[j])]
    low = half * (lax.axis_index("station") % 2)
    pairs += [(density.at[pl.ds(low, half)], raw)]
    run_copies(pairs, sems)
    for n in range(pulses.shape[0]):
        pulses[n : n + 1, :] = jnp.full((1, lanes), wavelet[n], F32)
    outer_ok = jnp.where(upper, m < count - 1, m > 0)
    outer_ok = jnp.where(outer_ok, 1.0, 0.0)
    column, source_lane = divmod_static(source[0], lanes)
    source_x, source_row = divmod_static(column, rows)
    row = lax.broadcasted_iota(jnp.int32, (rows, lanes), 0)
    lane = lax.broadcasted_iota(jnp.int32, (rows, lanes), 1)
    spot = jnp.where((row == source_row) & (lane == source_lane), 1.0, 0.0)
    for j in range(half):
        scaled = TIME_RATIO * vel[j]
        square = scaled * scaled
        cour[j] = square
        cour_outer[j] = square * outer_ok
        here = m * slab + plane_of(upper, j, slab) == source_x
        mask[j] = spot * jnp.where(here, 1.0, 0.0)
        dens[j] = raw[j].astype(jnp.bfloat16).astype(F32)


def setup(count, source_cell, wavelet, p_prev, velocity, density):
    slab, rows, lanes = p_prev.shape
    half = slab // 2
    part = shape((half, rows, lanes))
    held = pltpu.VMEM((half, rows, lanes), F32)
    return pl.pallas_call(
        functools.partial(setup_kernel, count),
        out_shape=(part,) * 5 + (shape((wavelet.shape[0], lanes)),),
        in_specs=[SMEM, SMEM] + [HBM] * 3,
        out_specs=(VMEM,) * 6,
        scratch_shapes=[held, held, pltpu.SemaphoreType.DMA((2 * half + 1,))],
        compiler_params=room(4),
        cost_estimate=pl.CostEstimate(
            flops=20 * half * rows * lanes, bytes_accessed=32 * half * rows * lanes, transcendentals=0
        ),
        name="setup",
    )(source_cell, wavelet, *in_place(p_prev, velocity, density))


def local_kernel(step, pulses, mask, cur, prev, cour, surf_in, base, surf, pad):
    planes, rows, lanes = prev.shape
    lane = lax.broadcasted_iota(jnp.int32, (rows, lanes), 1)
    weights = {}
    for d in range(1, REACH + 1):
        weights[d] = jnp.where(lane >= d, STENCIL[d], 0.0)
        weights[-d] = jnp.where(lane < lanes - d, STENCIL[d], 0.0)
    pulse = pulses[step : step + 1, :]
    for j in range(planes):
        pad[j, 0:8, :] = jnp.zeros((8, lanes), F32)
        pad[j, 8 + rows : 16 + rows, :] = jnp.zeros((8, lanes), F32)
        pad[j, 8 : 8 + rows, :] = cur[j]
    for j in range(planes):
        c = cur[j]
        acc = 3.0 * STENCIL[0] * c
        for d in range(1, REACH + 1):
            acc = acc + weights[d] * pltpu.roll(c, d, 1) + weights[-d] * pltpu.roll(c, lanes - d, 1)
            near = pad[j, 8 + d : 8 + d + rows, :] + pad[j, 8 - d : 8 - d + rows, :]
            for i in (j - d, j + d):
                if 0 <= i < planes:
                    near = near + cur[i]
            acc = acc + STENCIL[d] * near
        base[j] = 2.0 * c - prev[j] + cour[j] * acc + pulse * mask[j]
        if step == 0:
            surf[j] = jnp.zeros((rows, lanes), F32)
        else:
            surf[j] = jnp.where(
                lane == step - 1, jnp.broadcast_to(c[:, 0:1], (rows, lanes)), surf_in[j]
            )


def local_step(step, pulses, mask, cur, prev, cour, surf):
    planes, rows, lanes = cur.shape
    return pl.pallas_call(
        functools.partial(local_kernel, step),
        out_shape=(shape(cur.shape), shape(cur.shape)),
        in_specs=[VMEM] * 6,
        out_specs=(VMEM, VMEM),
        scratch_shapes=[pltpu.VMEM((planes, rows + 16, lanes), F32)],
        compiler_params=room(2),
        cost_estimate=pl.CostEstimate(
            flops=60 * cur.size, bytes_accessed=24 * cur.size, transcendentals=0
        ),
        name="wave_local",
    )(pulses, mask, cur, prev, cour, surf)


def halo_kernel(base, cour, cour_outer, outer, inner, out):
    planes = base.shape[0]
    for j in range(planes):
        far = near = None
        for d in range(j + 1, REACH + 1):
            term = STENCIL[d] * outer[d - j - 1]
            far = term if far is None else far + term
        for d in range(planes - j, REACH + 1):
            term = STENCIL[d] * inner[2 * planes - 1 - j - d]
            near = term if near is None else near + term
        out[j] = base[j] + (cour[j] * near + cour_outer[j] * far)


def halo_step(base, cour, cour_outer, outer, inner):
    return pl.pallas_call(
        halo_kernel,
        out_shape=shape(base.shape),
        in_specs=[VMEM] * 5,
        out_specs=VMEM,
        compiler_params=room(2),
        cost_estimate=pl.CostEstimate(
            flops=12 * base.size, bytes_accessed=20 * base.size, transcendentals=0
        ),
        name="wave_halo",
    )(base, cour, cour_outer, outer, inner)


def trace_kernel(step, place, cur, surf, predicted, out):
    planes, rows, lanes = cur.shape
    receivers = place.shape[0]
    steps = step + 1
    lane = lax.broadcasted_iota(jnp.int32, (rows, lanes), 1)
    columns = jnp.concatenate(
        [
            jnp.where(lane == step, jnp.broadcast_to(cur[j, :, 0:1], (rows, lanes)), surf[j])
            for j in range(planes)
        ],
        0,
    )
    where = lax.broadcasted_iota(jnp.int32, (receivers, planes * rows), 1)
    pick = jnp.where(place[...] == where, 1.0, 0.0).astype(jnp.bfloat16)
    total = None
    for _ in range(3):
        part = columns.astype(jnp.bfloat16)
        columns = columns - part.astype(F32)
        term = jnp.dot(pick, part, preferred_element_type=F32)
        total = term if total is None else total + term
    total = total.T
    for b in range(receivers // 128):
        out[b * steps : (b + 1) * steps, :] = total[:steps, b * 128 : (b + 1) * 128]
    out[steps * (receivers // 128) :, :] = predicted[...]


def recorded_traces(step, place, cur, surf, predicted):
    rows = (step + 1) * (place.shape[0] // 128) + predicted.shape[0]
    return pl.pallas_call(
        functools.partial(trace_kernel, step),
        out_shape=shape((rows, 128)),
        in_specs=[VMEM] * 4,
        out_specs=VMEM,
        compiler_params=room(4),
        name="traces",
    )(place, cur, surf, predicted)


def join_kernel(own, sibling, kept, out, sems):
    del kept
    slab = out.shape[0]
    _, upper = position()
    pairs = []
    for j in range(slab // 2):
        here = plane_of(upper, j, slab)
        pairs += [(own.at[j], out.at[here]), (sibling.at[j], out.at[slab - 1 - here])]
    run_copies(pairs, sems)


def join(own, sibling, kept):
    half, rows, lanes = own.shape
    return pl.pallas_call(
        join_kernel,
        out_shape=shape((2 * half, rows, lanes)),
        in_specs=[VMEM] * 3,
        out_specs=HBM,
        scratch_shapes=[pltpu.SemaphoreType.DMA((2 * half,))],
        compiler_params=room(2),
        name="join",
    )(own, sibling, kept)


def on_chip(value):
    return pltpu.with_memory_space_constraint(value, pltpu.VMEM)


def table_low(total_x, slab, offset):
    m, _ = position()
    return m * slab - (total_x - 1) + offset


def table_kernel(total_x, slab, spread, head, out):
    lanes = out.shape[1]
    low = table_low(total_x, slab, head[0])
    dy = (lax.broadcasted_iota(jnp.int32, (spread, lanes), 0) - (spread // 2 - 1)).astype(F32)
    dz = (lax.broadcasted_iota(jnp.int32, (spread, lanes), 1) + 1).astype(F32)
    side = dy * dy
    deep = dz * dz

    def one(t, carry):
        dx = (t + low).astype(F32)
        square = dx * dx + side + deep
        value = dz / (square * jnp.sqrt(square))
        start = pl.multiple_of(t * spread, spread)
        out[pl.ds(start, spread), :] = value.astype(jnp.bfloat16).astype(F32)
        return carry

    lax.fori_loop(0, out.shape[0] // spread, one, 0)


def gravity_table(total_x, slab, depth, lateral, vertical, head):
    size = depth * 2 * lateral * vertical
    return pl.pallas_call(
        functools.partial(table_kernel, total_x, slab, 2 * lateral),
        out_shape=shape((depth * 2 * lateral, vertical)),
        in_specs=[SMEM],
        out_specs=VMEM,
        cost_estimate=pl.CostEstimate(
            flops=20 * size, bytes_accessed=4 * size, transcendentals=2 * size
        ),
        compiler_params=room(8),
        name="gravity_table",
    )(head)


def forward_kernel(first, guard, total_x, slab, lateral, head, table, dens, out):
    planes, rows, lanes = dens.shape
    count = out.shape[0]
    spread = 2 * lateral
    core = lax.axis_index("station") % 2
    lead = total_x - 1 - head[0]
    if guard:
        out[...] = jnp.zeros_like(out)

    def one(s, carry):
        sx, sy = divmod_static(head[1 + first + s], lateral)
        shift = lead - sx
        start = (shift + core * planes) * spread + (lateral - 1 - sy)

        def accumulate():
            acc = None
            for p in range(planes):
                term = table[pl.ds(start + p * spread, rows), :] * dens[p]
                acc = term if acc is None else acc + term
            out[pl.ds(s, 1), :] = jnp.sum(acc, axis=0, keepdims=True)

        if guard:
            pl.when((shift >= 0) & (shift < guard))(accumulate)
        else:
            accumulate()
        return carry

    lax.fori_loop(0, count, one, 0, unroll=4)


def gravity_forward(first, count, guard, total_x, slab, lateral, head, table, dens):
    work = count * dens.size
    return pl.pallas_call(
        functools.partial(forward_kernel, first, guard, total_x, slab, lateral),
        out_shape=shape((count, dens.shape[2])),
        in_specs=[SMEM, VMEM, VMEM],
        out_specs=VMEM,
        cost_estimate=pl.CostEstimate(
            flops=4 * work, bytes_accessed=4 * dens.size, transcendentals=0
        ),
        compiler_params=room(8),
        name="gravity_forward",
    )(head, on_chip(table), dens)


def spread_back(guard, total_x, lateral, row_low, head, weights, table, out):
    slab, rows, lanes = out.shape
    groups = (head.shape[0] - 1) // 128
    spread = 2 * lateral
    lead = total_x - 1 - head[0]

    def one(k, i, acc):
        sx, sy = divmod_static(head[1 + 128 * k + i], lateral)
        shift = lead - sx
        weight = weights(k, i)
        if guard:
            keep = (shift >= 0) & (shift < guard)
            shift = jnp.where(keep, shift, 0)
            weight = jnp.where(keep, weight, 0.0)
        start = shift * spread + (lateral - 1 - sy + row_low)
        return tuple(
            acc[x] + weight * table[pl.ds(start + x * spread, rows), :] for x in range(slab)
        )

    zero = jnp.zeros((rows, lanes), F32)
    acc = (zero,) * slab
    for k in range(groups):
        acc = lax.fori_loop(0, 128, functools.partial(one, k), acc, unroll=4)
    for x in range(slab):
        out[x] = acc[x]


def adjoint_kernel(guard, total_x, lateral, head, weights, table, out):
    row_low = lax.axis_index("station") * out.shape[1]
    spread_back(guard, total_x, lateral, row_low, head, lambda k, i: weights[128 * k + i], table, out)


def gravity_adjoint(guard, total_x, slab, rows, lateral, head, weights, table):
    return pl.pallas_call(
        functools.partial(adjoint_kernel, guard, total_x, lateral),
        out_shape=shape((slab, rows, table.shape[1])),
        in_specs=[SMEM, SMEM, VMEM],
        out_specs=VMEM,
        compiler_params=room(8),
        name="gravity_adjoint",
    )(head, weights, table)


def last_kernel(total_x, lateral, head, packed, other, observed, table, traces, own, out, held, scalars, sem):
    steps, receivers = traces.shape
    blocks = receivers // 128
    total = packed[...] + other[...]
    residual = total[steps * blocks :, :] - observed[...]
    held[...] = residual.astype(jnp.bfloat16).astype(F32)
    copy = pltpu.make_async_copy(held, scalars, sem)
    copy.start()
    for b in range(blocks):
        traces[:, b * 128 : (b + 1) * 128] = total[b * steps : (b + 1) * steps, :]
    s = lax.axis_index("station")
    mine = own.shape[0]
    for k in range(residual.shape[0] // mine):

        @pl.when(s == k)
        def _(k=k):
            own[...] = residual[k * mine : (k + 1) * mine, :]

    copy.wait()
    spread_back(
        0,
        total_x,
        lateral,
        s * out.shape[1],
        head,
        lambda k, i: scalars[k, i],
        table,
        out,
    )


def gravity_last(steps, receivers, total_x, slab, rows, lateral, head, packed, other, observed, table):
    count = lax.axis_size("station")
    lines = observed.shape[0]
    return pl.pallas_call(
        functools.partial(last_kernel, total_x, lateral),
        out_shape=(
            shape((steps, receivers)),
            shape((lines // count, 128)),
            shape((slab, rows, table.shape[1])),
        ),
        in_specs=[SMEM] + [VMEM] * 4,
        out_specs=(VMEM,) * 3,
        scratch_shapes=[
            pltpu.VMEM((lines, 128), F32),
            pltpu.SMEM((lines, 128), F32),
            pltpu.SemaphoreType.DMA,
        ],
        compiler_params=room(8),
        name="gravity_last",
    )(head, packed, other, observed, on_chip(table))


def cross_kernel(count, velocity, density, outer, inner, out):
    slab, rows, lanes = velocity.shape
    half = slab // 2
    lane = lax.broadcasted_iota(jnp.int32, (rows, lanes), 1)
    row = lax.broadcasted_iota(jnp.int32, (rows, lanes), 0)
    m, flipped = position()
    left_ok = jnp.where(m > 0, 0.5, 0.0)
    right_ok = jnp.where(m < count - 1, 0.5, 0.0)

    def slopes(field, side, x):
        f = field[x]
        if x > 0:
            below = 0.5 * field[x - 1]
        else:
            below = left_ok * jnp.where(flipped, inner[side], outer[side])
        if x < slab - 1:
            above = 0.5 * field[x + 1]
        else:
            above = right_ok * jnp.where(flipped, outer[side], inner[side])
        up = jnp.where(row < rows - 1, pltpu.roll(f, rows - 1, 0), 0.0)
        down = jnp.where(row > 0, pltpu.roll(f, 1, 0), 0.0)
        ahead = jnp.where(lane < lanes - 1, pltpu.roll(f, lanes - 1, 1), 0.0)
        back = jnp.where(lane > 0, pltpu.roll(f, 1, 1), 0.0)
        return above - below, (up - down) * 0.5, (ahead - back) * 0.5

    for x in range(slab):
        v = slopes(velocity, half, x)
        q = slopes(density, half + 1, x)
        out[0, x] = v[1] * q[2] - v[2] * q[1]
        out[1, x] = v[2] * q[0] - v[0] * q[2]
        out[2, x] = v[0] * q[1] - v[1] * q[0]


def cross_gradient_of(count, velocity, density, outer, inner):
    return pl.pallas_call(
        functools.partial(cross_kernel, count),
        out_shape=shape((3,) + velocity.shape),
        in_specs=[VMEM] * 4,
        out_specs=VMEM,
        cost_estimate=pl.CostEstimate(
            flops=60 * velocity.size, bytes_accessed=24 * velocity.size, transcendentals=0
        ),
        compiler_params=room(8),
        name="cross_gradient",
    )(velocity, density, outer, inner)


def per_device(
    p_now, p_prev, velocity, density, wavelet, source_cell, receiver_cells, station_cells, observed
):
    slab, lateral, vertical = p_now.shape
    count = lax.axis_size("mp")
    stations = lax.axis_size("station")
    steps = wavelet.shape[0]
    half = slab // 2
    assert half == REACH and count % 2 == 0 and stations % 4 == 0
    total_x = slab * count
    m, upper = position()
    s = lax.axis_index("station")
    block = lateral // stations
    chain = pairs_of(count, stations, chain_partner(count))
    together = lax.optimization_barrier

    def across(value):
        return lax.ppermute(value, AXES, chain)

    def swap(value, slab_bit, station_bit):
        pairs = pairs_of(count, stations, lambda i, k: (i ^ slab_bit, k ^ station_bit))
        return lax.ppermute(value, AXES, pairs)

    cur, message = first_message(p_now, velocity, density)
    outer = across(message)
    inner = swap(cur, 0, 1)
    edges = outer
    prev, cour, cour_outer, mask, dens, pulses = setup(
        count, source_cell, wavelet, p_prev, velocity, density
    )

    receiver_x, receiver_y = divmod_static(receiver_cells, lateral)
    receiver_j = receiver_x - m * slab
    receiver_j = jnp.where(upper, slab - 1 - receiver_j, receiver_j)
    inside = (receiver_j >= 0) & (receiver_j < half)
    place = jnp.where(inside, receiver_j * lateral + receiver_y, -1)[:, None]

    reach = min(total_x, 64)
    chunks = -(-total_x // reach)
    span = reach + slab - 1
    own_stations = station_cells.shape[0]
    n_stations = own_stations * stations

    def head_of(offset, cells):
        return jnp.concatenate([jnp.reshape(offset, (1,)).astype(jnp.int32), cells])

    def table_of(head):
        return gravity_table(total_x, slab, span, lateral, vertical, head)

    state = {}

    def exchange(bit):
        def work(gate):
            if bit == 1:
                known = jnp.stack([gate(station_cells).astype(F32), observed])[:, None, :]
            else:
                known = gate(state["known"])
            other = swap(known, 0, bit)
            upper = (s // bit) % 2 == 1
            state["known"] = jnp.concatenate(
                [jnp.where(upper, other, known), jnp.where(upper, known, other)], 1
            )

        return work

    def share_edges(gate):
        state["inner"] = swap(gate(edges), 0, 1)

    def cross(gate):
        state["cross"] = cross_gradient_of(count, velocity, density, edges, gate(state["inner"]))
        return "cross"

    def build_table(gate):
        cells = state["known"][0].reshape(-1).astype(jnp.int32)
        state["head"] = head_of(0, cells)
        state["table"] = table_of(gate(jnp.zeros((1,), jnp.int32)))
        return "table"

    pieces = 8
    part = n_stations // pieces

    def forward(i):
        def work(gate):
            state[i] = gravity_forward(
                i * part, part, 0, total_x, slab, lateral, gate(state["head"]), state["table"], dens
            )
            return i

        return work

    def gather_sums(gate):
        sums = jnp.concatenate([state[i] for i in range(pieces)])
        state["predicted"] = jnp.sum(gate(sums), axis=1).reshape(-1, 128)
        return "predicted"

    jobs = [exchange(1 << b) for b in range(stations.bit_length() - 1)]
    jobs.insert(1, share_edges)
    jobs += [cross, None]
    if chunks == 1:
        jobs += [build_table] + [forward(i) for i in range(pieces)] + [gather_sums]

    surf = cour
    for step in range(steps):
        if step:
            outer = across(cur)
            inner = swap(cur, 0, 1)
        base, surf = local_step(step, pulses, mask, cur, prev, cour, surf)
        job = jobs.pop(0) if step and jobs else None
        done = None
        if job is not None:

            def gate(value):
                nonlocal base
                base, value = together((base, value))
                return value

            done = job(gate)
        cur, prev = halo_step(base, cour, cour_outer, outer, inner), cur
        if done is not None:
            cur, state[done] = together((cur, state[done]))
    assert not any(jobs)

    all_observed = state["known"][1].reshape(-1, 128)
    cells = state["known"][0].reshape(-1).astype(jnp.int32)
    if chunks == 1:
        predicted = state["predicted"]
    else:

        def add_chunk(i, total):
            head = head_of(i * reach, cells)
            return total + gravity_forward(
                0, n_stations, reach, total_x, slab, lateral, head, table_of(head[:1]), dens
            )

        sums = lax.fori_loop(0, chunks, add_chunk, jnp.zeros((n_stations, vertical), F32))
        predicted = jnp.sum(sums, axis=1).reshape(-1, 128)

    kept = state["table"] if chunks == 1 else predicted
    sibling = swap(cur, 0, 1)
    packed = recorded_traces(steps - 1, place, cur, surf, predicted)
    other = swap(packed, 0, 1)
    if count & (count - 1) == 0:
        bit = 1
        while bit < count:
            packed = packed + other
            other = swap(packed, bit, 1)
            if bit == 1:
                wavefield = join(cur, sibling, kept)
                other, wavefield = together((other, wavefield))
            bit *= 2
    else:
        wavefield = join(cur, sibling, kept)
        packed = lax.psum(packed + other, "mp")
        other = jnp.zeros_like(packed)

    receivers = receiver_cells.shape[0]
    if chunks == 1:
        traces, own, density_gradient = gravity_last(
            steps,
            receivers,
            total_x,
            slab,
            block,
            lateral,
            state["head"],
            packed,
            other,
            all_observed,
            state["table"],
        )
        gravity_residual = own.reshape(-1)
    else:
        packed = packed + other
        blocks = receivers // 128
        traces = jnp.concatenate(
            [packed[b * steps : (b + 1) * steps] for b in range(blocks)], axis=1
        )
        residual = (packed[steps * blocks :] - all_observed).reshape(-1)
        gravity_residual = lax.dynamic_slice(residual, (s * own_stations,), (own_stations,))
        weights = residual.astype(jnp.bfloat16).astype(F32)

        def back_chunk(i, total):
            head = head_of(i * reach, cells)
            return total + gravity_adjoint(
                reach, total_x, slab, block, lateral, head, weights, table_of(head[:1])
            )

        density_gradient = lax.fori_loop(
            0, chunks, back_chunk, jnp.zeros((slab, block, vertical), F32)
        )
    return (wavefield, traces, gravity_residual, density_gradient, state["cross"])


def solution(mesh):
    in_specs = (
        P("mp", None, None),
        P("mp", None, None),
        P("mp", None, None),
        P("mp", None, None),
        P(),
        P(),
        P(),
        P("station"),
        P("station"),
    )
    out_specs = (
        P("mp", None, None),
        P(),
        P("station"),
        P("mp", "station", None),
        P(None, "mp", None, None),
    )
    return jax.shard_map(
        per_device, mesh=mesh, in_specs=in_specs, out_specs=out_specs, check_vma=False
    )
```

```python
import functools

import jax
import jax.numpy as jnp
from jax import lax
from jax.experimental import pallas as pl
from jax.experimental.pallas import tpu as pltpu
from jax.sharding import PartitionSpec as P

STENCIL = (-205.0 / 72.0, 8.0 / 5.0, -1.0 / 5.0, 8.0 / 315.0, -1.0 / 560.0)
TIME_RATIO = 0.1
REACH = 4
AXES = ("mp", "station")
VMEM = pl.BlockSpec(memory_space=pltpu.VMEM)
SMEM = pl.BlockSpec(memory_space=pltpu.SMEM)
HBM = pl.BlockSpec(memory_space=pltpu.HBM)
F32 = jnp.float32
MIB = 1 << 20


def room(mib):
    return pltpu.CompilerParams(vmem_limit_bytes=mib * MIB)


def shape(dims):
    return jax.ShapeDtypeStruct(dims, F32)


def pairs_of(count, stations, partner):
    return [
        (m * stations + s, (lambda t: t[0] * stations + t[1])(partner(m, s)))
        for m in range(count)
        for s in range(stations)
    ]


def chain_partner(count):
    def partner(m, s):
        if s % 2 == 0:
            return (m ^ 1, s)
        other = m + 1 if m % 2 else m - 1
        if other < 0 or other >= count:
            return (m, s ^ 2)
        return (other, s)

    return partner


def position():
    m = lax.axis_index("mp")
    return m, (m + lax.axis_index("station")) % 2 == 0


def divmod_static(value, divisor):
    if divisor & (divisor - 1) == 0:
        return value >> (divisor.bit_length() - 1), value & (divisor - 1)
    return value // divisor, value % divisor


def in_place(*values):
    return [pltpu.with_memory_space_constraint(value, pltpu.HBM) for value in values]


def run_copies(pairs, sems):
    copies = [pltpu.make_async_copy(a, b, sems.at[i]) for i, (a, b) in enumerate(pairs)]
    for copy in copies:
        copy.start()
    for copy in copies:
        copy.wait()


def plane_of(upper, j, slab):
    return jnp.where(upper, slab - 1 - j, j)


def first_kernel(now, velocity, density, cur, message, sems):
    slab = now.shape[0]
    half = slab // 2
    _, upper = position()
    pairs = []
    for j in range(half):
        plane = plane_of(upper, j, slab)
        pairs += [(now.at[plane], cur.at[j]), (now.at[plane], message.at[j])]
    edge = plane_of(upper, 0, slab)
    pairs += [(velocity.at[edge], message.at[half]), (density.at[edge], message.at[half + 1])]
    run_copies(pairs, sems)


def first_message(p_now, velocity, density):
    slab, rows, lanes = p_now.shape
    half = slab // 2
    return pl.pallas_call(
        first_kernel,
        out_shape=(shape((half, rows, lanes)), shape((half + 2, rows, lanes))),
        in_specs=[HBM] * 3,
        out_specs=(VMEM, VMEM),
        scratch_shapes=[pltpu.SemaphoreType.DMA((2 * half + 2,))],
        compiler_params=room(2),
        name="first_message",
    )(*in_place(p_now, velocity, density))


def setup_kernel(
    count, source, wavelet, p_prev, velocity, density, prev, cour, cour_outer, mask, dens, pulses, vel, raw, sems
):
    slab = p_prev.shape[0]
    half, rows, lanes = prev.shape
    m, upper = position()
    pairs = []
    for j in range(half):
        plane = plane_of(upper, j, slab)
        pairs += [(p_prev.at[plane], prev.at[j]), (velocity.at[plane], vel.at[j])]
    low = half * (lax.axis_index("station") % 2)
    pairs += [(density.at[pl.ds(low, half)], raw)]
    run_copies(pairs, sems)
    for n in range(pulses.shape[0]):
        pulses[n : n + 1, :] = jnp.full((1, lanes), wavelet[n], F32)
    outer_ok = jnp.where(upper, m < count - 1, m > 0)
    outer_ok = jnp.where(outer_ok, 1.0, 0.0)
    column, source_lane = divmod_static(source[0], lanes)
    source_x, source_row = divmod_static(column, rows)
    row = lax.broadcasted_iota(jnp.int32, (rows, lanes), 0)
    lane = lax.broadcasted_iota(jnp.int32, (rows, lanes), 1)
    spot = jnp.where((row == source_row) & (lane == source_lane), 1.0, 0.0)
    for j in range(half):
        scaled = TIME_RATIO * vel[j]
        square = scaled * scaled
        cour[j] = square
        cour_outer[j] = square * outer_ok
        here = m * slab + plane_of(upper, j, slab) == source_x
        mask[j] = spot * jnp.where(here, 1.0, 0.0)
        dens[j] = raw[j].astype(jnp.bfloat16).astype(F32)


def setup(count, source_cell, wavelet, p_prev, velocity, density):
    slab, rows, lanes = p_prev.shape
    half = slab // 2
    part = shape((half, rows, lanes))
    held = pltpu.VMEM((half, rows, lanes), F32)
    return pl.pallas_call(
        functools.partial(setup_kernel, count),
        out_shape=(part,) * 5 + (shape((wavelet.shape[0], lanes)),),
        in_specs=[SMEM, SMEM] + [HBM] * 3,
        out_specs=(VMEM,) * 6,
        scratch_shapes=[held, held, pltpu.SemaphoreType.DMA((2 * half + 1,))],
        compiler_params=room(4),
        cost_estimate=pl.CostEstimate(
            flops=20 * half * rows * lanes, bytes_accessed=32 * half * rows * lanes, transcendentals=0
        ),
        name="setup",
    )(source_cell, wavelet, *in_place(p_prev, velocity, density))


def local_kernel(step, pulses, mask, cur, prev, cour, surf_in, base, surf, pad):
    planes, rows, lanes = prev.shape
    lane = lax.broadcasted_iota(jnp.int32, (rows, lanes), 1)
    weights = {}
    for d in range(1, REACH + 1):
        weights[d] = jnp.where(lane >= d, STENCIL[d], 0.0)
        weights[-d] = jnp.where(lane < lanes - d, STENCIL[d], 0.0)
    pulse = pulses[step : step + 1, :]
    for j in range(planes):
        pad[j, 0:8, :] = jnp.zeros((8, lanes), F32)
        pad[j, 8 + rows : 16 + rows, :] = jnp.zeros((8, lanes), F32)
        pad[j, 8 : 8 + rows, :] = cur[j]
    for j in range(planes):
        c = cur[j]
        acc = 3.0 * STENCIL[0] * c
        for d in range(1, REACH + 1):
            acc = acc + weights[d] * pltpu.roll(c, d, 1) + weights[-d] * pltpu.roll(c, lanes - d, 1)
            near = pad[j, 8 + d : 8 + d + rows, :] + pad[j, 8 - d : 8 - d + rows, :]
            for i in (j - d, j + d):
                if 0 <= i < planes:
                    near = near + cur[i]
            acc = acc + STENCIL[d] * near
        base[j] = 2.0 * c - prev[j] + cour[j] * acc + pulse * mask[j]
        if step == 0:
            surf[j] = jnp.zeros((rows, lanes), F32)
        else:
            surf[j] = jnp.where(
                lane == step - 1, jnp.broadcast_to(c[:, 0:1], (rows, lanes)), surf_in[j]
            )


def local_step(step, pulses, mask, cur, prev, cour, surf):
    planes, rows, lanes = cur.shape
    return pl.pallas_call(
        functools.partial(local_kernel, step),
        out_shape=(shape(cur.shape), shape(cur.shape)),
        in_specs=[VMEM] * 6,
        out_specs=(VMEM, VMEM),
        scratch_shapes=[pltpu.VMEM((planes, rows + 16, lanes), F32)],
        compiler_params=room(2),
        cost_estimate=pl.CostEstimate(
            flops=60 * cur.size, bytes_accessed=24 * cur.size, transcendentals=0
        ),
        name="wave_local",
    )(pulses, mask, cur, prev, cour, surf)


def halo_kernel(base, cour, cour_outer, outer, inner, out):
    planes = base.shape[0]
    for j in range(planes):
        far = near = None
        for d in range(j + 1, REACH + 1):
            term = STENCIL[d] * outer[d - j - 1]
            far = term if far is None else far + term
        for d in range(planes - j, REACH + 1):
            term = STENCIL[d] * inner[2 * planes - 1 - j - d]
            near = term if near is None else near + term
        out[j] = base[j] + (cour[j] * near + cour_outer[j] * far)


def halo_step(base, cour, cour_outer, outer, inner):
    return pl.pallas_call(
        halo_kernel,
        out_shape=shape(base.shape),
        in_specs=[VMEM] * 5,
        out_specs=VMEM,
        compiler_params=room(2),
        cost_estimate=pl.CostEstimate(
            flops=12 * base.size, bytes_accessed=20 * base.size, transcendentals=0
        ),
        name="wave_halo",
    )(base, cour, cour_outer, outer, inner)


def trace_kernel(step, place, cur, surf, out):
    planes, rows, lanes = cur.shape
    receivers = place.shape[1]
    steps = step + 1
    lane = lax.broadcasted_iota(jnp.int32, (rows, lanes), 1)
    columns = jnp.concatenate(
        [
            jnp.where(lane == step, jnp.broadcast_to(cur[j, :, 0:1], (rows, lanes)), surf[j])
            for j in range(planes)
        ],
        0,
    )
    columns = columns.T
    spot = lax.broadcasted_iota(jnp.int32, (planes * rows, receivers), 0)
    pick = jnp.where(place[...] == spot, 1.0, 0.0).astype(jnp.bfloat16)
    total = None
    for _ in range(3):
        part = columns.astype(jnp.bfloat16)
        columns = columns - part.astype(F32)
        term = jnp.dot(part, pick, preferred_element_type=F32)
        total = term if total is None else total + term
    for b in range(receivers // 128):
        out[b * steps : (b + 1) * steps, :] = total[:steps, b * 128 : (b + 1) * 128]


def recorded_traces(step, place, cur, surf):
    return pl.pallas_call(
        functools.partial(trace_kernel, step),
        out_shape=shape(((step + 1) * (place.shape[1] // 128), 128)),
        in_specs=[VMEM] * 3,
        out_specs=VMEM,
        compiler_params=room(4),
        name="traces",
    )(place, cur, surf)


def join_kernel(own, sibling, out, sems):
    slab = out.shape[0]
    _, upper = position()
    pairs = []
    for j in range(slab // 2):
        here = plane_of(upper, j, slab)
        pairs += [(own.at[j], out.at[here]), (sibling.at[j], out.at[slab - 1 - here])]
    run_copies(pairs, sems)


def join(own, sibling):
    half, rows, lanes = own.shape
    return pl.pallas_call(
        join_kernel,
        out_shape=shape((2 * half, rows, lanes)),
        in_specs=[VMEM] * 2,
        out_specs=HBM,
        scratch_shapes=[pltpu.SemaphoreType.DMA((2 * half,))],
        compiler_params=room(2),
        name="join",
    )(own, sibling)


def on_chip(value):
    return pltpu.with_memory_space_constraint(value, pltpu.VMEM)


def table_low(total_x, slab, offset):
    m, _ = position()
    return m * slab - (total_x - 1) + offset


def table_kernel(total_x, slab, spread, head, out):
    lanes = out.shape[1]
    low = table_low(total_x, slab, head[0])
    dy = (lax.broadcasted_iota(jnp.int32, (spread, lanes), 0) - (spread // 2 - 1)).astype(F32)
    dz = (lax.broadcasted_iota(jnp.int32, (spread, lanes), 1) + 1).astype(F32)
    side = dy * dy
    deep = dz * dz

    def one(t, carry):
        dx = (t + low).astype(F32)
        square = dx * dx + side + deep
        value = dz / (square * jnp.sqrt(square))
        start = pl.multiple_of(t * spread, spread)
        out[pl.ds(start, spread), :] = value.astype(jnp.bfloat16).astype(F32)
        return carry

    lax.fori_loop(0, out.shape[0] // spread, one, 0)


def gravity_table(total_x, slab, depth, lateral, vertical, head):
    size = depth * 2 * lateral * vertical
    return pl.pallas_call(
        functools.partial(table_kernel, total_x, slab, 2 * lateral),
        out_shape=shape((depth * 2 * lateral, vertical)),
        in_specs=[SMEM],
        out_specs=VMEM,
        cost_estimate=pl.CostEstimate(
            flops=20 * size, bytes_accessed=4 * size, transcendentals=2 * size
        ),
        compiler_params=room(8),
        name="gravity_table",
    )(head)


def forward_kernel(first, guard, total_x, slab, lateral, head, table, dens, out):
    planes, rows, lanes = dens.shape
    count = out.shape[0]
    spread = 2 * lateral
    core = lax.axis_index("station") % 2
    lead = total_x - 1 - head[0]
    if guard:
        out[...] = jnp.zeros_like(out)

    def one(s, carry):
        sx, sy = divmod_static(head[1 + first + s], lateral)
        shift = lead - sx
        start = (shift + core * planes) * spread + (lateral - 1 - sy)

        def accumulate():
            acc = None
            for p in range(planes):
                term = table[pl.ds(start + p * spread, rows), :] * dens[p]
                acc = term if acc is None else acc + term
            out[pl.ds(s, 1), :] = jnp.sum(acc, axis=0, keepdims=True)

        if guard:
            pl.when((shift >= 0) & (shift < guard))(accumulate)
        else:
            accumulate()
        return carry

    lax.fori_loop(0, count, one, 0, unroll=8)


def gravity_forward(first, count, guard, total_x, slab, lateral, head, table, dens):
    work = count * dens.size
    return pl.pallas_call(
        functools.partial(forward_kernel, first, guard, total_x, slab, lateral),
        out_shape=shape((count, dens.shape[2])),
        in_specs=[SMEM, VMEM, VMEM],
        out_specs=VMEM,
        cost_estimate=pl.CostEstimate(
            flops=4 * work, bytes_accessed=4 * dens.size, transcendentals=0
        ),
        compiler_params=room(8),
        name="gravity_forward",
    )(head, on_chip(table), dens)


def adjoint_kernel(lines, guard, total_x, lateral, head, weights, table, start_at, out):
    slab, rows, lanes = out.shape
    spread = 2 * lateral
    lead = total_x - 1 - head[0]
    row_low = lax.axis_index("station") * rows

    def one(k, i, acc):
        sx, sy = divmod_static(head[1 + 128 * k + i], lateral)
        shift = lead - sx
        weight = weights[k, i]
        if guard:
            keep = (shift >= 0) & (shift < guard)
            shift = jnp.where(keep, shift, 0)
            weight = jnp.where(keep, weight, 0.0)
        start = shift * spread + (lateral - 1 - sy + row_low)
        return tuple(
            acc[x] + weight * table[pl.ds(start + x * spread, rows), :] for x in range(slab)
        )

    acc = tuple(start_at[x] for x in range(slab))
    for k in lines:
        acc = lax.fori_loop(0, 128, functools.partial(one, k), acc, unroll=8)
    for x in range(slab):
        out[x] = acc[x]


def gravity_adjoint(lines, guard, total_x, lateral, head, weights, table, start_at):
    return pl.pallas_call(
        functools.partial(adjoint_kernel, lines, guard, total_x, lateral),
        out_shape=shape(start_at.shape),
        in_specs=[SMEM, SMEM, VMEM, VMEM],
        out_specs=VMEM,
        cost_estimate=pl.CostEstimate(
            flops=256 * len(lines) * start_at.size, bytes_accessed=8 * start_at.size, transcendentals=0
        ),
        compiler_params=room(8),
        name="gravity_adjoint",
    )(head, weights, table, start_at)


def small_call(kernel, outs, name, *values):
    single = not isinstance(outs, tuple)
    return pl.pallas_call(
        kernel,
        out_shape=outs,
        in_specs=[VMEM] * len(values),
        out_specs=VMEM if single else (VMEM,) * len(outs),
        compiler_params=room(2),
        name=name,
    )(*values)


def sum_kernel(first, second, out):
    out[...] = first[...] + second[...]


def plus(first, second):
    return small_call(sum_kernel, shape(first.shape), "sum", first, second)


def unpack_kernel(packed, other, out):
    steps, receivers = out.shape
    for b in range(receivers // 128):
        rows = slice(b * steps, (b + 1) * steps)
        out[:, b * 128 : (b + 1) * 128] = packed[rows, :] + other[rows, :]


def predict_kernel(*refs):
    pieces, out = refs[:-1], refs[-1]
    line = 0
    for piece in pieces:
        for k in range(piece.shape[0] // 128):
            block = piece[k * 128 : (k + 1) * 128, :].T
            out[line : line + 1, :] = jnp.sum(block, axis=0, keepdims=True)
            line += 1


def residual_kernel(packed, other, observed, weights, own):
    residual = packed[...] + other[...] - observed[...]
    weights[...] = residual.astype(jnp.bfloat16).astype(F32)
    mine = own.shape[0]
    for k in range(residual.shape[0] // mine):

        @pl.when(lax.axis_index("station") == k)
        def _(k=k):
            own[...] = residual[k * mine : (k + 1) * mine, :]


def cross_kernel(count, velocity, density, outer, inner, out):
    slab, rows, lanes = velocity.shape
    half = slab // 2
    lane = lax.broadcasted_iota(jnp.int32, (rows, lanes), 1)
    row = lax.broadcasted_iota(jnp.int32, (rows, lanes), 0)
    m, flipped = position()
    left_ok = jnp.where(m > 0, 0.5, 0.0)
    right_ok = jnp.where(m < count - 1, 0.5, 0.0)

    def slopes(field, side, x):
        f = field[x]
        if x > 0:
            below = 0.5 * field[x - 1]
        else:
            below = left_ok * jnp.where(flipped, inner[side], outer[side])
        if x < slab - 1:
            above = 0.5 * field[x + 1]
        else:
            above = right_ok * jnp.where(flipped, outer[side], inner[side])
        up = jnp.where(row < rows - 1, pltpu.roll(f, rows - 1, 0), 0.0)
        down = jnp.where(row > 0, pltpu.roll(f, 1, 0), 0.0)
        ahead = jnp.where(lane < lanes - 1, pltpu.roll(f, lanes - 1, 1), 0.0)
        back = jnp.where(lane > 0, pltpu.roll(f, 1, 1), 0.0)
        return above - below, (up - down) * 0.5, (ahead - back) * 0.5

    for x in range(slab):
        v = slopes(velocity, half, x)
        q = slopes(density, half + 1, x)
        out[0, x] = v[1] * q[2] - v[2] * q[1]
        out[1, x] = v[2] * q[0] - v[0] * q[2]
        out[2, x] = v[0] * q[1] - v[1] * q[0]


def cross_gradient_of(count, velocity, density, outer, inner):
    return pl.pallas_call(
        functools.partial(cross_kernel, count),
        out_shape=shape((3,) + velocity.shape),
        in_specs=[VMEM] * 4,
        out_specs=VMEM,
        cost_estimate=pl.CostEstimate(
            flops=60 * velocity.size, bytes_accessed=24 * velocity.size, transcendentals=0
        ),
        compiler_params=room(8),
        name="cross_gradient",
    )(velocity, density, outer, inner)


def per_device(
    p_now, p_prev, velocity, density, wavelet, source_cell, receiver_cells, station_cells, observed
):
    slab, lateral, vertical = p_now.shape
    count = lax.axis_size("mp")
    stations = lax.axis_size("station")
    steps = wavelet.shape[0]
    half = slab // 2
    assert half == REACH and count % 2 == 0 and stations % 4 == 0
    total_x = slab * count
    m, upper = position()
    s = lax.axis_index("station")
    block = lateral // stations
    chain = pairs_of(count, stations, chain_partner(count))
    together = lax.optimization_barrier

    def across(value):
        return lax.ppermute(value, AXES, chain)

    def swap(value, slab_bit, station_bit):
        pairs = pairs_of(count, stations, lambda i, k: (i ^ slab_bit, k ^ station_bit))
        return lax.ppermute(value, AXES, pairs)

    cur, message = first_message(p_now, velocity, density)
    outer = across(message)
    inner = swap(cur, 0, 1)
    edges = outer
    prev, cour, cour_outer, mask, dens, pulses = setup(
        count, source_cell, wavelet, p_prev, velocity, density
    )

    receiver_x, receiver_y = divmod_static(receiver_cells, lateral)
    receiver_j = receiver_x - m * slab
    receiver_j = jnp.where(upper, slab - 1 - receiver_j, receiver_j)
    inside = (receiver_j >= 0) & (receiver_j < half)
    place = jnp.where(inside, receiver_j * lateral + receiver_y, -1)[None, :]

    reach = min(total_x, 64)
    chunks = -(-total_x // reach)
    span = reach + slab - 1
    own_stations = station_cells.shape[0]
    n_stations = own_stations * stations

    def head_of(offset, cells):
        return jnp.concatenate([jnp.reshape(offset, (1,)).astype(jnp.int32), cells])

    def table_of(head):
        return gravity_table(total_x, slab, span, lateral, vertical, head)

    state = {}

    def exchange(bit):
        def work(gate):
            if bit == 1:
                known = jnp.stack([gate(station_cells).astype(F32), observed])[:, None, :]
            else:
                known = gate(state["known"])
            other = swap(known, 0, bit)
            upper = (s // bit) % 2 == 1
            state["known"] = jnp.concatenate(
                [jnp.where(upper, other, known), jnp.where(upper, known, other)], 1
            )

        return work

    def share_edges(gate):
        state["inner"] = swap(gate(edges), 0, 1)

    def cross(gate):
        state["cross"] = cross_gradient_of(count, velocity, density, edges, gate(state["inner"]))
        return "cross"

    lines = n_stations // 128

    def build_table(gate):
        known = gate(state["known"])
        cells = known[0].reshape(-1).astype(jnp.int32)
        head = head_of(0, cells)
        zero, head, observed_all, where = together(
            (jnp.zeros((1,), jnp.int32), head, known[1].reshape(-1, 128), place)
        )
        state.update(head=head, observed=observed_all, place=where)
        state["table"] = table_of(zero)
        return "table"

    pieces = 4
    part = n_stations // pieces

    def forward(i):
        def work(gate):
            state[i] = gravity_forward(
                i * part, part, 0, total_x, slab, lateral, gate(state["head"]), state["table"], dens
            )
            return i

        return work

    def predict(gate):
        sums = [state[i] for i in range(pieces)]
        sums[0] = gate(sums[0])
        packed = small_call(predict_kernel, shape((lines, 128)), "predict", *sums)
        state["packed"], state["other"] = packed, swap(packed, 0, 1)

    def add_up(bit):
        def work(gate):
            packed = plus(gate(state["packed"]), state["other"])
            state["packed"], state["other"] = packed, swap(packed, bit, 1)

        return work

    def residual(gate):
        state["weights"], state["own"] = small_call(
            residual_kernel,
            (shape((lines, 128)), shape((lines // stations, 128))),
            "residual",
            gate(state["packed"]),
            state["other"],
            state["observed"],
        )
        state["gradient"] = jnp.zeros((slab, block, vertical), F32)
        return "weights"

    def adjoint(half_lines):
        def work(gate):
            state["gradient"] = gravity_adjoint(
                half_lines,
                0,
                total_x,
                lateral,
                state["head"],
                gate(state["weights"]),
                state["table"],
                state["gradient"],
            )
            return "gradient"

        return work

    hidden = chunks == 1 and count & (count - 1) == 0
    jobs = [exchange(1 << b) for b in range(stations.bit_length() - 1)]
    if hidden:
        jobs += [build_table] + [forward(i) for i in range(pieces)] + [predict]
        jobs += [add_up(1 << b) for b in range(count.bit_length() - 1)] + [residual]
        jobs += [adjoint(range(lines // 2)), adjoint(range(lines // 2, lines))]
    jobs.insert(1, share_edges)
    jobs.append(cross)

    surf = cour
    for step in range(steps):
        if step:
            outer = across(cur)
            inner = swap(cur, 0, 1)
        base, surf = local_step(step, pulses, mask, cur, prev, cour, surf)

        def gate(value):
            nonlocal base
            base, value = together((base, value))
            return value

        ready = jobs.pop(0)(gate) if step and jobs else None
        if step == steps - 1:
            while jobs:
                ready = jobs.pop(0)(gate)
        cur, prev = halo_step(base, cour, cour_outer, outer, inner), cur
        if ready is not None:
            cur, state[ready] = together((cur, state[ready]))

    sibling = swap(cur, 0, 1)
    packed = recorded_traces(steps - 1, state.get("place", place), cur, surf)
    other = swap(packed, 0, 1)
    if count & (count - 1) == 0:
        bit = 1
        while bit < count:
            packed = plus(packed, other)
            other = swap(packed, bit, 1)
            if bit == 1:
                wavefield = join(cur, sibling)
                other, wavefield = together((other, wavefield))
            bit *= 2
    else:
        wavefield = join(cur, sibling)
        packed = lax.psum(packed + other, "mp")
        other = jnp.zeros_like(packed)
    traces = small_call(
        unpack_kernel, shape((steps, receiver_cells.shape[0])), "unpack", packed, other
    )
    if hidden:
        gravity_residual = state["own"].reshape(-1)
        density_gradient = state["gradient"]
    else:
        cells = state["known"][0].reshape(-1).astype(jnp.int32)

        def add_chunk(i, total):
            head = head_of(i * reach, cells)
            return total + gravity_forward(
                0, n_stations, reach, total_x, slab, lateral, head, table_of(head[:1]), dens
            )

        sums = lax.fori_loop(0, chunks, add_chunk, jnp.zeros((n_stations, vertical), F32))
        predicted = jnp.sum(sums, axis=1)
        predicted = lax.psum(predicted + swap(predicted, 0, 1), "mp")
        difference = predicted - state["known"][1].reshape(-1)
        gravity_residual = lax.dynamic_slice(difference, (s * own_stations,), (own_stations,))
        weights = difference.astype(jnp.bfloat16).astype(F32).reshape(-1, 128)

        def back_chunk(i, total):
            head = head_of(i * reach, cells)
            return gravity_adjoint(
                range(lines), reach, total_x, lateral, head, weights, table_of(head[:1]), total
            )

        density_gradient = lax.fori_loop(
            0, chunks, back_chunk, jnp.zeros((slab, block, vertical), F32)
        )
    return (wavefield, traces, gravity_residual, density_gradient, state["cross"])


def solution(mesh):
    in_specs = (
        P("mp", None, None),
        P("mp", None, None),
        P("mp", None, None),
        P("mp", None, None),
        P(),
        P(),
        P(),
        P("station"),
        P("station"),
    )
    out_specs = (
        P("mp", None, None),
        P(),
        P("station"),
        P("mp", "station", None),
        P(None, "mp", None, None),
    )
    return jax.shard_map(
        per_device, mesh=mesh, in_specs=in_specs, out_specs=out_specs, check_vma=False
    )
```

```python
import functools

import jax
import jax.numpy as jnp
from jax import lax
from jax.experimental import pallas as pl
from jax.experimental.pallas import tpu as pltpu
from jax.sharding import PartitionSpec as P


STENCIL = (-205.0 / 72.0, 8.0 / 5.0, -1.0 / 5.0, 8.0 / 315.0, -1.0 / 560.0)
TIME_RATIO = 0.1
REACH = 4
AXES = ("mp", "station")
VMEM = pl.BlockSpec(memory_space=pltpu.VMEM)
SMEM = pl.BlockSpec(memory_space=pltpu.SMEM)
HBM = pl.BlockSpec(memory_space=pltpu.HBM)
F32 = jnp.float32
MIB = 1 << 20


def room(mib):
    return pltpu.CompilerParams(vmem_limit_bytes=mib * MIB)


def shape(dims):
    return jax.ShapeDtypeStruct(dims, F32)


def pairs_of(count, stations, partner):
    return [
        (m * stations + s, (lambda t: t[0] * stations + t[1])(partner(m, s)))
        for m in range(count)
        for s in range(stations)
    ]


def chain_partner(count):
    def partner(m, s):
        if s % 2 == 0:
            return (m ^ 1, s)
        other = m + 1 if m % 2 else m - 1
        if other < 0 or other >= count:
            return (m, s ^ 2)
        return (other, s)

    return partner


def position():
    m = lax.axis_index("mp")
    return m, (m + lax.axis_index("station")) % 2 == 0


def divmod_static(value, divisor):
    if divisor & (divisor - 1) == 0:
        return value >> (divisor.bit_length() - 1), value & (divisor - 1)
    return value // divisor, value % divisor


def in_place(*values):
    return [pltpu.with_memory_space_constraint(value, pltpu.HBM) for value in values]


def run_copies(pairs, sems):
    copies = [pltpu.make_async_copy(a, b, sems.at[i]) for i, (a, b) in enumerate(pairs)]
    for copy in copies:
        copy.start()
    for copy in copies:
        copy.wait()


def plane_of(upper, j, slab):
    return jnp.where(upper, slab - 1 - j, j)


def first_kernel(now, velocity, density, cur, message, sems):
    slab = now.shape[0]
    half = slab // 2
    _, upper = position()
    pairs = []
    for j in range(half):
        plane = plane_of(upper, j, slab)
        pairs += [(now.at[plane], cur.at[j]), (now.at[plane], message.at[j])]
    edge = plane_of(upper, 0, slab)
    pairs += [(velocity.at[edge], message.at[half]), (density.at[edge], message.at[half + 1])]
    run_copies(pairs, sems)


def first_message(p_now, velocity, density):
    slab, rows, lanes = p_now.shape
    half = slab // 2
    return pl.pallas_call(
        first_kernel,
        out_shape=(shape((half, rows, lanes)), shape((half + 2, rows, lanes))),
        in_specs=[HBM] * 3,
        out_specs=(VMEM, VMEM),
        scratch_shapes=[pltpu.SemaphoreType.DMA((2 * half + 2,))],
        compiler_params=room(2),
        name="first_message",
    )(*in_place(p_now, velocity, density))


def setup_kernel(
    count, source, wavelet, p_prev, velocity, density, prev, cour, cour_outer, mask, dens, pulses, vel, raw, sems
):
    slab = p_prev.shape[0]
    half, rows, lanes = prev.shape
    m, upper = position()
    pairs = []
    for j in range(half):
        plane = plane_of(upper, j, slab)
        pairs += [(p_prev.at[plane], prev.at[j]), (velocity.at[plane], vel.at[j])]
    low = half * (lax.axis_index("station") % 2)
    pairs += [(density.at[pl.ds(low, half)], raw)]
    run_copies(pairs, sems)
    for n in range(pulses.shape[0]):
        pulses[n : n + 1, :] = jnp.full((1, lanes), wavelet[n], F32)
    outer_ok = jnp.where(upper, m < count - 1, m > 0)
    outer_ok = jnp.where(outer_ok, 1.0, 0.0)
    column, source_lane = divmod_static(source[0], lanes)
    source_x, source_row = divmod_static(column, rows)
    row = lax.broadcasted_iota(jnp.int32, (rows, lanes), 0)
    lane = lax.broadcasted_iota(jnp.int32, (rows, lanes), 1)
    spot = jnp.where((row == source_row) & (lane == source_lane), 1.0, 0.0)
    for j in range(half):
        scaled = TIME_RATIO * vel[j]
        square = scaled * scaled
        cour[j] = square
        cour_outer[j] = square * outer_ok
        here = m * slab + plane_of(upper, j, slab) == source_x
        mask[j] = spot * jnp.where(here, 1.0, 0.0)
        dens[j] = raw[j].astype(jnp.bfloat16).astype(F32)


def setup(count, source_cell, wavelet, p_prev, velocity, density):
    slab, rows, lanes = p_prev.shape
    half = slab // 2
    part = shape((half, rows, lanes))
    held = pltpu.VMEM((half, rows, lanes), F32)
    return pl.pallas_call(
        functools.partial(setup_kernel, count),
        out_shape=(part,) * 5 + (shape((wavelet.shape[0], lanes)),),
        in_specs=[SMEM, SMEM] + [HBM] * 3,
        out_specs=(VMEM,) * 6,
        scratch_shapes=[held, held, pltpu.SemaphoreType.DMA((2 * half + 1,))],
        compiler_params=room(4),
        cost_estimate=pl.CostEstimate(
            flops=20 * half * rows * lanes, bytes_accessed=32 * half * rows * lanes, transcendentals=0
        ),
        name="setup",
    )(source_cell, wavelet, *in_place(p_prev, velocity, density))


def local_kernel(step, pulses, mask, cur, prev, cour, surf_in, base, surf, pad):
    planes, rows, lanes = prev.shape
    lane = lax.broadcasted_iota(jnp.int32, (rows, lanes), 1)
    weights = {}
    for d in range(1, REACH + 1):
        weights[d] = jnp.where(lane >= d, STENCIL[d], 0.0)
        weights[-d] = jnp.where(lane < lanes - d, STENCIL[d], 0.0)
    pulse = pulses[step : step + 1, :]
    for j in range(planes):
        pad[j, 0:8, :] = jnp.zeros((8, lanes), F32)
        pad[j, 8 + rows : 16 + rows, :] = jnp.zeros((8, lanes), F32)
        pad[j, 8 : 8 + rows, :] = cur[j]
    for j in range(planes):
        c = cur[j]
        acc = 3.0 * STENCIL[0] * c
        for d in range(1, REACH + 1):
            acc = acc + weights[d] * pltpu.roll(c, d, 1) + weights[-d] * pltpu.roll(c, lanes - d, 1)
            near = pad[j, 8 + d : 8 + d + rows, :] + pad[j, 8 - d : 8 - d + rows, :]
            for i in (j - d, j + d):
                if 0 <= i < planes:
                    near = near + cur[i]
            acc = acc + STENCIL[d] * near
        base[j] = 2.0 * c - prev[j] + cour[j] * acc + pulse * mask[j]
        if step == 0:
            surf[j] = jnp.zeros((rows, lanes), F32)
        else:
            surf[j] = jnp.where(
                lane == step - 1, jnp.broadcast_to(c[:, 0:1], (rows, lanes)), surf_in[j]
            )


def local_step(step, pulses, mask, cur, prev, cour, surf):
    planes, rows, lanes = cur.shape
    return pl.pallas_call(
        functools.partial(local_kernel, step),
        out_shape=(shape(cur.shape), shape(cur.shape)),
        in_specs=[VMEM] * 6,
        out_specs=(VMEM, VMEM),
        scratch_shapes=[pltpu.VMEM((planes, rows + 16, lanes), F32)],
        compiler_params=room(2),
        cost_estimate=pl.CostEstimate(
            flops=60 * cur.size, bytes_accessed=24 * cur.size, transcendentals=0
        ),
        name="wave_local",
    )(pulses, mask, cur, prev, cour, surf)


def halo_kernel(base, cour, cour_outer, outer, inner, out):
    planes = base.shape[0]
    for j in range(planes):
        far = near = None
        for d in range(j + 1, REACH + 1):
            term = STENCIL[d] * outer[d - j - 1]
            far = term if far is None else far + term
        for d in range(planes - j, REACH + 1):
            term = STENCIL[d] * inner[2 * planes - 1 - j - d]
            near = term if near is None else near + term
        out[j] = base[j] + (cour[j] * near + cour_outer[j] * far)


def halo_step(base, cour, cour_outer, outer, inner):
    return pl.pallas_call(
        halo_kernel,
        out_shape=shape(base.shape),
        in_specs=[VMEM] * 5,
        out_specs=VMEM,
        compiler_params=room(2),
        cost_estimate=pl.CostEstimate(
            flops=12 * base.size, bytes_accessed=20 * base.size, transcendentals=0
        ),
        name="wave_halo",
    )(base, cour, cour_outer, outer, inner)


def trace_kernel(step, place, cur, surf, out):
    planes, rows, lanes = cur.shape
    receivers = place.shape[1]
    steps = step + 1
    lane = lax.broadcasted_iota(jnp.int32, (rows, lanes), 1)
    columns = jnp.concatenate(
        [
            jnp.where(lane == step, jnp.broadcast_to(cur[j, :, 0:1], (rows, lanes)), surf[j])
            for j in range(planes)
        ],
        0,
    )
    columns = columns.T
    spot = lax.broadcasted_iota(jnp.int32, (planes * rows, receivers), 0)
    pick = jnp.where(place[...] == spot, 1.0, 0.0).astype(jnp.bfloat16)
    total = None
    for _ in range(3):
        part = columns.astype(jnp.bfloat16)
        columns = columns - part.astype(F32)
        term = jnp.dot(part, pick, preferred_element_type=F32)
        total = term if total is None else total + term
    for b in range(receivers // 128):
        out[b * steps : (b + 1) * steps, :] = total[:steps, b * 128 : (b + 1) * 128]


def recorded_traces(step, place, cur, surf):
    return pl.pallas_call(
        functools.partial(trace_kernel, step),
        out_shape=shape(((step + 1) * (place.shape[1] // 128), 128)),
        in_specs=[VMEM] * 3,
        out_specs=VMEM,
        compiler_params=room(4),
        name="traces",
    )(place, cur, surf)


def join_kernel(own, sibling, out, sems):
    slab = out.shape[0]
    _, upper = position()
    pairs = []
    for j in range(slab // 2):
        here = plane_of(upper, j, slab)
        pairs += [(own.at[j], out.at[here]), (sibling.at[j], out.at[slab - 1 - here])]
    run_copies(pairs, sems)


def join(own, sibling):
    half, rows, lanes = own.shape
    return pl.pallas_call(
        join_kernel,
        out_shape=shape((2 * half, rows, lanes)),
        in_specs=[VMEM] * 2,
        out_specs=HBM,
        scratch_shapes=[pltpu.SemaphoreType.DMA((2 * half,))],
        compiler_params=room(2),
        name="join",
    )(own, sibling)


def on_chip(value):
    return pltpu.with_memory_space_constraint(value, pltpu.VMEM)


def table_low(total_x, slab, offset):
    m, _ = position()
    return m * slab - (total_x - 1) + offset


def table_kernel(total_x, slab, spread, head, out):
    lanes = out.shape[1]
    low = table_low(total_x, slab, head[0])
    dy = (lax.broadcasted_iota(jnp.int32, (spread, lanes), 0) - (spread // 2 - 1)).astype(F32)
    dz = (lax.broadcasted_iota(jnp.int32, (spread, lanes), 1) + 1).astype(F32)
    side = dy * dy
    deep = dz * dz

    def one(t, carry):
        dx = (t + low).astype(F32)
        square = dx * dx + side + deep
        value = dz / (square * jnp.sqrt(square))
        start = pl.multiple_of(t * spread, spread)
        out[pl.ds(start, spread), :] = value.astype(jnp.bfloat16).astype(F32)
        return carry

    lax.fori_loop(0, out.shape[0] // spread, one, 0)


def gravity_table(total_x, slab, depth, lateral, vertical, head):
    size = depth * 2 * lateral * vertical
    return pl.pallas_call(
        functools.partial(table_kernel, total_x, slab, 2 * lateral),
        out_shape=shape((depth * 2 * lateral, vertical)),
        in_specs=[SMEM],
        out_specs=VMEM,
        cost_estimate=pl.CostEstimate(
            flops=20 * size, bytes_accessed=4 * size, transcendentals=2 * size
        ),
        compiler_params=room(8),
        name="gravity_table",
    )(head)


def forward_kernel(first, guard, total_x, lateral, head, table, dens, out):
    planes, rows, _ = dens.shape
    count = out.shape[0]
    spread = 2 * lateral
    core = lax.axis_index("station") % 2
    lead = total_x - 1 - head[0]
    if guard:
        out[...] = jnp.zeros_like(out)

    def one(s, carry):
        sx, sy = divmod_static(head[1 + first + s], lateral)
        shift = lead - sx
        start = (shift + core * planes) * spread + (lateral - 1 - sy)

        def accumulate():
            acc = None
            for p in range(planes):
                term = table[pl.ds(start + p * spread, rows), :] * dens[p]
                acc = term if acc is None else acc + term
            out[pl.ds(s, 1), :] = jnp.sum(acc, axis=0, keepdims=True)

        if guard:
            pl.when((shift >= 0) & (shift < guard))(accumulate)
        else:
            accumulate()
        return carry

    lax.fori_loop(0, count, one, 0, unroll=8)


def gravity_forward(first, count, guard, total_x, lateral, head, table, dens):
    work = count * dens.size
    return pl.pallas_call(
        functools.partial(forward_kernel, first, guard, total_x, lateral),
        out_shape=shape((count, dens.shape[2])),
        in_specs=[SMEM, VMEM, VMEM],
        out_specs=VMEM,
        cost_estimate=pl.CostEstimate(
            flops=4 * work, bytes_accessed=4 * dens.size, transcendentals=0
        ),
        compiler_params=room(8),
        name="gravity_forward",
    )(head, on_chip(table), dens)


def adjoint_kernel(lines, guard, total_x, lateral, head, weights, table, start_at, out):
    slab, rows, _ = out.shape
    spread = 2 * lateral
    lead = total_x - 1 - head[0]
    row_low = lax.axis_index("station") * rows

    def one(k, i, acc):
        sx, sy = divmod_static(head[1 + 128 * k + i], lateral)
        shift = lead - sx
        weight = weights[k, i]
        if guard:
            keep = (shift >= 0) & (shift < guard)
            shift = jnp.where(keep, shift, 0)
            weight = jnp.where(keep, weight, 0.0)
        start = shift * spread + (lateral - 1 - sy + row_low)
        return tuple(
            acc[x] + weight * table[pl.ds(start + x * spread, rows), :] for x in range(slab)
        )

    acc = tuple(start_at[x] for x in range(slab))
    for k in lines:
        acc = lax.fori_loop(0, 128, functools.partial(one, k), acc, unroll=8)
    for x in range(slab):
        out[x] = acc[x]


def gravity_adjoint(lines, guard, total_x, lateral, head, weights, table, start_at):
    return pl.pallas_call(
        functools.partial(adjoint_kernel, lines, guard, total_x, lateral),
        out_shape=shape(start_at.shape),
        in_specs=[SMEM, SMEM, VMEM, VMEM],
        out_specs=VMEM,
        cost_estimate=pl.CostEstimate(
            flops=256 * len(lines) * start_at.size, bytes_accessed=8 * start_at.size, transcendentals=0
        ),
        compiler_params=room(8),
        name="gravity_adjoint",
    )(head, weights, table, start_at)


def small_call(kernel, outs, *values):
    single = not isinstance(outs, tuple)
    return pl.pallas_call(
        kernel,
        out_shape=outs,
        in_specs=[VMEM] * len(values),
        out_specs=VMEM if single else (VMEM,) * len(outs),
        compiler_params=room(2),
    )(*values)


def sum_kernel(first, second, out):
    out[...] = first[...] + second[...]


def plus(first, second):
    return small_call(sum_kernel, shape(first.shape), first, second)


def unpack_kernel(packed, other, out):
    steps, receivers = out.shape
    for b in range(receivers // 128):
        rows = slice(b * steps, (b + 1) * steps)
        out[:, b * 128 : (b + 1) * 128] = packed[rows, :] + other[rows, :]


def predict_kernel(*refs):
    pieces, out = refs[:-1], refs[-1]
    line = 0
    for piece in pieces:
        for k in range(piece.shape[0] // 128):
            block = piece[k * 128 : (k + 1) * 128, :].T
            out[line : line + 1, :] = jnp.sum(block, axis=0, keepdims=True)
            line += 1


def residual_kernel(packed, other, observed, weights, own):
    residual = packed[...] + other[...] - observed[...]
    weights[...] = residual.astype(jnp.bfloat16).astype(F32)
    mine = own.shape[0]
    for k in range(residual.shape[0] // mine):

        @pl.when(lax.axis_index("station") == k)
        def _(k=k):
            own[...] = residual[k * mine : (k + 1) * mine, :]


def cross_kernel(count, velocity, density, outer, inner, out):
    slab, rows, lanes = velocity.shape
    half = slab // 2
    lane = lax.broadcasted_iota(jnp.int32, (rows, lanes), 1)
    row = lax.broadcasted_iota(jnp.int32, (rows, lanes), 0)
    m, flipped = position()
    left_ok = jnp.where(m > 0, 0.5, 0.0)
    right_ok = jnp.where(m < count - 1, 0.5, 0.0)

    def slopes(field, side, x):
        f = field[x]
        if x > 0:
            below = 0.5 * field[x - 1]
        else:
            below = left_ok * jnp.where(flipped, inner[side], outer[side])
        if x < slab - 1:
            above = 0.5 * field[x + 1]
        else:
            above = right_ok * jnp.where(flipped, outer[side], inner[side])
        up = jnp.where(row < rows - 1, pltpu.roll(f, rows - 1, 0), 0.0)
        down = jnp.where(row > 0, pltpu.roll(f, 1, 0), 0.0)
        ahead = jnp.where(lane < lanes - 1, pltpu.roll(f, lanes - 1, 1), 0.0)
        back = jnp.where(lane > 0, pltpu.roll(f, 1, 1), 0.0)
        return above - below, (up - down) * 0.5, (ahead - back) * 0.5

    for x in range(slab):
        v = slopes(velocity, half, x)
        q = slopes(density, half + 1, x)
        out[0, x] = v[1] * q[2] - v[2] * q[1]
        out[1, x] = v[2] * q[0] - v[0] * q[2]
        out[2, x] = v[0] * q[1] - v[1] * q[0]


def cross_gradient_of(count, velocity, density, outer, inner):
    return pl.pallas_call(
        functools.partial(cross_kernel, count),
        out_shape=shape((3,) + velocity.shape),
        in_specs=[VMEM] * 4,
        out_specs=VMEM,
        cost_estimate=pl.CostEstimate(
            flops=60 * velocity.size, bytes_accessed=24 * velocity.size, transcendentals=0
        ),
        compiler_params=room(8),
        name="cross_gradient",
    )(velocity, density, outer, inner)


def per_device(
    p_now, p_prev, velocity, density, wavelet, source_cell, receiver_cells, station_cells, observed
):
    slab, lateral, vertical = p_now.shape
    count = lax.axis_size("mp")
    stations = lax.axis_size("station")
    steps = wavelet.shape[0]
    half = slab // 2
    assert half == REACH and count % 2 == 0 and stations % 4 == 0
    total_x = slab * count
    m, upper = position()
    s = lax.axis_index("station")
    block = lateral // stations
    chain = pairs_of(count, stations, chain_partner(count))
    together = lax.optimization_barrier

    def across(value):
        return lax.ppermute(value, AXES, chain)

    def swap(value, slab_bit, station_bit):
        pairs = pairs_of(count, stations, lambda i, k: (i ^ slab_bit, k ^ station_bit))
        return lax.ppermute(value, AXES, pairs)

    cur, message = first_message(p_now, velocity, density)
    outer = across(message)
    inner = swap(cur, 0, 1)
    edges = outer
    prev, cour, cour_outer, mask, dens, pulses = setup(
        count, source_cell, wavelet, p_prev, velocity, density
    )

    receiver_x, receiver_y = divmod_static(receiver_cells, lateral)
    receiver_j = receiver_x - m * slab
    receiver_j = jnp.where(upper, slab - 1 - receiver_j, receiver_j)
    inside = (receiver_j >= 0) & (receiver_j < half)
    place = jnp.where(inside, receiver_j * lateral + receiver_y, -1)[None, :]

    reach = min(total_x, 64)
    chunks = -(-total_x // reach)
    span = reach + slab - 1
    own_stations = station_cells.shape[0]
    n_stations = own_stations * stations

    def head_of(offset, cells):
        return jnp.concatenate([jnp.reshape(offset, (1,)).astype(jnp.int32), cells])

    def table_of(head):
        return gravity_table(total_x, slab, span, lateral, vertical, head)

    state = {}

    def exchange(bit):
        def work(gate):
            if bit == 1:
                known = jnp.stack([gate(station_cells).astype(F32), observed])[:, None, :]
            else:
                known = gate(state["known"])
            other = swap(known, 0, bit)
            upper = (s // bit) % 2 == 1
            state["known"] = jnp.concatenate(
                [jnp.where(upper, other, known), jnp.where(upper, known, other)], 1
            )

        return work

    def share_edges(gate):
        state["inner"] = swap(gate(edges), 0, 1)

    def cross(gate):
        state["cross"] = cross_gradient_of(count, velocity, density, edges, gate(state["inner"]))
        return "cross"

    lines = n_stations // 128

    def build_table(gate):
        known = gate(state["known"])
        cells = known[0].reshape(-1).astype(jnp.int32)
        head = head_of(0, cells)
        zero, head, observed_all, where = together(
            (jnp.zeros((1,), jnp.int32), head, known[1].reshape(-1, 128), place)
        )
        state.update(head=head, observed=observed_all, place=where)
        state["table"] = table_of(zero)
        return "table"

    pieces = 4
    part = n_stations // pieces

    def forward(i):
        def work(gate):
            state[i] = gravity_forward(
                i * part, part, 0, total_x, lateral, gate(state["head"]), state["table"], dens
            )
            return i

        return work

    def predict(gate):
        sums = [state[i] for i in range(pieces)]
        sums[0] = gate(sums[0])
        packed = small_call(predict_kernel, shape((lines, 128)), *sums)
        state["packed"], state["other"] = packed, swap(packed, 0, 1)

    def add_up(bit):
        def work(gate):
            packed = plus(gate(state["packed"]), state["other"])
            state["packed"], state["other"] = packed, swap(packed, bit, 1)

        return work

    def residual(gate):
        state["weights"], state["own"] = small_call(
            residual_kernel,
            (shape((lines, 128)), shape((lines // stations, 128))),
            gate(state["packed"]),
            state["other"],
            state["observed"],
        )
        state["gradient"] = jnp.zeros((slab, block, vertical), F32)
        return "weights"

    def adjoint(half_lines):
        def work(gate):
            state["gradient"] = gravity_adjoint(
                half_lines,
                0,
                total_x,
                lateral,
                state["head"],
                gate(state["weights"]),
                state["table"],
                state["gradient"],
            )
            return "gradient"

        return work

    def both(first, second):
        def work(gate):
            first(gate)
            return second(gate)

        return work

    hidden = chunks == 1 and count & (count - 1) == 0
    jobs = [exchange(1 << b) for b in range(stations.bit_length() - 1)]
    if hidden:
        jobs += [build_table] + [forward(i) for i in range(pieces)] + [predict]
        jobs += [add_up(1 << b) for b in range(count.bit_length() - 1)] + [residual]
        jobs += [adjoint(range(lines // 2)), adjoint(range(lines // 2, lines))]
    jobs[0] = both(share_edges, jobs[0])
    jobs.insert(2, cross)
    assert len(jobs) < steps

    surf = cour
    for step in range(steps):
        if step:
            outer = across(cur)
            inner = swap(cur, 0, 1)
        base, surf = local_step(step, pulses, mask, cur, prev, cour, surf)

        def gate(value):
            nonlocal base
            base, value = together((base, value))
            return value

        ready = None
        if step and jobs:
            ready = jobs.pop(0)(gate)
        cur, prev = halo_step(base, cour, cour_outer, outer, inner), cur
        if ready is not None:
            cur, state[ready] = together((cur, state[ready]))

    sibling = swap(cur, 0, 1)
    packed = recorded_traces(steps - 1, state.get("place", place), cur, surf)
    other = swap(packed, 0, 1)
    if count & (count - 1) == 0:
        bit = 1
        while bit < count:
            packed = plus(packed, other)
            other = swap(packed, bit, 1)
            if bit == 1:
                wavefield = join(cur, sibling)
                other, wavefield = together((other, wavefield))
            bit *= 2
    else:
        wavefield = join(cur, sibling)
        packed = lax.psum(packed + other, "mp")
        other = jnp.zeros_like(packed)
    traces = small_call(unpack_kernel, shape((steps, receiver_cells.shape[0])), packed, other)
    if hidden:
        gravity_residual = state["own"].reshape(-1)
        density_gradient = state["gradient"]
    else:
        cells = state["known"][0].reshape(-1).astype(jnp.int32)

        def add_chunk(i, total):
            head = head_of(i * reach, cells)
            return total + gravity_forward(
                0, n_stations, reach, total_x, lateral, head, table_of(head[:1]), dens
            )

        sums = lax.fori_loop(0, chunks, add_chunk, jnp.zeros((n_stations, vertical), F32))
        predicted = jnp.sum(sums, axis=1)
        predicted = lax.psum(predicted + swap(predicted, 0, 1), "mp")
        difference = predicted - state["known"][1].reshape(-1)
        gravity_residual = lax.dynamic_slice(difference, (s * own_stations,), (own_stations,))
        weights = difference.astype(jnp.bfloat16).astype(F32).reshape(-1, 128)

        def back_chunk(i, total):
            head = head_of(i * reach, cells)
            return gravity_adjoint(
                range(lines), reach, total_x, lateral, head, weights, table_of(head[:1]), total
            )

        density_gradient = lax.fori_loop(
            0, chunks, back_chunk, jnp.zeros((slab, block, vertical), F32)
        )
    return (wavefield, traces, gravity_residual, density_gradient, state["cross"])


def solution(mesh):
    in_specs = (
        P("mp", None, None),
        P("mp", None, None),
        P("mp", None, None),
        P("mp", None, None),
        P(),
        P(),
        P(),
        P("station"),
        P("station"),
    )
    out_specs = (
        P("mp", None, None),
        P(),
        P("station"),
        P("mp", "station", None),
        P(None, "mp", None, None),
    )

    return jax.shard_map(
        per_device, mesh=mesh, in_specs=in_specs, out_specs=out_specs, check_vma=False
    )
```

```python
import functools

import jax
import jax.numpy as jnp
from jax import lax
from jax.experimental import pallas as pl
from jax.experimental.pallas import tpu as pltpu
from jax.sharding import PartitionSpec as P


STENCIL = (-205.0 / 72.0, 8.0 / 5.0, -1.0 / 5.0, 8.0 / 315.0, -1.0 / 560.0)
TIME_RATIO = 0.1
REACH = 4
AXES = ("mp", "station")
VMEM = pl.BlockSpec(memory_space=pltpu.VMEM)
SMEM = pl.BlockSpec(memory_space=pltpu.SMEM)
HBM = pl.BlockSpec(memory_space=pltpu.HBM)
F32 = jnp.float32
MIB = 1 << 20


def room(mib):
    return pltpu.CompilerParams(vmem_limit_bytes=mib * MIB)


def shape(dims):
    return jax.ShapeDtypeStruct(dims, F32)


def pairs_of(count, stations, partner):
    return [
        (m * stations + s, (lambda t: t[0] * stations + t[1])(partner(m, s)))
        for m in range(count)
        for s in range(stations)
    ]


def chain_partner(count):
    def partner(m, s):
        if s % 2 == 0:
            return (m ^ 1, s)
        other = m + 1 if m % 2 else m - 1
        if other < 0 or other >= count:
            return (m, s ^ 2)
        return (other, s)

    return partner


def position():
    m = lax.axis_index("mp")
    return m, (m + lax.axis_index("station")) % 2 == 0


def divmod_static(value, divisor):
    if divisor & (divisor - 1) == 0:
        return value >> (divisor.bit_length() - 1), value & (divisor - 1)
    return value // divisor, value % divisor


def in_place(*values):
    return [pltpu.with_memory_space_constraint(value, pltpu.HBM) for value in values]


def run_copies(pairs, sems):
    copies = [pltpu.make_async_copy(a, b, sems.at[i]) for i, (a, b) in enumerate(pairs)]
    for copy in copies:
        copy.start()
    for copy in copies:
        copy.wait()


def plane_of(upper, j, slab):
    return jnp.where(upper, slab - 1 - j, j)


def first_kernel(now, cur, sems):
    slab = now.shape[0]
    _, upper = position()
    run_copies([(now.at[plane_of(upper, j, slab)], cur.at[j]) for j in range(slab // 2)], sems)


def first_planes(p_now):
    slab, rows, lanes = p_now.shape
    half = slab // 2
    return pl.pallas_call(
        first_kernel,
        out_shape=shape((half, rows, lanes)),
        in_specs=[HBM],
        out_specs=VMEM,
        scratch_shapes=[pltpu.SemaphoreType.DMA((half,))],
        compiler_params=room(2),
        name="first_planes",
    )(*in_place(p_now))


def setup_kernel(
    count,
    source,
    wavelet,
    cells,
    observed,
    p_prev,
    velocity,
    density,
    prev,
    cour,
    cour_outer,
    mask,
    dens,
    pulses,
    known,
    edges,
    vel,
    raw,
    sems,
):
    slab = p_prev.shape[0]
    half, rows, lanes = prev.shape
    m, upper = position()
    pairs = []
    for j in range(half):
        plane = plane_of(upper, j, slab)
        pairs += [(p_prev.at[plane], prev.at[j]), (velocity.at[plane], vel.at[j])]
    low = half * (lax.axis_index("station") % 2)
    pairs += [(density.at[pl.ds(low, half)], raw)]
    edge = plane_of(upper, 0, slab)
    pairs += [(velocity.at[edge], edges.at[0]), (density.at[edge], edges.at[1])]
    run_copies(pairs, sems)
    known[0] = cells[...].astype(F32)
    known[1] = observed[...]
    for n in range(pulses.shape[0]):
        pulses[n : n + 1, :] = jnp.full((1, lanes), wavelet[n], F32)
    outer_ok = jnp.where(upper, m < count - 1, m > 0)
    outer_ok = jnp.where(outer_ok, 1.0, 0.0)
    column, source_lane = divmod_static(source[0], lanes)
    source_x, source_row = divmod_static(column, rows)
    row = lax.broadcasted_iota(jnp.int32, (rows, lanes), 0)
    lane = lax.broadcasted_iota(jnp.int32, (rows, lanes), 1)
    spot = jnp.where((row == source_row) & (lane == source_lane), 1.0, 0.0)
    for j in range(half):
        scaled = TIME_RATIO * vel[j]
        square = scaled * scaled
        cour[j] = square
        cour_outer[j] = square * outer_ok
        here = m * slab + plane_of(upper, j, slab) == source_x
        mask[j] = spot * jnp.where(here, 1.0, 0.0)
        dens[j] = raw[j].astype(jnp.bfloat16).astype(F32)


def setup(count, source_cell, wavelet, cells, observed, p_prev, velocity, density):
    slab, rows, lanes = p_prev.shape
    half = slab // 2
    part = shape((half, rows, lanes))
    held = pltpu.VMEM((half, rows, lanes), F32)
    return pl.pallas_call(
        functools.partial(setup_kernel, count),
        out_shape=(part,) * 5
        + (
            shape((wavelet.shape[0], lanes)),
            shape((2,) + cells.shape),
            shape((2, rows, lanes)),
        ),
        in_specs=[SMEM, SMEM, VMEM, VMEM] + [HBM] * 3,
        out_specs=(VMEM,) * 8,
        scratch_shapes=[held, held, pltpu.SemaphoreType.DMA((2 * half + 3,))],
        compiler_params=room(4),
        cost_estimate=pl.CostEstimate(
            flops=20 * half * rows * lanes, bytes_accessed=32 * half * rows * lanes, transcendentals=0
        ),
        name="setup",
    )(source_cell, wavelet, cells, observed, *in_place(p_prev, velocity, density))


def local_kernel(step, pulses, mask, cur, prev, cour, surf_in, base, surf, pad):
    planes, rows, lanes = prev.shape
    lane = lax.broadcasted_iota(jnp.int32, (rows, lanes), 1)
    weights = {}
    for d in range(1, REACH + 1):
        weights[d] = jnp.where(lane >= d, STENCIL[d], 0.0)
        weights[-d] = jnp.where(lane < lanes - d, STENCIL[d], 0.0)
    pulse = pulses[step : step + 1, :]
    for j in range(planes):
        pad[j, 0:8, :] = jnp.zeros((8, lanes), F32)
        pad[j, 8 + rows : 16 + rows, :] = jnp.zeros((8, lanes), F32)
        pad[j, 8 : 8 + rows, :] = cur[j]
    for j in range(planes):
        c = cur[j]
        acc = 3.0 * STENCIL[0] * c
        for d in range(1, REACH + 1):
            acc = acc + weights[d] * pltpu.roll(c, d, 1) + weights[-d] * pltpu.roll(c, lanes - d, 1)
            near = pad[j, 8 + d : 8 + d + rows, :] + pad[j, 8 - d : 8 - d + rows, :]
            for i in (j - d, j + d):
                if 0 <= i < planes:
                    near = near + cur[i]
            acc = acc + STENCIL[d] * near
        base[j] = 2.0 * c - prev[j] + cour[j] * acc + pulse * mask[j]
        if step == 0:
            surf[j] = jnp.zeros((rows, lanes), F32)
        else:
            surf[j] = jnp.where(
                lane == step - 1, jnp.broadcast_to(c[:, 0:1], (rows, lanes)), surf_in[j]
            )


def local_step(step, pulses, mask, cur, prev, cour, surf):
    planes, rows, lanes = cur.shape
    return pl.pallas_call(
        functools.partial(local_kernel, step),
        out_shape=(shape(cur.shape), shape(cur.shape)),
        in_specs=[VMEM] * 6,
        out_specs=(VMEM, VMEM),
        scratch_shapes=[pltpu.VMEM((planes, rows + 16, lanes), F32)],
        compiler_params=room(2),
        cost_estimate=pl.CostEstimate(
            flops=60 * cur.size, bytes_accessed=24 * cur.size, transcendentals=0
        ),
        name="wave_local",
    )(pulses, mask, cur, prev, cour, surf)


def halo_kernel(base, cour, cour_outer, outer, inner, out):
    planes = base.shape[0]
    for j in range(planes):
        far = near = None
        for d in range(j + 1, REACH + 1):
            term = STENCIL[d] * outer[d - j - 1]
            far = term if far is None else far + term
        for d in range(planes - j, REACH + 1):
            term = STENCIL[d] * inner[2 * planes - 1 - j - d]
            near = term if near is None else near + term
        out[j] = base[j] + (cour[j] * near + cour_outer[j] * far)


def halo_step(base, cour, cour_outer, outer, inner):
    return pl.pallas_call(
        halo_kernel,
        out_shape=shape(base.shape),
        in_specs=[VMEM] * 5,
        out_specs=VMEM,
        compiler_params=room(2),
        cost_estimate=pl.CostEstimate(
            flops=12 * base.size, bytes_accessed=20 * base.size, transcendentals=0
        ),
        name="wave_halo",
    )(base, cour, cour_outer, outer, inner)


def trace_kernel(step, place, cur, surf, out):
    planes, rows, lanes = cur.shape
    receivers = place.shape[1]
    steps = step + 1
    lane = lax.broadcasted_iota(jnp.int32, (rows, lanes), 1)
    columns = jnp.concatenate(
        [
            jnp.where(lane == step, jnp.broadcast_to(cur[j, :, 0:1], (rows, lanes)), surf[j])
            for j in range(planes)
        ],
        0,
    )
    columns = columns.T
    spot = lax.broadcasted_iota(jnp.int32, (planes * rows, receivers), 0)
    pick = jnp.where(place[...] == spot, 1.0, 0.0).astype(jnp.bfloat16)
    total = None
    for _ in range(3):
        part = columns.astype(jnp.bfloat16)
        columns = columns - part.astype(F32)
        term = jnp.dot(part, pick, preferred_element_type=F32)
        total = term if total is None else total + term
    for b in range(receivers // 128):
        out[b * steps : (b + 1) * steps, :] = total[:steps, b * 128 : (b + 1) * 128]


def recorded_traces(step, place, cur, surf):
    return pl.pallas_call(
        functools.partial(trace_kernel, step),
        out_shape=shape(((step + 1) * (place.shape[1] // 128), 128)),
        in_specs=[VMEM] * 3,
        out_specs=VMEM,
        compiler_params=room(4),
        name="traces",
    )(place, cur, surf)


def join_kernel(own, sibling, out, sems):
    slab = out.shape[0]
    _, upper = position()
    pairs = []
    for j in range(slab // 2):
        here = plane_of(upper, j, slab)
        pairs += [(own.at[j], out.at[here]), (sibling.at[j], out.at[slab - 1 - here])]
    run_copies(pairs, sems)


def join(own, sibling):
    half, rows, lanes = own.shape
    return pl.pallas_call(
        join_kernel,
        out_shape=shape((2 * half, rows, lanes)),
        in_specs=[VMEM] * 2,
        out_specs=HBM,
        scratch_shapes=[pltpu.SemaphoreType.DMA((2 * half,))],
        compiler_params=room(2),
        name="join",
    )(own, sibling)


def on_chip(value):
    return pltpu.with_memory_space_constraint(value, pltpu.VMEM)


def table_low(total_x, slab, offset):
    m, _ = position()
    return m * slab - (total_x - 1) + offset


def table_kernel(total_x, slab, spread, head, out):
    lanes = out.shape[1]
    low = table_low(total_x, slab, head[0])
    dy = (lax.broadcasted_iota(jnp.int32, (spread, lanes), 0) - (spread // 2 - 1)).astype(F32)
    dz = (lax.broadcasted_iota(jnp.int32, (spread, lanes), 1) + 1).astype(F32)
    side = dy * dy
    deep = dz * dz

    def one(t, carry):
        dx = (t + low).astype(F32)
        inverse = lax.rsqrt(dx * dx + side + deep)
        value = dz * (inverse * inverse * inverse)
        start = pl.multiple_of(t * spread, spread)
        out[pl.ds(start, spread), :] = value.astype(jnp.bfloat16).astype(F32)
        return carry

    lax.fori_loop(0, out.shape[0] // spread, one, 0)


def gravity_table(total_x, slab, depth, lateral, vertical, head):
    size = depth * 2 * lateral * vertical
    return pl.pallas_call(
        functools.partial(table_kernel, total_x, slab, 2 * lateral),
        out_shape=shape((depth * 2 * lateral, vertical)),
        in_specs=[SMEM],
        out_specs=VMEM,
        cost_estimate=pl.CostEstimate(
            flops=20 * size, bytes_accessed=4 * size, transcendentals=2 * size
        ),
        compiler_params=room(8),
        name="gravity_table",
    )(head)


def forward_kernel(first, guard, total_x, lateral, head, table, dens, out):
    planes, rows, _ = dens.shape
    count = out.shape[0]
    spread = 2 * lateral
    core = lax.axis_index("station") % 2
    lead = total_x - 1 - head[0]
    if guard:
        out[...] = jnp.zeros_like(out)

    def window(s):
        sx, sy = divmod_static(head[1 + first + s], lateral)
        shift = lead - sx
        return shift, (shift + core * planes) * spread + (lateral - 1 - sy)

    def several(s, starts):
        totals = [None] * len(starts)
        for p in range(planes):
            for r in range(0, rows, 8):
                value = dens[p, r : r + 8, :]
                for q, start in enumerate(starts):
                    term = table[pl.ds(start + (p * spread + r), 8), :] * value
                    totals[q] = term if totals[q] is None else totals[q] + term
        for q, total in enumerate(totals):
            out[pl.ds(s + q, 1), :] = jnp.sum(total, axis=0, keepdims=True)

    def one(g, carry):
        if guard:
            shift, start = window(g)
            pl.when((shift >= 0) & (shift < guard))(lambda: several(g, [start]))
        else:
            several(4 * g, [window(4 * g + q)[1] for q in range(4)])
        return carry

    if guard:
        lax.fori_loop(0, count, one, 0)
    else:
        lax.fori_loop(0, count // 4, one, 0, unroll=2)


def gravity_forward(first, count, guard, total_x, lateral, head, table, dens):
    work = count * dens.size
    return pl.pallas_call(
        functools.partial(forward_kernel, first, guard, total_x, lateral),
        out_shape=shape((count, dens.shape[2])),
        in_specs=[SMEM, VMEM, VMEM],
        out_specs=VMEM,
        cost_estimate=pl.CostEstimate(
            flops=4 * work, bytes_accessed=4 * dens.size, transcendentals=0
        ),
        compiler_params=room(8),
        name="gravity_forward",
    )(head, on_chip(table), dens)


def adjoint_kernel(lines, guard, total_x, lateral, head, weights, table, start_at, out):
    slab, rows, _ = out.shape
    spread = 2 * lateral
    lead = total_x - 1 - head[0]
    row_low = lax.axis_index("station") * rows

    def one(k, i, acc):
        sx, sy = divmod_static(head[1 + 128 * k + i], lateral)
        shift = lead - sx
        weight = weights[k, i]
        if guard:
            keep = (shift >= 0) & (shift < guard)
            shift = jnp.where(keep, shift, 0)
            weight = jnp.where(keep, weight, 0.0)
        start = shift * spread + (lateral - 1 - sy + row_low)
        return tuple(
            acc[x] + weight * table[pl.ds(start + x * spread, rows), :] for x in range(slab)
        )

    acc = tuple(start_at[x] for x in range(slab))
    for k in lines:
        acc = lax.fori_loop(0, 128, functools.partial(one, k), acc, unroll=8)
    for x in range(slab):
        out[x] = acc[x]


def gravity_adjoint(lines, guard, total_x, lateral, head, weights, table, start_at):
    return pl.pallas_call(
        functools.partial(adjoint_kernel, lines, guard, total_x, lateral),
        out_shape=shape(start_at.shape),
        in_specs=[SMEM, SMEM, VMEM, VMEM],
        out_specs=VMEM,
        cost_estimate=pl.CostEstimate(
            flops=256 * len(lines) * start_at.size, bytes_accessed=8 * start_at.size, transcendentals=0
        ),
        compiler_params=room(8),
        name="gravity_adjoint",
    )(head, weights, table, start_at)


def small_call(kernel, outs, *values):
    single = not isinstance(outs, tuple)
    return pl.pallas_call(
        kernel,
        out_shape=outs,
        in_specs=[VMEM] * len(values),
        out_specs=VMEM if single else (VMEM,) * len(outs),
        compiler_params=room(2),
    )(*values)


def sum_kernel(first, second, out):
    out[...] = first[...] + second[...]


def plus(first, second):
    return small_call(sum_kernel, shape(first.shape), first, second)


def unpack_kernel(packed, other, out):
    steps, receivers = out.shape
    for b in range(receivers // 128):
        rows = slice(b * steps, (b + 1) * steps)
        out[:, b * 128 : (b + 1) * 128] = packed[rows, :] + other[rows, :]


def predict_kernel(*refs):
    pieces, out = refs[:-1], refs[-1]
    line = 0
    for piece in pieces:
        for k in range(piece.shape[0] // 128):
            block = piece[k * 128 : (k + 1) * 128, :].T
            out[line : line + 1, :] = jnp.sum(block, axis=0, keepdims=True)
            line += 1


def residual_kernel(packed, other, observed, weights, own):
    residual = packed[...] + other[...] - observed[...]
    weights[...] = residual.astype(jnp.bfloat16).astype(F32)
    mine = own.shape[0]
    for k in range(residual.shape[0] // mine):

        @pl.when(lax.axis_index("station") == k)
        def _(k=k):
            own[...] = residual[k * mine : (k + 1) * mine, :]


def cross_kernel(count, velocity, density, outer, inner, out):
    slab, rows, lanes = velocity.shape
    lane = lax.broadcasted_iota(jnp.int32, (rows, lanes), 1)
    row = lax.broadcasted_iota(jnp.int32, (rows, lanes), 0)
    m, flipped = position()
    left_ok = jnp.where(m > 0, 0.5, 0.0)
    right_ok = jnp.where(m < count - 1, 0.5, 0.0)

    def slopes(field, side, x):
        f = field[x]
        if x > 0:
            below = 0.5 * field[x - 1]
        else:
            below = left_ok * jnp.where(flipped, inner[side], outer[side])
        if x < slab - 1:
            above = 0.5 * field[x + 1]
        else:
            above = right_ok * jnp.where(flipped, outer[side], inner[side])
        up = jnp.where(row < rows - 1, pltpu.roll(f, rows - 1, 0), 0.0)
        down = jnp.where(row > 0, pltpu.roll(f, 1, 0), 0.0)
        ahead = jnp.where(lane < lanes - 1, pltpu.roll(f, lanes - 1, 1), 0.0)
        back = jnp.where(lane > 0, pltpu.roll(f, 1, 1), 0.0)
        return above - below, (up - down) * 0.5, (ahead - back) * 0.5

    for x in range(slab):
        v = slopes(velocity, 0, x)
        q = slopes(density, 1, x)
        out[0, x] = v[1] * q[2] - v[2] * q[1]
        out[1, x] = v[2] * q[0] - v[0] * q[2]
        out[2, x] = v[0] * q[1] - v[1] * q[0]


def cross_gradient_of(count, velocity, density, outer, inner):
    return pl.pallas_call(
        functools.partial(cross_kernel, count),
        out_shape=shape((3,) + velocity.shape),
        in_specs=[VMEM] * 4,
        out_specs=VMEM,
        cost_estimate=pl.CostEstimate(
            flops=60 * velocity.size, bytes_accessed=24 * velocity.size, transcendentals=0
        ),
        compiler_params=room(8),
        name="cross_gradient",
    )(velocity, density, outer, inner)


def per_device(
    p_now, p_prev, velocity, density, wavelet, source_cell, receiver_cells, station_cells, observed
):
    slab, lateral, vertical = p_now.shape
    count = lax.axis_size("mp")
    stations = lax.axis_size("station")
    steps = wavelet.shape[0]
    half = slab // 2
    assert half == REACH and count % 2 == 0 and stations % 4 == 0
    total_x = slab * count
    m, upper = position()
    s = lax.axis_index("station")
    block = lateral // stations
    chain = pairs_of(count, stations, chain_partner(count))
    together = lax.optimization_barrier

    def across(value):
        return lax.ppermute(value, AXES, chain)

    def swap(value, slab_bit, station_bit):
        pairs = pairs_of(count, stations, lambda i, k: (i ^ slab_bit, k ^ station_bit))
        return lax.ppermute(value, AXES, pairs)

    cur = first_planes(p_now)
    outer = across(cur)
    inner = swap(cur, 0, 1)
    prev, cour, cour_outer, mask, dens, pulses, known, edges = setup(
        count,
        source_cell,
        wavelet,
        station_cells.reshape(-1, 128),
        observed.reshape(-1, 128),
        p_prev,
        velocity,
        density,
    )

    receiver_x, receiver_y = divmod_static(receiver_cells, lateral)
    receiver_j = receiver_x - m * slab
    receiver_j = jnp.where(upper, slab - 1 - receiver_j, receiver_j)
    inside = (receiver_j >= 0) & (receiver_j < half)
    place = jnp.where(inside, receiver_j * lateral + receiver_y, -1)[None, :]

    reach = min(total_x, 64)
    chunks = -(-total_x // reach)
    span = reach + slab - 1
    own_stations = station_cells.shape[0]
    n_stations = own_stations * stations

    def head_of(offset, cells):
        return jnp.concatenate([jnp.reshape(offset, (1,)).astype(jnp.int32), cells])

    def table_of(head):
        return gravity_table(total_x, slab, span, lateral, vertical, head)

    state = {"known": known, "edges": edges}

    def exchange(bit):
        def work(gate):
            known = gate(state["known"])
            other = swap(known, 0, bit)
            upper = (s // bit) % 2 == 1
            state["known"] = jnp.concatenate(
                [jnp.where(upper, other, known), jnp.where(upper, known, other)], 1
            )

        return work

    def send_edges(gate):
        state["outer"] = across(gate(state["edges"]))

    def share_edges(gate):
        state["inner"] = swap(gate(state["outer"]), 0, 1)

    def cross(gate):
        state["cross"] = cross_gradient_of(
            count, velocity, density, state["outer"], gate(state["inner"])
        )
        return "cross"

    lines = n_stations // 128

    def build_table(gate):
        known = gate(state["known"])
        cells = known[0].reshape(-1).astype(jnp.int32)
        head = head_of(0, cells)
        zero, head, observed_all, where = together(
            (jnp.zeros((1,), jnp.int32), head, known[1].reshape(-1, 128), place)
        )
        state.update(head=head, observed=observed_all, place=where)
        state["table"] = table_of(zero)
        return "table"

    pieces = 4
    part = n_stations // pieces

    def forward(i):
        def work(gate):
            state[i] = gravity_forward(
                i * part, part, 0, total_x, lateral, gate(state["head"]), state["table"], dens
            )
            return i

        return work

    def predict(gate):
        sums = [state[i] for i in range(pieces)]
        sums[0] = gate(sums[0])
        packed = small_call(predict_kernel, shape((lines, 128)), *sums)
        state["packed"], state["other"] = packed, swap(packed, 0, 1)

    def add_up(bit):
        def work(gate):
            packed = plus(gate(state["packed"]), state["other"])
            state["packed"], state["other"] = packed, swap(packed, bit, 1)

        return work

    def residual(gate):
        state["weights"], state["own"] = small_call(
            residual_kernel,
            (shape((lines, 128)), shape((lines // stations, 128))),
            gate(state["packed"]),
            state["other"],
            state["observed"],
        )
        state["gradient"] = jnp.zeros((slab, block, vertical), F32)
        return "weights"

    def adjoint(half_lines):
        def work(gate):
            state["gradient"] = gravity_adjoint(
                half_lines,
                0,
                total_x,
                lateral,
                state["head"],
                gate(state["weights"]),
                state["table"],
                state["gradient"],
            )
            return "gradient"

        return work

    def both(first, second):
        def work(gate):
            first(gate)
            return second(gate)

        return work

    hidden = chunks == 1 and count & (count - 1) == 0
    jobs = [exchange(1 << b) for b in range(stations.bit_length() - 1)]
    if hidden:
        jobs += [build_table] + [forward(i) for i in range(pieces)] + [predict]
        jobs += [add_up(1 << b) for b in range(count.bit_length() - 1)] + [residual]
        jobs += [adjoint(range(lines // 2)), adjoint(range(lines // 2, lines))]
    jobs[0] = both(send_edges, jobs[0])
    jobs[1] = both(share_edges, jobs[1])
    jobs.insert(2, cross)
    assert len(jobs) < steps

    surf = cour
    for step in range(steps):
        if step:
            outer = across(cur)
            inner = swap(cur, 0, 1)
        base, surf = local_step(step, pulses, mask, cur, prev, cour, surf)

        def gate(value):
            nonlocal base
            base, value = together((base, value))
            return value

        ready = None
        if step and jobs:
            ready = jobs.pop(0)(gate)
        cur, prev = halo_step(base, cour, cour_outer, outer, inner), cur
        if ready is not None:
            cur, state[ready] = together((cur, state[ready]))

    sibling = swap(cur, 0, 1)
    packed = recorded_traces(steps - 1, state.get("place", place), cur, surf)
    other = swap(packed, 0, 1)
    if count & (count - 1) == 0:
        bit = 1
        while bit < count:
            packed = plus(packed, other)
            other = swap(packed, bit, 1)
            if bit == 1:
                wavefield = join(cur, sibling)
            if bit == 2:
                other, wavefield = together((other, wavefield))
            bit *= 2
    else:
        wavefield = join(cur, sibling)
        packed = lax.psum(packed + other, "mp")
        other = jnp.zeros_like(packed)
    traces = small_call(unpack_kernel, shape((steps, receiver_cells.shape[0])), packed, other)
    if hidden:
        gravity_residual = state["own"].reshape(-1)
        density_gradient = state["gradient"]
    else:
        cells = state["known"][0].reshape(-1).astype(jnp.int32)

        def add_chunk(i, total):
            head = head_of(i * reach, cells)
            return total + gravity_forward(
                0, n_stations, reach, total_x, lateral, head, table_of(head[:1]), dens
            )

        sums = lax.fori_loop(0, chunks, add_chunk, jnp.zeros((n_stations, vertical), F32))
        predicted = jnp.sum(sums, axis=1)
        predicted = lax.psum(predicted + swap(predicted, 0, 1), "mp")
        difference = predicted - state["known"][1].reshape(-1)
        gravity_residual = lax.dynamic_slice(difference, (s * own_stations,), (own_stations,))
        weights = difference.astype(jnp.bfloat16).astype(F32).reshape(-1, 128)

        def back_chunk(i, total):
            head = head_of(i * reach, cells)
            return gravity_adjoint(
                range(lines), reach, total_x, lateral, head, weights, table_of(head[:1]), total
            )

        density_gradient = lax.fori_loop(
            0, chunks, back_chunk, jnp.zeros((slab, block, vertical), F32)
        )
    return (wavefield, traces, gravity_residual, density_gradient, state["cross"])


def solution(mesh):
    in_specs = (
        P("mp", None, None),
        P("mp", None, None),
        P("mp", None, None),
        P("mp", None, None),
        P(),
        P(),
        P(),
        P("station"),
        P("station"),
    )
    out_specs = (
        P("mp", None, None),
        P(),
        P("station"),
        P("mp", "station", None),
        P(None, "mp", None, None),
    )

    return jax.shard_map(
        per_device, mesh=mesh, in_specs=in_specs, out_specs=out_specs, check_vma=False
    )
```

```python
import functools

import jax
import jax.numpy as jnp
from jax import lax
from jax.experimental import pallas as pl
from jax.experimental.pallas import tpu as pltpu
from jax.sharding import PartitionSpec as P


STENCIL = (-205.0 / 72.0, 8.0 / 5.0, -1.0 / 5.0, 8.0 / 315.0, -1.0 / 560.0)
TIME_RATIO = 0.1
REACH = 4
AXES = ("mp", "station")
VMEM = pl.BlockSpec(memory_space=pltpu.VMEM)
SMEM = pl.BlockSpec(memory_space=pltpu.SMEM)
HBM = pl.BlockSpec(memory_space=pltpu.HBM)
F32 = jnp.float32
MIB = 1 << 20


def room(mib):
    return pltpu.CompilerParams(vmem_limit_bytes=mib * MIB)


def shape(dims):
    return jax.ShapeDtypeStruct(dims, F32)


def pairs_of(count, stations, partner):
    return [
        (m * stations + s, (lambda t: t[0] * stations + t[1])(partner(m, s)))
        for m in range(count)
        for s in range(stations)
    ]


def chain_partner(count):
    def partner(m, s):
        if s % 2 == 0:
            return (m ^ 1, s)
        other = m + 1 if m % 2 else m - 1
        if other < 0 or other >= count:
            return (m, s ^ 2)
        return (other, s)

    return partner


def position():
    m = lax.axis_index("mp")
    return m, (m + lax.axis_index("station")) % 2 == 0


def divmod_static(value, divisor):
    if divisor & (divisor - 1) == 0:
        return value >> (divisor.bit_length() - 1), value & (divisor - 1)
    return value // divisor, value % divisor


def in_place(*values):
    return [pltpu.with_memory_space_constraint(value, pltpu.HBM) for value in values]


def run_copies(pairs, sems):
    copies = [pltpu.make_async_copy(a, b, sems.at[i]) for i, (a, b) in enumerate(pairs)]
    for copy in copies:
        copy.start()
    for copy in copies:
        copy.wait()


def plane_of(upper, j, slab):
    return jnp.where(upper, slab - 1 - j, j)


def first_kernel(now, cur, sems):
    slab = now.shape[0]
    _, upper = position()
    run_copies([(now.at[plane_of(upper, j, slab)], cur.at[j]) for j in range(slab // 2)], sems)


def first_planes(p_now):
    slab, rows, lanes = p_now.shape
    half = slab // 2
    return pl.pallas_call(
        first_kernel,
        out_shape=shape((half, rows, lanes)),
        in_specs=[HBM],
        out_specs=VMEM,
        scratch_shapes=[pltpu.SemaphoreType.DMA((half,))],
        compiler_params=room(2),
        name="first_planes",
    )(*in_place(p_now))


def setup_kernel(
    count,
    source,
    wavelet_in,
    cells_in,
    observed,
    p_prev,
    velocity,
    density,
    prev,
    cour,
    cour_outer,
    mask,
    dens,
    pulses,
    known,
    edges,
    vel,
    raw,
    wavelet,
    cells,
    sems,
):
    slab = p_prev.shape[0]
    half, rows, lanes = prev.shape
    m, upper = position()
    pairs = []
    for j in range(half):
        plane = plane_of(upper, j, slab)
        pairs += [(p_prev.at[plane], prev.at[j]), (velocity.at[plane], vel.at[j])]
    low = half * (lax.axis_index("station") % 2)
    pairs += [(density.at[pl.ds(low, half)], raw)]
    edge = plane_of(upper, 0, slab)
    pairs += [(velocity.at[edge], edges.at[0]), (density.at[edge], edges.at[1])]
    pairs += [(wavelet_in, wavelet), (cells_in, cells), (observed, known.at[1])]
    run_copies(pairs, sems)
    known[0] = cells[...].astype(F32)
    for n in range(pulses.shape[0]):
        pulses[n : n + 1, :] = jnp.full((1, lanes), wavelet[n], F32)
    outer_ok = jnp.where(upper, m < count - 1, m > 0)
    outer_ok = jnp.where(outer_ok, 1.0, 0.0)
    column, source_lane = divmod_static(source[0], lanes)
    source_x, source_row = divmod_static(column, rows)
    row = lax.broadcasted_iota(jnp.int32, (rows, lanes), 0)
    lane = lax.broadcasted_iota(jnp.int32, (rows, lanes), 1)
    spot = jnp.where((row == source_row) & (lane == source_lane), 1.0, 0.0)
    for j in range(half):
        scaled = TIME_RATIO * vel[j]
        square = scaled * scaled
        cour[j] = square
        cour_outer[j] = square * outer_ok
        here = m * slab + plane_of(upper, j, slab) == source_x
        mask[j] = spot * jnp.where(here, 1.0, 0.0)
        dens[j] = raw[j].astype(jnp.bfloat16).astype(F32)


def setup(count, source_cell, wavelet, cells, observed, p_prev, velocity, density):
    slab, rows, lanes = p_prev.shape
    half = slab // 2
    part = shape((half, rows, lanes))
    held = pltpu.VMEM((half, rows, lanes), F32)
    return pl.pallas_call(
        functools.partial(setup_kernel, count),
        out_shape=(part,) * 5
        + (
            shape((wavelet.shape[0], lanes)),
            shape((2,) + cells.shape),
            shape((2, rows, lanes)),
        ),
        in_specs=[SMEM] + [HBM] * 6,
        out_specs=(VMEM,) * 8,
        scratch_shapes=[
            held,
            held,
            pltpu.SMEM(wavelet.shape, F32),
            pltpu.VMEM(cells.shape, jnp.int32),
            pltpu.SemaphoreType.DMA((2 * half + 6,)),
        ],
        compiler_params=room(4),
        cost_estimate=pl.CostEstimate(
            flops=20 * half * rows * lanes, bytes_accessed=32 * half * rows * lanes, transcendentals=0
        ),
        name="setup",
    )(source_cell, *in_place(wavelet, cells, observed, p_prev, velocity, density))


def local_kernel(step, pulses, mask, cur, prev, cour, surf_in, base, surf, pad):
    planes, rows, lanes = prev.shape
    lane = lax.broadcasted_iota(jnp.int32, (rows, lanes), 1)
    weights = {}
    for d in range(1, REACH + 1):
        weights[d] = jnp.where(lane >= d, STENCIL[d], 0.0)
        weights[-d] = jnp.where(lane < lanes - d, STENCIL[d], 0.0)
    pulse = pulses[step : step + 1, :]
    for j in range(planes):
        pad[j, 0:8, :] = jnp.zeros((8, lanes), F32)
        pad[j, 8 + rows : 16 + rows, :] = jnp.zeros((8, lanes), F32)
        pad[j, 8 : 8 + rows, :] = cur[j]
    for j in range(planes):
        c = cur[j]
        acc = 3.0 * STENCIL[0] * c
        for d in range(1, REACH + 1):
            acc = acc + weights[d] * pltpu.roll(c, d, 1) + weights[-d] * pltpu.roll(c, lanes - d, 1)
            near = pad[j, 8 + d : 8 + d + rows, :] + pad[j, 8 - d : 8 - d + rows, :]
            for i in (j - d, j + d):
                if 0 <= i < planes:
                    near = near + cur[i]
            acc = acc + STENCIL[d] * near
        base[j] = 2.0 * c - prev[j] + cour[j] * acc + pulse * mask[j]
        if step == 0:
            surf[j] = jnp.zeros((rows, lanes), F32)
        else:
            surf[j] = jnp.where(
                lane == step - 1, jnp.broadcast_to(c[:, 0:1], (rows, lanes)), surf_in[j]
            )


def local_step(step, pulses, mask, cur, prev, cour, surf):
    planes, rows, lanes = cur.shape
    return pl.pallas_call(
        functools.partial(local_kernel, step),
        out_shape=(shape(cur.shape), shape(cur.shape)),
        in_specs=[VMEM] * 6,
        out_specs=(VMEM, VMEM),
        scratch_shapes=[pltpu.VMEM((planes, rows + 16, lanes), F32)],
        compiler_params=room(2),
        cost_estimate=pl.CostEstimate(
            flops=60 * cur.size, bytes_accessed=24 * cur.size, transcendentals=0
        ),
        name="wave_local",
    )(pulses, mask, cur, prev, cour, surf)


def halo_kernel(base, cour, cour_outer, outer, inner, out):
    planes = base.shape[0]
    for j in range(planes):
        far = near = None
        for d in range(j + 1, REACH + 1):
            term = STENCIL[d] * outer[d - j - 1]
            far = term if far is None else far + term
        for d in range(planes - j, REACH + 1):
            term = STENCIL[d] * inner[2 * planes - 1 - j - d]
            near = term if near is None else near + term
        out[j] = base[j] + (cour[j] * near + cour_outer[j] * far)


def halo_step(base, cour, cour_outer, outer, inner):
    return pl.pallas_call(
        halo_kernel,
        out_shape=shape(base.shape),
        in_specs=[VMEM] * 5,
        out_specs=VMEM,
        compiler_params=room(2),
        cost_estimate=pl.CostEstimate(
            flops=12 * base.size, bytes_accessed=20 * base.size, transcendentals=0
        ),
        name="wave_halo",
    )(base, cour, cour_outer, outer, inner)


def trace_kernel(step, place, cur, surf, out):
    planes, rows, lanes = cur.shape
    receivers = place.shape[1]
    steps = step + 1
    lane = lax.broadcasted_iota(jnp.int32, (rows, lanes), 1)
    columns = jnp.concatenate(
        [
            jnp.where(lane == step, jnp.broadcast_to(cur[j, :, 0:1], (rows, lanes)), surf[j])
            for j in range(planes)
        ],
        0,
    )
    columns = columns.T
    spot = lax.broadcasted_iota(jnp.int32, (planes * rows, receivers), 0)
    pick = jnp.where(place[...] == spot, 1.0, 0.0).astype(jnp.bfloat16)
    total = None
    for _ in range(3):
        part = columns.astype(jnp.bfloat16)
        columns = columns - part.astype(F32)
        term = jnp.dot(part, pick, preferred_element_type=F32)
        total = term if total is None else total + term
    for b in range(receivers // 128):
        out[b * steps : (b + 1) * steps, :] = total[:steps, b * 128 : (b + 1) * 128]


def recorded_traces(step, place, cur, surf):
    return pl.pallas_call(
        functools.partial(trace_kernel, step),
        out_shape=shape(((step + 1) * (place.shape[1] // 128), 128)),
        in_specs=[VMEM] * 3,
        out_specs=VMEM,
        compiler_params=room(4),
        name="traces",
    )(place, cur, surf)


def join_kernel(own, sibling, out, sems):
    slab = out.shape[0]
    _, upper = position()
    pairs = []
    for j in range(slab // 2):
        here = plane_of(upper, j, slab)
        pairs += [(own.at[j], out.at[here]), (sibling.at[j], out.at[slab - 1 - here])]
    run_copies(pairs, sems)


def join(own, sibling):
    half, rows, lanes = own.shape
    return pl.pallas_call(
        join_kernel,
        out_shape=shape((2 * half, rows, lanes)),
        in_specs=[VMEM] * 2,
        out_specs=HBM,
        scratch_shapes=[pltpu.SemaphoreType.DMA((2 * half,))],
        compiler_params=room(2),
        name="join",
    )(own, sibling)


def on_chip(value):
    return pltpu.with_memory_space_constraint(value, pltpu.VMEM)


def table_low(total_x, slab, offset):
    m, _ = position()
    return m * slab - (total_x - 1) + offset


def table_kernel(total_x, slab, spread, head, out):
    lanes = out.shape[1]
    low = table_low(total_x, slab, head[0])
    dy = (lax.broadcasted_iota(jnp.int32, (spread, lanes), 0) - (spread // 2 - 1)).astype(F32)
    dz = (lax.broadcasted_iota(jnp.int32, (spread, lanes), 1) + 1).astype(F32)
    side = dy * dy
    deep = dz * dz

    def one(t, carry):
        dx = (t + low).astype(F32)
        inverse = lax.rsqrt(dx * dx + side + deep)
        value = dz * (inverse * inverse * inverse)
        start = pl.multiple_of(t * spread, spread)
        out[pl.ds(start, spread), :] = value.astype(jnp.bfloat16).astype(F32)
        return carry

    lax.fori_loop(0, out.shape[0] // spread, one, 0)


def gravity_table(total_x, slab, depth, lateral, vertical, head):
    size = depth * 2 * lateral * vertical
    return pl.pallas_call(
        functools.partial(table_kernel, total_x, slab, 2 * lateral),
        out_shape=shape((depth * 2 * lateral, vertical)),
        in_specs=[SMEM],
        out_specs=VMEM,
        cost_estimate=pl.CostEstimate(
            flops=20 * size, bytes_accessed=4 * size, transcendentals=2 * size
        ),
        compiler_params=room(8),
        name="gravity_table",
    )(head)


def forward_kernel(first, guard, total_x, lateral, head, table, dens, out):
    planes, rows, _ = dens.shape
    count = out.shape[0]
    spread = 2 * lateral
    core = lax.axis_index("station") % 2
    lead = total_x - 1 - head[0]
    if guard:
        out[...] = jnp.zeros_like(out)

    def one(s, carry):
        sx, sy = divmod_static(head[1 + first + s], lateral)
        shift = lead - sx
        start = (shift + core * planes) * spread + (lateral - 1 - sy)

        def accumulate():
            acc = None
            for p in range(planes):
                term = table[pl.ds(start + p * spread, rows), :] * dens[p]
                acc = term if acc is None else acc + term
            out[pl.ds(s, 1), :] = jnp.sum(acc, axis=0, keepdims=True)

        if guard:
            pl.when((shift >= 0) & (shift < guard))(accumulate)
        else:
            accumulate()
        return carry

    lax.fori_loop(0, count, one, 0, unroll=8)


def gravity_forward(first, count, guard, total_x, lateral, head, table, dens):
    work = count * dens.size
    return pl.pallas_call(
        functools.partial(forward_kernel, first, guard, total_x, lateral),
        out_shape=shape((count, dens.shape[2])),
        in_specs=[SMEM, VMEM, VMEM],
        out_specs=VMEM,
        cost_estimate=pl.CostEstimate(
            flops=4 * work, bytes_accessed=4 * dens.size, transcendentals=0
        ),
        compiler_params=room(8),
        name="gravity_forward",
    )(head, on_chip(table), dens)


def adjoint_kernel(lines, guard, total_x, lateral, head, weights, table, start_at, out):
    slab, rows, _ = out.shape
    spread = 2 * lateral
    lead = total_x - 1 - head[0]
    row_low = lax.axis_index("station") * rows

    def one(k, i, acc):
        sx, sy = divmod_static(head[1 + 128 * k + i], lateral)
        shift = lead - sx
        weight = weights[k, i]
        if guard:
            keep = (shift >= 0) & (shift < guard)
            shift = jnp.where(keep, shift, 0)
            weight = jnp.where(keep, weight, 0.0)
        start = shift * spread + (lateral - 1 - sy + row_low)
        return tuple(
            acc[x] + weight * table[pl.ds(start + x * spread, rows), :] for x in range(slab)
        )

    acc = tuple(start_at[x] for x in range(slab))
    for k in lines:
        acc = lax.fori_loop(0, 128, functools.partial(one, k), acc, unroll=16)
    for x in range(slab):
        out[x] = acc[x]


def gravity_adjoint(lines, guard, total_x, lateral, head, weights, table, start_at):
    return pl.pallas_call(
        functools.partial(adjoint_kernel, lines, guard, total_x, lateral),
        out_shape=shape(start_at.shape),
        in_specs=[SMEM, SMEM, VMEM, VMEM],
        out_specs=VMEM,
        cost_estimate=pl.CostEstimate(
            flops=256 * len(lines) * start_at.size, bytes_accessed=8 * start_at.size, transcendentals=0
        ),
        compiler_params=room(8),
        name="gravity_adjoint",
    )(head, weights, table, start_at)


def small_call(kernel, outs, *values):
    single = not isinstance(outs, tuple)
    return pl.pallas_call(
        kernel,
        out_shape=outs,
        in_specs=[VMEM] * len(values),
        out_specs=VMEM if single else (VMEM,) * len(outs),
        compiler_params=room(2),
    )(*values)


def sum_kernel(first, second, out):
    out[...] = first[...] + second[...]


def plus(first, second):
    return small_call(sum_kernel, shape(first.shape), first, second)


def unpack_kernel(packed, other, out):
    steps, receivers = out.shape
    for b in range(receivers // 128):
        rows = slice(b * steps, (b + 1) * steps)
        out[:, b * 128 : (b + 1) * 128] = packed[rows, :] + other[rows, :]


def predict_kernel(*refs):
    pieces, out = refs[:-1], refs[-1]
    sums = jnp.concatenate([piece[...] for piece in pieces], 0)
    for k in range(out.shape[0]):
        out[k : k + 1, :] = jnp.sum(sums[k * 128 : (k + 1) * 128, :].T, axis=0, keepdims=True)


def residual_kernel(packed, other, observed, weights, own):
    residual = packed[...] + other[...] - observed[...]
    weights[...] = residual.astype(jnp.bfloat16).astype(F32)
    mine = own.shape[0]
    for k in range(residual.shape[0] // mine):

        @pl.when(lax.axis_index("station") == k)
        def _(k=k):
            own[...] = residual[k * mine : (k + 1) * mine, :]


def cross_kernel(count, velocity, density, outer, inner, out):
    slab, rows, lanes = velocity.shape
    lane = lax.broadcasted_iota(jnp.int32, (rows, lanes), 1)
    row = lax.broadcasted_iota(jnp.int32, (rows, lanes), 0)
    m, flipped = position()
    left_ok = jnp.where(m > 0, 0.5, 0.0)
    right_ok = jnp.where(m < count - 1, 0.5, 0.0)

    def slopes(field, side, x):
        f = field[x]
        if x > 0:
            below = 0.5 * field[x - 1]
        else:
            below = left_ok * jnp.where(flipped, inner[side], outer[side])
        if x < slab - 1:
            above = 0.5 * field[x + 1]
        else:
            above = right_ok * jnp.where(flipped, outer[side], inner[side])
        up = jnp.where(row < rows - 1, pltpu.roll(f, rows - 1, 0), 0.0)
        down = jnp.where(row > 0, pltpu.roll(f, 1, 0), 0.0)
        ahead = jnp.where(lane < lanes - 1, pltpu.roll(f, lanes - 1, 1), 0.0)
        back = jnp.where(lane > 0, pltpu.roll(f, 1, 1), 0.0)
        return above - below, (up - down) * 0.5, (ahead - back) * 0.5

    for x in range(slab):
        v = slopes(velocity, 0, x)
        q = slopes(density, 1, x)
        out[0, x] = v[1] * q[2] - v[2] * q[1]
        out[1, x] = v[2] * q[0] - v[0] * q[2]
        out[2, x] = v[0] * q[1] - v[1] * q[0]


def cross_gradient_of(count, velocity, density, outer, inner):
    return pl.pallas_call(
        functools.partial(cross_kernel, count),
        out_shape=shape((3,) + velocity.shape),
        in_specs=[VMEM] * 4,
        out_specs=VMEM,
        cost_estimate=pl.CostEstimate(
            flops=60 * velocity.size, bytes_accessed=24 * velocity.size, transcendentals=0
        ),
        compiler_params=room(8),
        name="cross_gradient",
    )(velocity, density, outer, inner)


def per_device(
    p_now, p_prev, velocity, density, wavelet, source_cell, receiver_cells, station_cells, observed
):
    slab, lateral, vertical = p_now.shape
    count = lax.axis_size("mp")
    stations = lax.axis_size("station")
    steps = wavelet.shape[0]
    half = slab // 2
    assert half == REACH and count % 2 == 0 and stations % 4 == 0
    total_x = slab * count
    m, upper = position()
    s = lax.axis_index("station")
    block = lateral // stations
    chain = pairs_of(count, stations, chain_partner(count))
    together = lax.optimization_barrier

    def across(value):
        return lax.ppermute(value, AXES, chain)

    def swap(value, slab_bit, station_bit):
        pairs = pairs_of(count, stations, lambda i, k: (i ^ slab_bit, k ^ station_bit))
        return lax.ppermute(value, AXES, pairs)

    cur = first_planes(p_now)
    outer = across(cur)
    inner = swap(cur, 0, 1)
    prev, cour, cour_outer, mask, dens, pulses, known, edges = setup(
        count,
        source_cell,
        wavelet,
        station_cells.reshape(-1, 128),
        observed.reshape(-1, 128),
        p_prev,
        velocity,
        density,
    )

    receiver_x, receiver_y = divmod_static(receiver_cells, lateral)
    receiver_j = receiver_x - m * slab
    receiver_j = jnp.where(upper, slab - 1 - receiver_j, receiver_j)
    inside = (receiver_j >= 0) & (receiver_j < half)
    place = jnp.where(inside, receiver_j * lateral + receiver_y, -1)[None, :]

    reach = min(total_x, 64)
    chunks = -(-total_x // reach)
    span = reach + slab - 1
    own_stations = station_cells.shape[0]
    n_stations = own_stations * stations

    def head_of(offset, cells):
        return jnp.concatenate([jnp.reshape(offset, (1,)).astype(jnp.int32), cells])

    def table_of(head):
        return gravity_table(total_x, slab, span, lateral, vertical, head)

    state = {"known": known, "edges": edges}

    def merged(gate):
        if "pending" not in state:
            return gate(state["known"])
        known, other, bit = state.pop("pending")
        other = gate(other)
        upper = (s // bit) % 2 == 1
        pair = [jnp.where(upper, other, known), jnp.where(upper, known, other)]
        state["known"] = jnp.concatenate(pair, 1)
        return state["known"]

    def exchange(bit):
        def work(gate):
            known = merged(gate)
            state["pending"] = known, swap(known, 0, bit), bit

        return work

    def send_edges(gate):
        state["outer"] = across(gate(state["edges"]))

    def share_edges(gate):
        state["inner"] = swap(gate(state["outer"]), 0, 1)

    def cross(gate):
        state["cross"] = cross_gradient_of(
            count, velocity, density, state["outer"], gate(state["inner"])
        )
        return "cross"

    lines = n_stations // 128

    def build_table(gate):
        known = merged(gate)
        cells = known[0].reshape(-1).astype(jnp.int32)
        head = head_of(0, cells)
        zero, head, observed_all, where = together(
            (jnp.zeros((1,), jnp.int32), head, known[1].reshape(-1, 128), place)
        )
        state.update(head=head, observed=observed_all, place=where)
        state["table"] = table_of(zero)
        return "table"

    pieces = 5
    part = -(-n_stations // (8 * pieces)) * 8

    def forward(i):
        def work(gate):
            size = min(part, n_stations - i * part)
            state[i] = gravity_forward(
                i * part, size, 0, total_x, lateral, gate(state["head"]), state["table"], dens
            )
            return i

        return work

    def predict(gate):
        sums = [state[i] for i in range(pieces)]
        sums[0] = gate(sums[0])
        packed = small_call(predict_kernel, shape((lines, 128)), *sums)
        state["packed"], state["other"] = packed, swap(packed, 0, 1)

    def add_up(bit):
        def work(gate):
            packed = plus(gate(state["packed"]), state["other"])
            state["packed"], state["other"] = packed, swap(packed, bit, 1)

        return work

    def residual(gate):
        state["weights"], state["own"] = small_call(
            residual_kernel,
            (shape((lines, 128)), shape((lines // stations, 128))),
            gate(state["packed"]),
            state["other"],
            state["observed"],
        )
        state["gradient"] = jnp.zeros((slab, block, vertical), F32)
        return "weights"

    def adjoint(half_lines):
        def work(gate):
            state["gradient"] = gravity_adjoint(
                half_lines,
                0,
                total_x,
                lateral,
                state["head"],
                gate(state["weights"]),
                state["table"],
                state["gradient"],
            )
            return "gradient"

        return work

    def both(first, second):
        def work(gate):
            first(gate)
            return second(gate)

        return work

    hidden = chunks == 1 and count & (count - 1) == 0
    jobs = [exchange(1 << b) for b in range(stations.bit_length() - 1)]
    if hidden:
        jobs += [build_table] + [forward(i) for i in range(pieces)] + [both(predict, cross)]
        jobs += [add_up(1 << b) for b in range(count.bit_length() - 1)] + [residual]
        jobs += [adjoint(range(lines // 2)), adjoint(range(lines // 2, lines))]
    jobs[0] = both(send_edges, jobs[0])
    jobs[1] = both(share_edges, jobs[1])
    if not hidden:
        jobs.append(cross)
    assert len(jobs) < steps

    surf = cour
    for step in range(steps):
        if step:
            outer = across(cur)
            inner = swap(cur, 0, 1)
        base, surf = local_step(step, pulses, mask, cur, prev, cour, surf)

        def gate(value):
            nonlocal base
            base, value = together((base, value))
            return value

        ready = None
        if step and jobs:
            ready = jobs.pop(0)(gate)
        cur, prev = halo_step(base, cour, cour_outer, outer, inner), cur
        if ready is not None:
            cur, state[ready] = together((cur, state[ready]))

    sibling = swap(cur, 0, 1)
    packed = recorded_traces(steps - 1, state.get("place", place), cur, surf)
    other = swap(packed, 0, 1)
    if count & (count - 1) == 0:
        bit = 1
        while bit < count:
            packed = plus(packed, other)
            other = swap(packed, bit, 1)
            if bit == 1:
                wavefield = join(cur, sibling)
            if bit == 2:
                other, wavefield = together((other, wavefield))
            bit *= 2
    else:
        wavefield = join(cur, sibling)
        packed = lax.psum(packed + other, "mp")
        other = jnp.zeros_like(packed)
    traces = small_call(unpack_kernel, shape((steps, receiver_cells.shape[0])), packed, other)
    if hidden:
        gravity_residual = state["own"].reshape(-1)
        density_gradient = state["gradient"]
    else:
        known = merged(lambda value: value)
        cells = known[0].reshape(-1).astype(jnp.int32)

        def add_chunk(i, total):
            head = head_of(i * reach, cells)
            return total + gravity_forward(
                0, n_stations, reach, total_x, lateral, head, table_of(head[:1]), dens
            )

        sums = lax.fori_loop(0, chunks, add_chunk, jnp.zeros((n_stations, vertical), F32))
        predicted = jnp.sum(sums, axis=1)
        predicted = lax.psum(predicted + swap(predicted, 0, 1), "mp")
        difference = predicted - known[1].reshape(-1)
        gravity_residual = lax.dynamic_slice(difference, (s * own_stations,), (own_stations,))
        weights = difference.astype(jnp.bfloat16).astype(F32).reshape(-1, 128)

        def back_chunk(i, total):
            head = head_of(i * reach, cells)
            return gravity_adjoint(
                range(lines), reach, total_x, lateral, head, weights, table_of(head[:1]), total
            )

        density_gradient = lax.fori_loop(
            0, chunks, back_chunk, jnp.zeros((slab, block, vertical), F32)
        )
    return (wavefield, traces, gravity_residual, density_gradient, state["cross"])


def solution(mesh):
    in_specs = (
        P("mp", None, None),
        P("mp", None, None),
        P("mp", None, None),
        P("mp", None, None),
        P(),
        P(),
        P(),
        P("station"),
        P("station"),
    )
    out_specs = (
        P("mp", None, None),
        P(),
        P("station"),
        P("mp", "station", None),
        P(None, "mp", None, None),
    )

    return jax.shard_map(
        per_device, mesh=mesh, in_specs=in_specs, out_specs=out_specs, check_vma=False
    )
```

```python
import functools

import jax
import jax.numpy as jnp
from jax import lax
from jax.experimental import pallas as pl
from jax.experimental.pallas import tpu as pltpu
from jax.sharding import PartitionSpec as P


STENCIL = (-205.0 / 72.0, 8.0 / 5.0, -1.0 / 5.0, 8.0 / 315.0, -1.0 / 560.0)
TIME_RATIO = 0.1
REACH = 4
AXES = ("mp", "station")
VMEM = pl.BlockSpec(memory_space=pltpu.VMEM)
SMEM = pl.BlockSpec(memory_space=pltpu.SMEM)
HBM = pl.BlockSpec(memory_space=pltpu.HBM)
F32 = jnp.float32
MIB = 1 << 20


def room(mib):
    return pltpu.CompilerParams(vmem_limit_bytes=mib * MIB)


def shape(dims):
    return jax.ShapeDtypeStruct(dims, F32)


def pairs_of(count, stations, partner):
    return [
        (m * stations + s, (lambda t: t[0] * stations + t[1])(partner(m, s)))
        for m in range(count)
        for s in range(stations)
    ]


def chain_partner(count):
    def partner(m, s):
        if s % 2 == 0:
            return (m ^ 1, s)
        other = m + 1 if m % 2 else m - 1
        if other < 0 or other >= count:
            return (m, s ^ 2)
        return (other, s)

    return partner


def position():
    m = lax.axis_index("mp")
    return m, (m + lax.axis_index("station")) % 2 == 0


def divmod_static(value, divisor):
    if divisor & (divisor - 1) == 0:
        return value >> (divisor.bit_length() - 1), value & (divisor - 1)
    return value // divisor, value % divisor


def in_place(*values):
    return [pltpu.with_memory_space_constraint(value, pltpu.HBM) for value in values]


def run_copies(pairs, sems):
    copies = [pltpu.make_async_copy(a, b, sems.at[i]) for i, (a, b) in enumerate(pairs)]
    for copy in copies:
        copy.start()
    for copy in copies:
        copy.wait()


def plane_of(upper, j, slab):
    return jnp.where(upper, slab - 1 - j, j)


def first_kernel(now, cur, sems):
    slab = now.shape[0]
    _, upper = position()
    run_copies([(now.at[plane_of(upper, j, slab)], cur.at[j]) for j in range(slab // 2)], sems)


def first_planes(p_now):
    slab, rows, lanes = p_now.shape
    half = slab // 2
    return pl.pallas_call(
        first_kernel,
        out_shape=shape((half, rows, lanes)),
        in_specs=[HBM],
        out_specs=VMEM,
        scratch_shapes=[pltpu.SemaphoreType.DMA((half,))],
        compiler_params=room(2),
        name="first_planes",
    )(*in_place(p_now))


def setup_kernel(
    count,
    source,
    wavelet_in,
    cells_in,
    observed,
    p_prev,
    velocity,
    density,
    prev,
    cour,
    cour_outer,
    mask,
    dens,
    pulses,
    known,
    edges,
    vel,
    raw,
    wavelet,
    cells,
    sems,
):
    slab = p_prev.shape[0]
    half, rows, lanes = prev.shape
    m, upper = position()
    pairs = []
    for j in range(half):
        plane = plane_of(upper, j, slab)
        pairs += [(p_prev.at[plane], prev.at[j]), (velocity.at[plane], vel.at[j])]
    low = half * (lax.axis_index("station") % 2)
    pairs += [(density.at[pl.ds(low, half)], raw)]
    edge = plane_of(upper, 0, slab)
    pairs += [(velocity.at[edge], edges.at[0]), (density.at[edge], edges.at[1])]
    pairs += [(wavelet_in, wavelet), (cells_in, cells), (observed, known.at[1])]
    run_copies(pairs, sems)
    known[0] = cells[...].astype(F32)
    for n in range(pulses.shape[0]):
        pulses[n : n + 1, :] = jnp.full((1, lanes), wavelet[n], F32)
    outer_ok = jnp.where(upper, m < count - 1, m > 0)
    outer_ok = jnp.where(outer_ok, 1.0, 0.0)
    column, source_lane = divmod_static(source[0], lanes)
    source_x, source_row = divmod_static(column, rows)
    row = lax.broadcasted_iota(jnp.int32, (rows, lanes), 0)
    lane = lax.broadcasted_iota(jnp.int32, (rows, lanes), 1)
    spot = jnp.where((row == source_row) & (lane == source_lane), 1.0, 0.0)
    for j in range(half):
        scaled = TIME_RATIO * vel[j]
        square = scaled * scaled
        cour[j] = square
        cour_outer[j] = square * outer_ok
        here = m * slab + plane_of(upper, j, slab) == source_x
        mask[j] = spot * jnp.where(here, 1.0, 0.0)
        dens[j] = raw[j].astype(jnp.bfloat16).astype(F32)


def setup(count, source_cell, wavelet, cells, observed, p_prev, velocity, density):
    slab, rows, lanes = p_prev.shape
    half = slab // 2
    part = shape((half, rows, lanes))
    held = pltpu.VMEM((half, rows, lanes), F32)
    return pl.pallas_call(
        functools.partial(setup_kernel, count),
        out_shape=(part,) * 5
        + (
            shape((wavelet.shape[0], lanes)),
            shape((2,) + cells.shape),
            shape((2, rows, lanes)),
        ),
        in_specs=[SMEM] + [HBM] * 6,
        out_specs=(VMEM,) * 8,
        scratch_shapes=[
            held,
            held,
            pltpu.SMEM(wavelet.shape, F32),
            pltpu.VMEM(cells.shape, jnp.int32),
            pltpu.SemaphoreType.DMA((2 * half + 6,)),
        ],
        compiler_params=room(4),
        cost_estimate=pl.CostEstimate(
            flops=20 * half * rows * lanes, bytes_accessed=32 * half * rows * lanes, transcendentals=0
        ),
        name="setup",
    )(source_cell, *in_place(wavelet, cells, observed, p_prev, velocity, density))


def local_kernel(step, pulses, mask, cur, prev, cour, surf_in, base, surf, pad):
    planes, rows, lanes = prev.shape
    lane = lax.broadcasted_iota(jnp.int32, (rows, lanes), 1)
    weights = {}
    for d in range(1, REACH + 1):
        weights[d] = jnp.where(lane >= d, STENCIL[d], 0.0)
        weights[-d] = jnp.where(lane < lanes - d, STENCIL[d], 0.0)
    pulse = pulses[step : step + 1, :]
    for j in range(planes):
        pad[j, 0:8, :] = jnp.zeros((8, lanes), F32)
        pad[j, 8 + rows : 16 + rows, :] = jnp.zeros((8, lanes), F32)
        pad[j, 8 : 8 + rows, :] = cur[j]
    for j in range(planes):
        c = cur[j]
        acc = 3.0 * STENCIL[0] * c
        for d in range(1, REACH + 1):
            acc = acc + weights[d] * pltpu.roll(c, d, 1) + weights[-d] * pltpu.roll(c, lanes - d, 1)
            near = pad[j, 8 + d : 8 + d + rows, :] + pad[j, 8 - d : 8 - d + rows, :]
            for i in (j - d, j + d):
                if 0 <= i < planes:
                    near = near + cur[i]
            acc = acc + STENCIL[d] * near
        base[j] = 2.0 * c - prev[j] + cour[j] * acc + pulse * mask[j]
        if step == 0:
            surf[j] = jnp.zeros((rows, lanes), F32)
        else:
            surf[j] = jnp.where(
                lane == step - 1, jnp.broadcast_to(c[:, 0:1], (rows, lanes)), surf_in[j]
            )


def local_step(step, pulses, mask, cur, prev, cour, surf):
    planes, rows, lanes = cur.shape
    return pl.pallas_call(
        functools.partial(local_kernel, step),
        out_shape=(shape(cur.shape), shape(cur.shape)),
        in_specs=[VMEM] * 6,
        out_specs=(VMEM, VMEM),
        scratch_shapes=[pltpu.VMEM((planes, rows + 16, lanes), F32)],
        compiler_params=room(2),
        cost_estimate=pl.CostEstimate(
            flops=60 * cur.size, bytes_accessed=24 * cur.size, transcendentals=0
        ),
        name="wave_local",
    )(pulses, mask, cur, prev, cour, surf)


def halo_kernel(base, cour, cour_outer, outer, inner, out):
    planes = base.shape[0]
    for j in range(planes):
        far = near = None
        for d in range(j + 1, REACH + 1):
            term = STENCIL[d] * outer[d - j - 1]
            far = term if far is None else far + term
        for d in range(planes - j, REACH + 1):
            term = STENCIL[d] * inner[2 * planes - 1 - j - d]
            near = term if near is None else near + term
        out[j] = base[j] + (cour[j] * near + cour_outer[j] * far)


def halo_step(base, cour, cour_outer, outer, inner):
    return pl.pallas_call(
        halo_kernel,
        out_shape=shape(base.shape),
        in_specs=[VMEM] * 5,
        out_specs=VMEM,
        compiler_params=room(2),
        cost_estimate=pl.CostEstimate(
            flops=12 * base.size, bytes_accessed=20 * base.size, transcendentals=0
        ),
        name="wave_halo",
    )(base, cour, cour_outer, outer, inner)


def trace_kernel(step, place, cur, surf, out):
    planes, rows, lanes = cur.shape
    receivers = place.shape[1]
    steps = step + 1
    lane = lax.broadcasted_iota(jnp.int32, (rows, lanes), 1)
    columns = jnp.concatenate(
        [
            jnp.where(lane == step, jnp.broadcast_to(cur[j, :, 0:1], (rows, lanes)), surf[j])
            for j in range(planes)
        ],
        0,
    )
    columns = columns.T
    spot = lax.broadcasted_iota(jnp.int32, (planes * rows, receivers), 0)
    pick = jnp.where(place[...] == spot, 1.0, 0.0).astype(jnp.bfloat16)
    total = None
    for _ in range(3):
        part = columns.astype(jnp.bfloat16)
        columns = columns - part.astype(F32)
        term = jnp.dot(part, pick, preferred_element_type=F32)
        total = term if total is None else total + term
    for b in range(receivers // 128):
        out[b * steps : (b + 1) * steps, :] = total[:steps, b * 128 : (b + 1) * 128]


def recorded_traces(step, place, cur, surf):
    return pl.pallas_call(
        functools.partial(trace_kernel, step),
        out_shape=shape(((step + 1) * (place.shape[1] // 128), 128)),
        in_specs=[VMEM] * 3,
        out_specs=VMEM,
        compiler_params=room(4),
        name="traces",
    )(place, cur, surf)


def join_kernel(own, sibling, out, sems):
    slab = out.shape[0]
    _, upper = position()
    pairs = []
    for j in range(slab // 2):
        here = plane_of(upper, j, slab)
        pairs += [(own.at[j], out.at[here]), (sibling.at[j], out.at[slab - 1 - here])]
    run_copies(pairs, sems)


def join(own, sibling):
    half, rows, lanes = own.shape
    return pl.pallas_call(
        join_kernel,
        out_shape=shape((2 * half, rows, lanes)),
        in_specs=[VMEM] * 2,
        out_specs=HBM,
        scratch_shapes=[pltpu.SemaphoreType.DMA((2 * half,))],
        compiler_params=room(2),
        name="join",
    )(own, sibling)


def on_chip(value):
    return pltpu.with_memory_space_constraint(value, pltpu.VMEM)


def table_low(total_x, slab, offset):
    m, _ = position()
    return m * slab - (total_x - 1) + offset


def table_kernel(total_x, slab, spread, head, out):
    lanes = out.shape[1]
    low = table_low(total_x, slab, head[0])
    dy = (lax.broadcasted_iota(jnp.int32, (spread, lanes), 0) - (spread // 2 - 1)).astype(F32)
    dz = (lax.broadcasted_iota(jnp.int32, (spread, lanes), 1) + 1).astype(F32)
    side = dy * dy
    deep = dz * dz

    def one(t, carry):
        dx = (t + low).astype(F32)
        inverse = lax.rsqrt(dx * dx + side + deep)
        value = dz * (inverse * inverse * inverse)
        start = pl.multiple_of(t * spread, spread)
        out[pl.ds(start, spread), :] = value.astype(jnp.bfloat16).astype(F32)
        return carry

    lax.fori_loop(0, out.shape[0] // spread, one, 0)


def gravity_table(total_x, slab, depth, lateral, vertical, head):
    size = depth * 2 * lateral * vertical
    return pl.pallas_call(
        functools.partial(table_kernel, total_x, slab, 2 * lateral),
        out_shape=shape((depth * 2 * lateral, vertical)),
        in_specs=[SMEM],
        out_specs=VMEM,
        cost_estimate=pl.CostEstimate(
            flops=20 * size, bytes_accessed=4 * size, transcendentals=2 * size
        ),
        compiler_params=room(8),
        name="gravity_table",
    )(head)


def forward_kernel(first, guard, total_x, lateral, head, table, dens, out):
    planes, rows, _ = dens.shape
    count = out.shape[0]
    spread = 2 * lateral
    core = lax.axis_index("station") % 2
    lead = total_x - 1 - head[0]
    if guard:
        out[...] = jnp.zeros_like(out)

    def one(s, carry):
        sx, sy = divmod_static(head[1 + first + s], lateral)
        shift = lead - sx
        start = (shift + core * planes) * spread + (lateral - 1 - sy)

        def accumulate():
            acc = None
            for p in range(planes):
                term = table[pl.ds(start + p * spread, rows), :] * dens[p]
                acc = term if acc is None else acc + term
            out[pl.ds(s, 1), :] = jnp.sum(acc, axis=0, keepdims=True)

        if guard:
            pl.when((shift >= 0) & (shift < guard))(accumulate)
        else:
            accumulate()
        return carry

    lax.fori_loop(0, count, one, 0, unroll=8)


def gravity_forward(first, count, guard, total_x, lateral, head, table, dens):
    work = count * dens.size
    return pl.pallas_call(
        functools.partial(forward_kernel, first, guard, total_x, lateral),
        out_shape=shape((count, dens.shape[2])),
        in_specs=[SMEM, VMEM, VMEM],
        out_specs=VMEM,
        cost_estimate=pl.CostEstimate(
            flops=4 * work, bytes_accessed=4 * dens.size, transcendentals=0
        ),
        compiler_params=room(8),
        name="gravity_forward",
    )(head, on_chip(table), dens)


def adjoint_kernel(lines, guard, total_x, lateral, head, weights, table, start_at, out):
    slab, rows, _ = out.shape
    spread = 2 * lateral
    lead = total_x - 1 - head[0]
    row_low = lax.axis_index("station") * rows

    def one(k, i, acc):
        sx, sy = divmod_static(head[1 + 128 * k + i], lateral)
        shift = lead - sx
        weight = weights[k, i]
        if guard:
            keep = (shift >= 0) & (shift < guard)
            shift = jnp.where(keep, shift, 0)
            weight = jnp.where(keep, weight, 0.0)
        start = shift * spread + (lateral - 1 - sy + row_low)
        return tuple(
            acc[x] + weight * table[pl.ds(start + x * spread, rows), :] for x in range(slab)
        )

    acc = tuple(start_at[x] for x in range(slab))
    for k in lines:
        acc = lax.fori_loop(0, 128, functools.partial(one, k), acc, unroll=16)
    for x in range(slab):
        out[x] = acc[x]


def gravity_adjoint(lines, guard, total_x, lateral, head, weights, table, start_at):
    return pl.pallas_call(
        functools.partial(adjoint_kernel, lines, guard, total_x, lateral),
        out_shape=shape(start_at.shape),
        in_specs=[SMEM, SMEM, VMEM, VMEM],
        out_specs=VMEM,
        cost_estimate=pl.CostEstimate(
            flops=256 * len(lines) * start_at.size, bytes_accessed=8 * start_at.size, transcendentals=0
        ),
        compiler_params=room(8),
        name="gravity_adjoint",
    )(head, weights, table, start_at)


def small_call(kernel, outs, *values):
    single = not isinstance(outs, tuple)
    return pl.pallas_call(
        kernel,
        out_shape=outs,
        in_specs=[VMEM] * len(values),
        out_specs=VMEM if single else (VMEM,) * len(outs),
        compiler_params=room(2),
    )(*values)


def sum_kernel(first, second, out):
    out[...] = first[...] + second[...]


def plus(first, second):
    return small_call(sum_kernel, shape(first.shape), first, second)


def unpack_kernel(packed, other, out):
    steps, receivers = out.shape
    for b in range(receivers // 128):
        rows = slice(b * steps, (b + 1) * steps)
        out[:, b * 128 : (b + 1) * 128] = packed[rows, :] + other[rows, :]


def predict_kernel(*refs):
    pieces, out = refs[:-1], refs[-1]
    sums = jnp.concatenate([piece[...] for piece in pieces], 0)
    for k in range(out.shape[0]):
        out[k : k + 1, :] = jnp.sum(sums[k * 128 : (k + 1) * 128, :].T, axis=0, keepdims=True)


def residual_kernel(packed, other, observed, weights, own):
    residual = packed[...] + other[...] - observed[...]
    weights[...] = residual.astype(jnp.bfloat16).astype(F32)
    mine = own.shape[0]
    for k in range(residual.shape[0] // mine):

        @pl.when(lax.axis_index("station") == k)
        def _(k=k):
            own[...] = residual[k * mine : (k + 1) * mine, :]


def cross_kernel(count, velocity, density, outer, inner, out):
    slab, rows, lanes = velocity.shape
    lane = lax.broadcasted_iota(jnp.int32, (rows, lanes), 1)
    row = lax.broadcasted_iota(jnp.int32, (rows, lanes), 0)
    m, flipped = position()
    left_ok = jnp.where(m > 0, 0.5, 0.0)
    right_ok = jnp.where(m < count - 1, 0.5, 0.0)

    def slopes(field, side, x):
        f = field[x]
        if x > 0:
            below = 0.5 * field[x - 1]
        else:
            below = left_ok * jnp.where(flipped, inner[side], outer[side])
        if x < slab - 1:
            above = 0.5 * field[x + 1]
        else:
            above = right_ok * jnp.where(flipped, outer[side], inner[side])
        up = jnp.where(row < rows - 1, pltpu.roll(f, rows - 1, 0), 0.0)
        down = jnp.where(row > 0, pltpu.roll(f, 1, 0), 0.0)
        ahead = jnp.where(lane < lanes - 1, pltpu.roll(f, lanes - 1, 1), 0.0)
        back = jnp.where(lane > 0, pltpu.roll(f, 1, 1), 0.0)
        return above - below, (up - down) * 0.5, (ahead - back) * 0.5

    for x in range(slab):
        v = slopes(velocity, 0, x)
        q = slopes(density, 1, x)
        out[0, x] = v[1] * q[2] - v[2] * q[1]
        out[1, x] = v[2] * q[0] - v[0] * q[2]
        out[2, x] = v[0] * q[1] - v[1] * q[0]


def cross_gradient_of(count, velocity, density, outer, inner):
    return pl.pallas_call(
        functools.partial(cross_kernel, count),
        out_shape=shape((3,) + velocity.shape),
        in_specs=[VMEM] * 4,
        out_specs=VMEM,
        cost_estimate=pl.CostEstimate(
            flops=60 * velocity.size, bytes_accessed=24 * velocity.size, transcendentals=0
        ),
        compiler_params=room(8),
        name="cross_gradient",
    )(velocity, density, outer, inner)


def per_device(
    p_now, p_prev, velocity, density, wavelet, source_cell, receiver_cells, station_cells, observed
):
    slab, lateral, vertical = p_now.shape
    count = lax.axis_size("mp")
    stations = lax.axis_size("station")
    steps = wavelet.shape[0]
    half = slab // 2
    assert half == REACH and count % 2 == 0 and stations % 4 == 0
    total_x = slab * count
    m, upper = position()
    s = lax.axis_index("station")
    block = lateral // stations
    chain = pairs_of(count, stations, chain_partner(count))
    together = lax.optimization_barrier

    def across(value):
        return lax.ppermute(value, AXES, chain)

    def swap(value, slab_bit, station_bit):
        pairs = pairs_of(count, stations, lambda i, k: (i ^ slab_bit, k ^ station_bit))
        return lax.ppermute(value, AXES, pairs)

    cur = first_planes(p_now)
    outer = across(cur)
    inner = swap(cur, 0, 1)
    prev, cour, cour_outer, mask, dens, pulses, known, edges = setup(
        count,
        source_cell,
        wavelet,
        station_cells.reshape(-1, 128),
        observed.reshape(-1, 128),
        p_prev,
        velocity,
        density,
    )

    receiver_x, receiver_y = divmod_static(receiver_cells, lateral)
    receiver_j = receiver_x - m * slab
    receiver_j = jnp.where(upper, slab - 1 - receiver_j, receiver_j)
    inside = (receiver_j >= 0) & (receiver_j < half)
    place = jnp.where(inside, receiver_j * lateral + receiver_y, -1)[None, :]

    reach = min(total_x, 64)
    chunks = -(-total_x // reach)
    span = reach + slab - 1
    own_stations = station_cells.shape[0]
    n_stations = own_stations * stations

    def head_of(offset, cells):
        return jnp.concatenate([jnp.reshape(offset, (1,)).astype(jnp.int32), cells])

    def table_of(head):
        return gravity_table(total_x, slab, span, lateral, vertical, head)

    state = {"known": known, "edges": edges}

    def merged(gate):
        if "pending" not in state:
            return gate(state["known"])
        known, other, bit = state.pop("pending")
        other = gate(other)
        upper = (s // bit) % 2 == 1
        pair = [jnp.where(upper, other, known), jnp.where(upper, known, other)]
        state["known"] = jnp.concatenate(pair, 1)
        return state["known"]

    def exchange(bit):
        def work(gate):
            known = merged(gate)
            state["pending"] = known, swap(known, 0, bit), bit

        return work

    def send_edges(gate):
        state["outer"] = across(gate(state["edges"]))

    def share_edges(gate):
        state["inner"] = swap(gate(state["outer"]), 0, 1)

    def cross(gate):
        state["cross"] = cross_gradient_of(
            count, velocity, density, state["outer"], gate(state["inner"])
        )
        return "cross"

    lines = n_stations // 128

    def build_table(gate):
        known = merged(gate)
        cells = known[0].reshape(-1).astype(jnp.int32)
        head = head_of(0, cells)
        zero, head, observed_all, where = together(
            (jnp.zeros((1,), jnp.int32), head, known[1].reshape(-1, 128), place)
        )
        state.update(head=head, observed=observed_all, place=where)
        state["table"] = table_of(zero)
        return "table"

    pieces = 5
    part = -(-n_stations // (8 * pieces)) * 8

    def forward(i):
        def work(gate):
            size = min(part, n_stations - i * part)
            state[i] = gravity_forward(
                i * part, size, 0, total_x, lateral, gate(state["head"]), state["table"], dens
            )
            return i

        return work

    def predict(gate):
        sums = [state[i] for i in range(pieces)]
        sums[0] = gate(sums[0])
        packed = small_call(predict_kernel, shape((lines, 128)), *sums)
        state["packed"], state["other"] = packed, swap(packed, 0, 1)

    def add_up(bit):
        def work(gate):
            packed = plus(gate(state["packed"]), state["other"])
            state["packed"], state["other"] = packed, swap(packed, bit, 1)

        return work

    def residual(gate):
        state["weights"], state["own"] = small_call(
            residual_kernel,
            (shape((lines, 128)), shape((lines // stations, 128))),
            gate(state["packed"]),
            state["other"],
            state["observed"],
        )
        state["gradient"] = jnp.zeros((slab, block, vertical), F32)
        return "weights"

    def adjoint(half_lines):
        def work(gate):
            state["gradient"] = gravity_adjoint(
                half_lines,
                0,
                total_x,
                lateral,
                state["head"],
                gate(state["weights"]),
                state["table"],
                state["gradient"],
            )
            return "gradient"

        return work

    def both(first, second):
        def work(gate):
            first(gate)
            return second(gate)

        return work

    hidden = chunks == 1 and count & (count - 1) == 0
    jobs = [exchange(1 << b) for b in range(stations.bit_length() - 1)]
    if hidden:
        jobs += [build_table] + [forward(i) for i in range(pieces)] + [both(predict, cross)]
        jobs += [add_up(1 << b) for b in range(count.bit_length() - 1)]
        quarter = lines // 4
        jobs += [both(residual, adjoint(range(quarter)))]
        jobs += [adjoint(range(quarter, 3 * quarter)), adjoint(range(3 * quarter, lines))]
    jobs[0] = both(send_edges, jobs[0])
    jobs[1] = both(share_edges, jobs[1])
    if not hidden:
        jobs.append(cross)
    assert len(jobs) < steps

    surf = cour
    for step in range(steps):
        if step:
            outer = across(cur)
            inner = swap(cur, 0, 1)
        base, surf = local_step(step, pulses, mask, cur, prev, cour, surf)

        def gate(value):
            nonlocal base
            base, value = together((base, value))
            return value

        ready = None
        if step and jobs:
            ready = jobs.pop(0)(gate)
        cur, prev = halo_step(base, cour, cour_outer, outer, inner), cur
        if ready is not None:
            cur, state[ready] = together((cur, state[ready]))

    sibling = swap(cur, 0, 1)
    packed = recorded_traces(steps - 1, state.get("place", place), cur, surf)
    other = swap(packed, 0, 1)
    if count & (count - 1) == 0:
        bit = 1
        while bit < count:
            packed = plus(packed, other)
            other = swap(packed, bit, 1)
            if bit == 1:
                wavefield = join(cur, sibling)
            if bit == 2:
                other, wavefield = together((other, wavefield))
            bit *= 2
    else:
        wavefield = join(cur, sibling)
        packed = lax.psum(packed + other, "mp")
        other = jnp.zeros_like(packed)
    traces = small_call(unpack_kernel, shape((steps, receiver_cells.shape[0])), packed, other)
    if hidden:
        gravity_residual = state["own"].reshape(-1)
        density_gradient = state["gradient"]
    else:
        known = merged(lambda value: value)
        cells = known[0].reshape(-1).astype(jnp.int32)

        def add_chunk(i, total):
            head = head_of(i * reach, cells)
            return total + gravity_forward(
                0, n_stations, reach, total_x, lateral, head, table_of(head[:1]), dens
            )

        sums = lax.fori_loop(0, chunks, add_chunk, jnp.zeros((n_stations, vertical), F32))
        predicted = jnp.sum(sums, axis=1)
        predicted = lax.psum(predicted + swap(predicted, 0, 1), "mp")
        difference = predicted - known[1].reshape(-1)
        gravity_residual = lax.dynamic_slice(difference, (s * own_stations,), (own_stations,))
        weights = difference.astype(jnp.bfloat16).astype(F32).reshape(-1, 128)

        def back_chunk(i, total):
            head = head_of(i * reach, cells)
            return gravity_adjoint(
                range(lines), reach, total_x, lateral, head, weights, table_of(head[:1]), total
            )

        density_gradient = lax.fori_loop(
            0, chunks, back_chunk, jnp.zeros((slab, block, vertical), F32)
        )
    return (wavefield, traces, gravity_residual, density_gradient, state["cross"])


def solution(mesh):
    in_specs = (
        P("mp", None, None),
        P("mp", None, None),
        P("mp", None, None),
        P("mp", None, None),
        P(),
        P(),
        P(),
        P("station"),
        P("station"),
    )
    out_specs = (
        P("mp", None, None),
        P(),
        P("station"),
        P("mp", "station", None),
        P(None, "mp", None, None),
    )

    return jax.shard_map(
        per_device, mesh=mesh, in_specs=in_specs, out_specs=out_specs, check_vma=False
    )
```

```python
import functools

import jax
import jax.numpy as jnp
from jax import lax
from jax.experimental import pallas as pl
from jax.experimental.pallas import tpu as pltpu
from jax.sharding import PartitionSpec as P


STENCIL = (-205.0 / 72.0, 8.0 / 5.0, -1.0 / 5.0, 8.0 / 315.0, -1.0 / 560.0)
TIME_RATIO = 0.1
REACH = 4
AXES = ("mp", "station")
VMEM = pl.BlockSpec(memory_space=pltpu.VMEM)
SMEM = pl.BlockSpec(memory_space=pltpu.SMEM)
HBM = pl.BlockSpec(memory_space=pltpu.HBM)
F32 = jnp.float32
MIB = 1 << 20


def room(mib):
    return pltpu.CompilerParams(vmem_limit_bytes=mib * MIB)


def shape(dims):
    return jax.ShapeDtypeStruct(dims, F32)


def pairs_of(count, stations, partner):
    return [
        (m * stations + s, (lambda t: t[0] * stations + t[1])(partner(m, s)))
        for m in range(count)
        for s in range(stations)
    ]


def chain_partner(count):
    def partner(m, s):
        if s % 2 == 0:
            return (m ^ 1, s)
        other = m + 1 if m % 2 else m - 1
        if other < 0 or other >= count:
            return (m, s ^ 2)
        return (other, s)

    return partner


def position():
    m = lax.axis_index("mp")
    return m, (m + lax.axis_index("station")) % 2 == 0


def divmod_static(value, divisor):
    if divisor & (divisor - 1) == 0:
        return value >> (divisor.bit_length() - 1), value & (divisor - 1)
    return value // divisor, value % divisor


def in_place(*values):
    return [pltpu.with_memory_space_constraint(value, pltpu.HBM) for value in values]


def run_copies(pairs, sems):
    copies = [pltpu.make_async_copy(a, b, sems.at[i]) for i, (a, b) in enumerate(pairs)]
    for copy in copies:
        copy.start()
    for copy in copies:
        copy.wait()


def plane_of(upper, j, slab):
    return jnp.where(upper, slab - 1 - j, j)


def first_kernel(now, cur, sems):
    slab = now.shape[0]
    _, upper = position()
    run_copies([(now.at[plane_of(upper, j, slab)], cur.at[j]) for j in range(slab // 2)], sems)


def first_planes(p_now):
    slab, rows, lanes = p_now.shape
    half = slab // 2
    return pl.pallas_call(
        first_kernel,
        out_shape=shape((half, rows, lanes)),
        in_specs=[HBM],
        out_specs=VMEM,
        scratch_shapes=[pltpu.SemaphoreType.DMA((half,))],
        compiler_params=room(2),
        name="first_planes",
    )(*in_place(p_now))


def setup_kernel(
    count,
    source,
    wavelet_in,
    cells_in,
    observed,
    p_prev,
    velocity,
    density,
    prev,
    cour,
    cour_outer,
    mask,
    dens,
    pulses,
    known,
    edges,
    vel,
    raw,
    wavelet,
    cells,
    sems,
):
    slab = p_prev.shape[0]
    half, rows, lanes = prev.shape
    m, upper = position()
    pairs = []
    for j in range(half):
        plane = plane_of(upper, j, slab)
        pairs += [(p_prev.at[plane], prev.at[j]), (velocity.at[plane], vel.at[j])]
    low = half * (lax.axis_index("station") % 2)
    pairs += [(density.at[pl.ds(low, half)], raw)]
    edge = plane_of(upper, 0, slab)
    pairs += [(velocity.at[edge], edges.at[0]), (density.at[edge], edges.at[1])]
    pairs += [(wavelet_in, wavelet), (cells_in, cells), (observed, known.at[1])]
    run_copies(pairs, sems)
    known[0] = cells[...].astype(F32)
    for n in range(pulses.shape[0]):
        pulses[n : n + 1, :] = jnp.full((1, lanes), wavelet[n], F32)
    outer_ok = jnp.where(upper, m < count - 1, m > 0)
    outer_ok = jnp.where(outer_ok, 1.0, 0.0)
    column, source_lane = divmod_static(source[0], lanes)
    source_x, source_row = divmod_static(column, rows)
    row = lax.broadcasted_iota(jnp.int32, (rows, lanes), 0)
    lane = lax.broadcasted_iota(jnp.int32, (rows, lanes), 1)
    spot = jnp.where((row == source_row) & (lane == source_lane), 1.0, 0.0)
    for j in range(half):
        scaled = TIME_RATIO * vel[j]
        square = scaled * scaled
        cour[j] = square
        cour_outer[j] = square * outer_ok
        here = m * slab + plane_of(upper, j, slab) == source_x
        mask[j] = spot * jnp.where(here, 1.0, 0.0)
        dens[j] = raw[j].astype(jnp.bfloat16).astype(F32)


def setup(count, source_cell, wavelet, cells, observed, p_prev, velocity, density):
    slab, rows, lanes = p_prev.shape
    half = slab // 2
    part = shape((half, rows, lanes))
    held = pltpu.VMEM((half, rows, lanes), F32)
    return pl.pallas_call(
        functools.partial(setup_kernel, count),
        out_shape=(part,) * 5
        + (
            shape((wavelet.shape[0], lanes)),
            shape((2,) + cells.shape),
            shape((2, rows, lanes)),
        ),
        in_specs=[SMEM] + [HBM] * 6,
        out_specs=(VMEM,) * 8,
        scratch_shapes=[
            held,
            held,
            pltpu.SMEM(wavelet.shape, F32),
            pltpu.VMEM(cells.shape, jnp.int32),
            pltpu.SemaphoreType.DMA((2 * half + 6,)),
        ],
        compiler_params=room(4),
        cost_estimate=pl.CostEstimate(
            flops=20 * half * rows * lanes, bytes_accessed=32 * half * rows * lanes, transcendentals=0
        ),
        name="setup",
    )(source_cell, *in_place(wavelet, cells, observed, p_prev, velocity, density))


def local_kernel(step, pulses, mask, cur, prev, cour, surf_in, base, surf, pad):
    planes, rows, lanes = prev.shape
    lane = lax.broadcasted_iota(jnp.int32, (rows, lanes), 1)
    weights = {}
    for d in range(1, REACH + 1):
        weights[d] = jnp.where(lane >= d, STENCIL[d], 0.0)
        weights[-d] = jnp.where(lane < lanes - d, STENCIL[d], 0.0)
    pulse = pulses[step : step + 1, :]
    for j in range(planes):
        pad[j, 0:8, :] = jnp.zeros((8, lanes), F32)
        pad[j, 8 + rows : 16 + rows, :] = jnp.zeros((8, lanes), F32)
        pad[j, 8 : 8 + rows, :] = cur[j]
    for j in range(planes):
        c = cur[j]
        acc = 3.0 * STENCIL[0] * c
        for d in range(1, REACH + 1):
            acc = acc + weights[d] * pltpu.roll(c, d, 1) + weights[-d] * pltpu.roll(c, lanes - d, 1)
            near = pad[j, 8 + d : 8 + d + rows, :] + pad[j, 8 - d : 8 - d + rows, :]
            for i in (j - d, j + d):
                if 0 <= i < planes:
                    near = near + cur[i]
            acc = acc + STENCIL[d] * near
        base[j] = 2.0 * c - prev[j] + cour[j] * acc + pulse * mask[j]
        if step == 0:
            surf[j] = jnp.zeros((rows, lanes), F32)
        else:
            surf[j] = jnp.where(
                lane == step - 1, jnp.broadcast_to(c[:, 0:1], (rows, lanes)), surf_in[j]
            )


def local_step(step, pulses, mask, cur, prev, cour, surf):
    planes, rows, lanes = cur.shape
    return pl.pallas_call(
        functools.partial(local_kernel, step),
        out_shape=(shape(cur.shape), shape(cur.shape)),
        in_specs=[VMEM] * 6,
        out_specs=(VMEM, VMEM),
        scratch_shapes=[pltpu.VMEM((planes, rows + 16, lanes), F32)],
        compiler_params=room(2),
        cost_estimate=pl.CostEstimate(
            flops=60 * cur.size, bytes_accessed=24 * cur.size, transcendentals=0
        ),
        name="wave_local",
    )(pulses, mask, cur, prev, cour, surf)


def halo_kernel(base, cour, cour_outer, outer, inner, out):
    planes = base.shape[0]
    for j in range(planes):
        far = near = None
        for d in range(j + 1, REACH + 1):
            term = STENCIL[d] * outer[d - j - 1]
            far = term if far is None else far + term
        for d in range(planes - j, REACH + 1):
            term = STENCIL[d] * inner[2 * planes - 1 - j - d]
            near = term if near is None else near + term
        out[j] = base[j] + (cour[j] * near + cour_outer[j] * far)


def halo_step(base, cour, cour_outer, outer, inner):
    return pl.pallas_call(
        halo_kernel,
        out_shape=shape(base.shape),
        in_specs=[VMEM] * 5,
        out_specs=VMEM,
        compiler_params=room(2),
        cost_estimate=pl.CostEstimate(
            flops=12 * base.size, bytes_accessed=20 * base.size, transcendentals=0
        ),
        name="wave_halo",
    )(base, cour, cour_outer, outer, inner)


def trace_kernel(step, place, cur, surf, out):
    planes, rows, lanes = cur.shape
    receivers = place.shape[1]
    steps = step + 1
    lane = lax.broadcasted_iota(jnp.int32, (rows, lanes), 1)
    columns = jnp.concatenate(
        [
            jnp.where(lane == step, jnp.broadcast_to(cur[j, :, 0:1], (rows, lanes)), surf[j])
            for j in range(planes)
        ],
        0,
    )
    columns = columns.T
    spot = lax.broadcasted_iota(jnp.int32, (planes * rows, receivers), 0)
    pick = jnp.where(place[...] == spot, 1.0, 0.0).astype(jnp.bfloat16)
    total = None
    for _ in range(3):
        part = columns.astype(jnp.bfloat16)
        columns = columns - part.astype(F32)
        term = jnp.dot(part, pick, preferred_element_type=F32)
        total = term if total is None else total + term
    for b in range(receivers // 128):
        out[b * steps : (b + 1) * steps, :] = total[:steps, b * 128 : (b + 1) * 128]


def recorded_traces(step, place, cur, surf):
    return pl.pallas_call(
        functools.partial(trace_kernel, step),
        out_shape=shape(((step + 1) * (place.shape[1] // 128), 128)),
        in_specs=[VMEM] * 3,
        out_specs=VMEM,
        compiler_params=room(4),
        name="traces",
    )(place, cur, surf)


def join_kernel(own, sibling, out, sems):
    slab = out.shape[0]
    _, upper = position()
    pairs = []
    for j in range(slab // 2):
        here = plane_of(upper, j, slab)
        pairs += [(own.at[j], out.at[here]), (sibling.at[j], out.at[slab - 1 - here])]
    run_copies(pairs, sems)


def join(own, sibling):
    half, rows, lanes = own.shape
    return pl.pallas_call(
        join_kernel,
        out_shape=shape((2 * half, rows, lanes)),
        in_specs=[VMEM] * 2,
        out_specs=HBM,
        scratch_shapes=[pltpu.SemaphoreType.DMA((2 * half,))],
        compiler_params=room(2),
        name="join",
    )(own, sibling)


def on_chip(value):
    return pltpu.with_memory_space_constraint(value, pltpu.VMEM)


def table_low(total_x, slab, offset):
    m, _ = position()
    return m * slab - (total_x - 1) + offset


def table_kernel(total_x, slab, spread, head, out):
    lanes = out.shape[1]
    low = table_low(total_x, slab, head[0])
    dy = (lax.broadcasted_iota(jnp.int32, (spread, lanes), 0) - (spread // 2 - 1)).astype(F32)
    dz = (lax.broadcasted_iota(jnp.int32, (spread, lanes), 1) + 1).astype(F32)
    side = dy * dy
    deep = dz * dz

    def one(t, carry):
        dx = (t + low).astype(F32)
        inverse = lax.rsqrt(dx * dx + side + deep)
        value = dz * (inverse * inverse * inverse)
        start = pl.multiple_of(t * spread, spread)
        out[pl.ds(start, spread), :] = value.astype(jnp.bfloat16).astype(F32)
        return carry

    lax.fori_loop(0, out.shape[0] // spread, one, 0)


def gravity_table(total_x, slab, depth, lateral, vertical, head):
    size = depth * 2 * lateral * vertical
    return pl.pallas_call(
        functools.partial(table_kernel, total_x, slab, 2 * lateral),
        out_shape=shape((depth * 2 * lateral, vertical)),
        in_specs=[SMEM],
        out_specs=VMEM,
        cost_estimate=pl.CostEstimate(
            flops=20 * size, bytes_accessed=4 * size, transcendentals=2 * size
        ),
        compiler_params=room(8),
        name="gravity_table",
    )(head)


def forward_kernel(first, guard, total_x, lateral, head, table, dens, out):
    planes, rows, _ = dens.shape
    count = out.shape[0]
    spread = 2 * lateral
    core = lax.axis_index("station") % 2
    lead = total_x - 1 - head[0]
    if guard:
        out[...] = jnp.zeros_like(out)

    def one(s, carry):
        sx, sy = divmod_static(head[1 + first + s], lateral)
        shift = lead - sx
        start = (shift + core * planes) * spread + (lateral - 1 - sy)

        def accumulate():
            acc = None
            for p in range(planes):
                term = table[pl.ds(start + p * spread, rows), :] * dens[p]
                acc = term if acc is None else acc + term
            out[pl.ds(s, 1), :] = jnp.sum(acc, axis=0, keepdims=True)

        if guard:
            pl.when((shift >= 0) & (shift < guard))(accumulate)
        else:
            accumulate()
        return carry

    lax.fori_loop(0, count, one, 0, unroll=8)


def gravity_forward(first, count, guard, total_x, lateral, head, table, dens):
    work = count * dens.size
    return pl.pallas_call(
        functools.partial(forward_kernel, first, guard, total_x, lateral),
        out_shape=shape((count, dens.shape[2])),
        in_specs=[SMEM, VMEM, VMEM],
        out_specs=VMEM,
        cost_estimate=pl.CostEstimate(
            flops=4 * work, bytes_accessed=4 * dens.size, transcendentals=0
        ),
        compiler_params=room(8),
        name="gravity_forward",
    )(head, on_chip(table), dens)


def adjoint_kernel(lines, guard, total_x, lateral, head, weights, table, start_at, out):
    slab, rows, _ = out.shape
    spread = 2 * lateral
    lead = total_x - 1 - head[0]
    row_low = lax.axis_index("station") * rows

    def one(k, i, acc):
        sx, sy = divmod_static(head[1 + 128 * k + i], lateral)
        shift = lead - sx
        weight = weights[k, i]
        if guard:
            keep = (shift >= 0) & (shift < guard)
            shift = jnp.where(keep, shift, 0)
            weight = jnp.where(keep, weight, 0.0)
        start = shift * spread + (lateral - 1 - sy + row_low)
        return tuple(
            acc[x] + weight * table[pl.ds(start + x * spread, rows), :] for x in range(slab)
        )

    acc = tuple(start_at[x] for x in range(slab))
    for k in lines:
        acc = lax.fori_loop(0, 128, functools.partial(one, k), acc, unroll=16)
    for x in range(slab):
        out[x] = acc[x]


def gravity_adjoint(lines, guard, total_x, lateral, head, weights, table, start_at):
    return pl.pallas_call(
        functools.partial(adjoint_kernel, lines, guard, total_x, lateral),
        out_shape=shape(start_at.shape),
        in_specs=[SMEM, SMEM, VMEM, VMEM],
        out_specs=VMEM,
        cost_estimate=pl.CostEstimate(
            flops=256 * len(lines) * start_at.size, bytes_accessed=8 * start_at.size, transcendentals=0
        ),
        compiler_params=room(8),
        name="gravity_adjoint",
    )(head, weights, table, start_at)


def small_call(kernel, outs, *values):
    single = not isinstance(outs, tuple)
    return pl.pallas_call(
        kernel,
        out_shape=outs,
        in_specs=[VMEM] * len(values),
        out_specs=VMEM if single else (VMEM,) * len(outs),
        compiler_params=room(2),
    )(*values)


def sum_kernel(first, second, out):
    out[...] = first[...] + second[...]


def plus(first, second):
    return small_call(sum_kernel, shape(first.shape), first, second)


def unpack_kernel(packed, other, out):
    steps, receivers = out.shape
    for b in range(receivers // 128):
        rows = slice(b * steps, (b + 1) * steps)
        out[:, b * 128 : (b + 1) * 128] = packed[rows, :] + other[rows, :]


def predict_kernel(*refs):
    pieces, out = refs[:-1], refs[-1]
    sums = jnp.concatenate([piece[...] for piece in pieces], 0)
    for k in range(out.shape[0]):
        out[k : k + 1, :] = jnp.sum(sums[k * 128 : (k + 1) * 128, :].T, axis=0, keepdims=True)


def residual_kernel(packed, other, observed, weights, own):
    residual = packed[...] + other[...] - observed[...]
    weights[...] = residual.astype(jnp.bfloat16).astype(F32)
    mine = own.shape[0]
    for k in range(residual.shape[0] // mine):

        @pl.when(lax.axis_index("station") == k)
        def _(k=k):
            own[...] = residual[k * mine : (k + 1) * mine, :]


def cross_kernel(count, velocity, density, outer, inner, out):
    slab, rows, lanes = velocity.shape
    lane = lax.broadcasted_iota(jnp.int32, (rows, lanes), 1)
    row = lax.broadcasted_iota(jnp.int32, (rows, lanes), 0)
    m, flipped = position()
    left_ok = jnp.where(m > 0, 0.5, 0.0)
    right_ok = jnp.where(m < count - 1, 0.5, 0.0)

    def slopes(field, side, x):
        f = field[x]
        if x > 0:
            below = 0.5 * field[x - 1]
        else:
            below = left_ok * jnp.where(flipped, inner[side], outer[side])
        if x < slab - 1:
            above = 0.5 * field[x + 1]
        else:
            above = right_ok * jnp.where(flipped, outer[side], inner[side])
        up = jnp.where(row < rows - 1, pltpu.roll(f, rows - 1, 0), 0.0)
        down = jnp.where(row > 0, pltpu.roll(f, 1, 0), 0.0)
        ahead = jnp.where(lane < lanes - 1, pltpu.roll(f, lanes - 1, 1), 0.0)
        back = jnp.where(lane > 0, pltpu.roll(f, 1, 1), 0.0)
        return above - below, (up - down) * 0.5, (ahead - back) * 0.5

    for x in range(slab):
        v = slopes(velocity, 0, x)
        q = slopes(density, 1, x)
        out[0, x] = v[1] * q[2] - v[2] * q[1]
        out[1, x] = v[2] * q[0] - v[0] * q[2]
        out[2, x] = v[0] * q[1] - v[1] * q[0]


def cross_gradient_of(count, velocity, density, outer, inner):
    return pl.pallas_call(
        functools.partial(cross_kernel, count),
        out_shape=shape((3,) + velocity.shape),
        in_specs=[VMEM] * 4,
        out_specs=VMEM,
        cost_estimate=pl.CostEstimate(
            flops=60 * velocity.size, bytes_accessed=24 * velocity.size, transcendentals=0
        ),
        compiler_params=room(8),
        name="cross_gradient",
    )(velocity, density, outer, inner)


def per_device(
    p_now, p_prev, velocity, density, wavelet, source_cell, receiver_cells, station_cells, observed
):
    slab, lateral, vertical = p_now.shape
    count = lax.axis_size("mp")
    stations = lax.axis_size("station")
    steps = wavelet.shape[0]
    half = slab // 2
    assert half == REACH and count % 2 == 0 and stations % 4 == 0
    total_x = slab * count
    m, upper = position()
    s = lax.axis_index("station")
    block = lateral // stations
    chain = pairs_of(count, stations, chain_partner(count))
    together = lax.optimization_barrier

    def across(value):
        return lax.ppermute(value, AXES, chain)

    def swap(value, slab_bit, station_bit):
        pairs = pairs_of(count, stations, lambda i, k: (i ^ slab_bit, k ^ station_bit))
        return lax.ppermute(value, AXES, pairs)

    cur = first_planes(p_now)
    outer = across(cur)
    inner = swap(cur, 0, 1)
    prev, cour, cour_outer, mask, dens, pulses, known, edges = setup(
        count,
        source_cell,
        wavelet,
        station_cells.reshape(-1, 128),
        observed.reshape(-1, 128),
        p_prev,
        velocity,
        density,
    )

    receiver_x, receiver_y = divmod_static(receiver_cells, lateral)
    receiver_j = receiver_x - m * slab
    receiver_j = jnp.where(upper, slab - 1 - receiver_j, receiver_j)
    inside = (receiver_j >= 0) & (receiver_j < half)
    place = jnp.where(inside, receiver_j * lateral + receiver_y, -1)[None, :]

    reach = min(total_x, 64)
    chunks = -(-total_x // reach)
    span = reach + slab - 1
    own_stations = station_cells.shape[0]
    n_stations = own_stations * stations

    def head_of(offset, cells):
        return jnp.concatenate([jnp.reshape(offset, (1,)).astype(jnp.int32), cells])

    def table_of(head):
        return gravity_table(total_x, slab, span, lateral, vertical, head)

    state = {"known": known, "edges": edges}

    def merged(gate):
        if "pending" not in state:
            return gate(state["known"])
        known, other, bit = state.pop("pending")
        other = gate(other)
        upper = (s // bit) % 2 == 1
        pair = [jnp.where(upper, other, known), jnp.where(upper, known, other)]
        state["known"] = jnp.concatenate(pair, 1)
        return state["known"]

    def exchange(bit):
        def work(gate):
            known = merged(gate)
            state["pending"] = known, swap(known, 0, bit), bit

        return work

    def send_edges(gate):
        state["outer"] = across(gate(state["edges"]))

    def share_edges(gate):
        state["inner"] = swap(gate(state["outer"]), 0, 1)

    def cross(gate):
        state["cross"] = cross_gradient_of(
            count, velocity, density, state["outer"], gate(state["inner"])
        )
        return "cross"

    lines = n_stations // 128

    def build_table(gate):
        known = merged(gate)
        cells = known[0].reshape(-1).astype(jnp.int32)
        head = head_of(0, cells)
        zero, head, observed_all, where = together(
            (jnp.zeros((1,), jnp.int32), head, known[1].reshape(-1, 128), place)
        )
        state.update(head=head, observed=observed_all, place=where)
        state["table"] = table_of(zero)
        return "table"

    pieces = 5
    part = n_stations * 7 // 256 * 8

    def forward(i):
        def work(gate):
            size = part if i < pieces - 1 else n_stations - i * part
            state[i] = gravity_forward(
                i * part, size, 0, total_x, lateral, gate(state["head"]), state["table"], dens
            )
            return i

        return work

    def predict(gate):
        sums = [state[i] for i in range(pieces)]
        sums[0] = gate(sums[0])
        packed = small_call(predict_kernel, shape((lines, 128)), *sums)
        state["packed"], state["other"] = packed, swap(packed, 0, 1)

    def add_up(bit):
        def work(gate):
            packed = plus(gate(state["packed"]), state["other"])
            state["packed"], state["other"] = packed, swap(packed, bit, 1)

        return work

    def residual(gate):
        state["weights"], state["own"] = small_call(
            residual_kernel,
            (shape((lines, 128)), shape((lines // stations, 128))),
            gate(state["packed"]),
            state["other"],
            state["observed"],
        )
        state["gradient"] = jnp.zeros((slab, block, vertical), F32)
        return "weights"

    def adjoint(half_lines):
        def work(gate):
            state["gradient"] = gravity_adjoint(
                half_lines,
                0,
                total_x,
                lateral,
                state["head"],
                gate(state["weights"]),
                state["table"],
                state["gradient"],
            )
            return "gradient"

        return work

    def both(first, second):
        def work(gate):
            first(gate)
            return second(gate)

        return work

    hidden = chunks == 1 and count & (count - 1) == 0
    jobs = [exchange(1 << b) for b in range(stations.bit_length() - 1)]
    if hidden:
        jobs += [build_table] + [forward(i) for i in range(pieces - 1)]
        jobs += [both(share_edges, forward(pieces - 1)), both(predict, cross)]
        jobs += [add_up(1 << b) for b in range(count.bit_length() - 1)]
        quarter = lines // 4
        jobs += [both(residual, adjoint(range(quarter)))]
        jobs += [adjoint(range(quarter, 3 * quarter)), adjoint(range(3 * quarter, lines))]
    jobs[0] = both(send_edges, jobs[0])
    if not hidden:
        jobs += [share_edges, cross]
    assert len(jobs) < steps

    surf = cour
    for step in range(steps):
        if step:
            outer = across(cur)
            inner = swap(cur, 0, 1)
        base, surf = local_step(step, pulses, mask, cur, prev, cour, surf)

        def gate(value):
            nonlocal base
            base, value = together((base, value))
            return value

        ready = None
        if step and jobs:
            ready = jobs.pop(0)(gate)
        cur, prev = halo_step(base, cour, cour_outer, outer, inner), cur
        if ready is not None:
            cur, state[ready] = together((cur, state[ready]))

    sibling = swap(cur, 0, 1)
    packed = recorded_traces(steps - 1, state.get("place", place), cur, surf)
    other = swap(packed, 0, 1)
    if count & (count - 1) == 0:
        bit = 1
        while bit < count:
            packed = plus(packed, other)
            other = swap(packed, bit, 1)
            if bit == 1:
                wavefield = join(cur, sibling)
            if bit == 2:
                other, wavefield = together((other, wavefield))
            bit *= 2
    else:
        wavefield = join(cur, sibling)
        packed = lax.psum(packed + other, "mp")
        other = jnp.zeros_like(packed)
    traces = small_call(unpack_kernel, shape((steps, receiver_cells.shape[0])), packed, other)
    if hidden:
        gravity_residual = state["own"].reshape(-1)
        density_gradient = state["gradient"]
    else:
        known = merged(lambda value: value)
        cells = known[0].reshape(-1).astype(jnp.int32)

        def add_chunk(i, total):
            head = head_of(i * reach, cells)
            return total + gravity_forward(
                0, n_stations, reach, total_x, lateral, head, table_of(head[:1]), dens
            )

        sums = lax.fori_loop(0, chunks, add_chunk, jnp.zeros((n_stations, vertical), F32))
        predicted = jnp.sum(sums, axis=1)
        predicted = lax.psum(predicted + swap(predicted, 0, 1), "mp")
        difference = predicted - known[1].reshape(-1)
        gravity_residual = lax.dynamic_slice(difference, (s * own_stations,), (own_stations,))
        weights = difference.astype(jnp.bfloat16).astype(F32).reshape(-1, 128)

        def back_chunk(i, total):
            head = head_of(i * reach, cells)
            return gravity_adjoint(
                range(lines), reach, total_x, lateral, head, weights, table_of(head[:1]), total
            )

        density_gradient = lax.fori_loop(
            0, chunks, back_chunk, jnp.zeros((slab, block, vertical), F32)
        )
    return (wavefield, traces, gravity_residual, density_gradient, state["cross"])


def solution(mesh):
    in_specs = (
        P("mp", None, None),
        P("mp", None, None),
        P("mp", None, None),
        P("mp", None, None),
        P(),
        P(),
        P(),
        P("station"),
        P("station"),
    )
    out_specs = (
        P("mp", None, None),
        P(),
        P("station"),
        P("mp", "station", None),
        P(None, "mp", None, None),
    )

    return jax.shard_map(
        per_device, mesh=mesh, in_specs=in_specs, out_specs=out_specs, check_vma=False
    )
```

```python
import functools

import jax
import jax.numpy as jnp
from jax import lax
from jax.experimental import pallas as pl
from jax.experimental.pallas import tpu as pltpu
from jax.sharding import PartitionSpec as P


STENCIL = (-205.0 / 72.0, 8.0 / 5.0, -1.0 / 5.0, 8.0 / 315.0, -1.0 / 560.0)
TIME_RATIO = 0.1
REACH = 4
AXES = ("mp", "station")
VMEM = pl.BlockSpec(memory_space=pltpu.VMEM)
SMEM = pl.BlockSpec(memory_space=pltpu.SMEM)
HBM = pl.BlockSpec(memory_space=pltpu.HBM)
F32 = jnp.float32
MIB = 1 << 20


def room(mib):
    return pltpu.CompilerParams(vmem_limit_bytes=mib * MIB)


def shape(dims):
    return jax.ShapeDtypeStruct(dims, F32)


def pairs_of(count, stations, partner):
    return [
        (m * stations + s, (lambda t: t[0] * stations + t[1])(partner(m, s)))
        for m in range(count)
        for s in range(stations)
    ]


def chain_partner(count):
    def partner(m, s):
        if s % 2 == 0:
            return (m ^ 1, s)
        other = m + 1 if m % 2 else m - 1
        if other < 0 or other >= count:
            return (m, s ^ 2)
        return (other, s)

    return partner


def position():
    m = lax.axis_index("mp")
    return m, (m + lax.axis_index("station")) % 2 == 0


def divmod_static(value, divisor):
    if divisor & (divisor - 1) == 0:
        return value >> (divisor.bit_length() - 1), value & (divisor - 1)
    return value // divisor, value % divisor


def in_place(*values):
    return [pltpu.with_memory_space_constraint(value, pltpu.HBM) for value in values]


def run_copies(pairs, sems):
    copies = [pltpu.make_async_copy(a, b, sems.at[i]) for i, (a, b) in enumerate(pairs)]
    for copy in copies:
        copy.start()
    for copy in copies:
        copy.wait()


def plane_of(upper, j, slab):
    return jnp.where(upper, slab - 1 - j, j)


def first_kernel(now, cur, sems):
    slab = now.shape[0]
    _, upper = position()
    run_copies([(now.at[plane_of(upper, j, slab)], cur.at[j]) for j in range(slab // 2)], sems)


def first_planes(p_now):
    slab, rows, lanes = p_now.shape
    half = slab // 2
    return pl.pallas_call(
        first_kernel,
        out_shape=shape((half, rows, lanes)),
        in_specs=[HBM],
        out_specs=VMEM,
        scratch_shapes=[pltpu.SemaphoreType.DMA((half,))],
        compiler_params=room(2),
        name="first_planes",
    )(*in_place(p_now))


def setup_kernel(
    count,
    source,
    wavelet_in,
    cells_in,
    observed,
    p_prev,
    velocity,
    density,
    prev,
    cour,
    cour_outer,
    mask,
    dens,
    pulses,
    known,
    edges,
    vel,
    raw,
    wavelet,
    cells,
    sems,
):
    slab = p_prev.shape[0]
    half, rows, lanes = prev.shape
    m, upper = position()
    pairs = []
    for j in range(half):
        plane = plane_of(upper, j, slab)
        pairs += [(p_prev.at[plane], prev.at[j]), (velocity.at[plane], vel.at[j])]
    low = half * (lax.axis_index("station") % 2)
    pairs += [(density.at[pl.ds(low, half)], raw)]
    edge = plane_of(upper, 0, slab)
    pairs += [(velocity.at[edge], edges.at[0]), (density.at[edge], edges.at[1])]
    pairs += [(wavelet_in, wavelet), (cells_in, cells), (observed, known.at[1])]
    run_copies(pairs, sems)
    known[0] = cells[...].astype(F32)
    for n in range(pulses.shape[0]):
        pulses[n : n + 1, :] = jnp.full((1, lanes), wavelet[n], F32)
    outer_ok = jnp.where(upper, m < count - 1, m > 0)
    outer_ok = jnp.where(outer_ok, 1.0, 0.0)
    column, source_lane = divmod_static(source[0], lanes)
    source_x, source_row = divmod_static(column, rows)
    row = lax.broadcasted_iota(jnp.int32, (rows, lanes), 0)
    lane = lax.broadcasted_iota(jnp.int32, (rows, lanes), 1)
    spot = jnp.where((row == source_row) & (lane == source_lane), 1.0, 0.0)
    for j in range(half):
        scaled = TIME_RATIO * vel[j]
        square = scaled * scaled
        cour[j] = square
        cour_outer[j] = square * outer_ok
        here = m * slab + plane_of(upper, j, slab) == source_x
        mask[j] = spot * jnp.where(here, 1.0, 0.0)
        dens[j] = raw[j].astype(jnp.bfloat16).astype(F32)


def setup(count, source_cell, wavelet, cells, observed, p_prev, velocity, density):
    slab, rows, lanes = p_prev.shape
    half = slab // 2
    part = shape((half, rows, lanes))
    held = pltpu.VMEM((half, rows, lanes), F32)
    return pl.pallas_call(
        functools.partial(setup_kernel, count),
        out_shape=(part,) * 5
        + (
            shape((wavelet.shape[0], lanes)),
            shape((2,) + cells.shape),
            shape((2, rows, lanes)),
        ),
        in_specs=[SMEM] + [HBM] * 6,
        out_specs=(VMEM,) * 8,
        scratch_shapes=[
            held,
            held,
            pltpu.SMEM(wavelet.shape, F32),
            pltpu.VMEM(cells.shape, jnp.int32),
            pltpu.SemaphoreType.DMA((2 * half + 6,)),
        ],
        compiler_params=room(4),
        cost_estimate=pl.CostEstimate(
            flops=20 * half * rows * lanes, bytes_accessed=32 * half * rows * lanes, transcendentals=0
        ),
        name="setup",
    )(source_cell, *in_place(wavelet, cells, observed, p_prev, velocity, density))


def local_kernel(step, pulses, mask, cur, prev, cour, surf_in, base, surf, pad):
    planes, rows, lanes = prev.shape
    lane = lax.broadcasted_iota(jnp.int32, (rows, lanes), 1)
    weights = {}
    for d in range(1, REACH + 1):
        weights[d] = jnp.where(lane >= d, STENCIL[d], 0.0)
        weights[-d] = jnp.where(lane < lanes - d, STENCIL[d], 0.0)
    pulse = pulses[step : step + 1, :]
    for j in range(planes):
        pad[j, 0:8, :] = jnp.zeros((8, lanes), F32)
        pad[j, 8 + rows : 16 + rows, :] = jnp.zeros((8, lanes), F32)
        pad[j, 8 : 8 + rows, :] = cur[j]
    for j in range(planes):
        c = cur[j]
        acc = 3.0 * STENCIL[0] * c
        for d in range(1, REACH + 1):
            acc = acc + weights[d] * pltpu.roll(c, d, 1) + weights[-d] * pltpu.roll(c, lanes - d, 1)
            near = pad[j, 8 + d : 8 + d + rows, :] + pad[j, 8 - d : 8 - d + rows, :]
            for i in (j - d, j + d):
                if 0 <= i < planes:
                    near = near + cur[i]
            acc = acc + STENCIL[d] * near
        base[j] = 2.0 * c - prev[j] + cour[j] * acc + pulse * mask[j]
        if step == 0:
            surf[j] = jnp.zeros((rows, lanes), F32)
        else:
            surf[j] = jnp.where(
                lane == step - 1, jnp.broadcast_to(c[:, 0:1], (rows, lanes)), surf_in[j]
            )


def local_step(step, pulses, mask, cur, prev, cour, surf):
    planes, rows, lanes = cur.shape
    return pl.pallas_call(
        functools.partial(local_kernel, step),
        out_shape=(shape(cur.shape), shape(cur.shape)),
        in_specs=[VMEM] * 6,
        out_specs=(VMEM, VMEM),
        scratch_shapes=[pltpu.VMEM((planes, rows + 16, lanes), F32)],
        compiler_params=room(2),
        cost_estimate=pl.CostEstimate(
            flops=60 * cur.size, bytes_accessed=24 * cur.size, transcendentals=0
        ),
        name="wave_local",
    )(pulses, mask, cur, prev, cour, surf)


def halo_kernel(base, cour, cour_outer, outer, inner, out):
    planes = base.shape[0]
    for j in range(planes):
        far = near = None
        for d in range(j + 1, REACH + 1):
            term = STENCIL[d] * outer[d - j - 1]
            far = term if far is None else far + term
        for d in range(planes - j, REACH + 1):
            term = STENCIL[d] * inner[2 * planes - 1 - j - d]
            near = term if near is None else near + term
        out[j] = base[j] + (cour[j] * near + cour_outer[j] * far)


def halo_step(base, cour, cour_outer, outer, inner):
    return pl.pallas_call(
        halo_kernel,
        out_shape=shape(base.shape),
        in_specs=[VMEM] * 5,
        out_specs=VMEM,
        compiler_params=room(2),
        cost_estimate=pl.CostEstimate(
            flops=12 * base.size, bytes_accessed=20 * base.size, transcendentals=0
        ),
        name="wave_halo",
    )(base, cour, cour_outer, outer, inner)


def trace_kernel(step, place, cur, surf, out):
    planes, rows, lanes = cur.shape
    receivers = place.shape[1]
    steps = step + 1
    lane = lax.broadcasted_iota(jnp.int32, (rows, lanes), 1)
    columns = jnp.concatenate(
        [
            jnp.where(lane == step, jnp.broadcast_to(cur[j, :, 0:1], (rows, lanes)), surf[j])
            for j in range(planes)
        ],
        0,
    )
    columns = columns.T
    spot = lax.broadcasted_iota(jnp.int32, (planes * rows, receivers), 0)
    pick = jnp.where(place[...] == spot, 1.0, 0.0).astype(jnp.bfloat16)
    total = None
    for _ in range(3):
        part = columns.astype(jnp.bfloat16)
        columns = columns - part.astype(F32)
        term = jnp.dot(part, pick, preferred_element_type=F32)
        total = term if total is None else total + term
    for b in range(receivers // 128):
        out[b * steps : (b + 1) * steps, :] = total[:steps, b * 128 : (b + 1) * 128]


def recorded_traces(step, place, cur, surf):
    return pl.pallas_call(
        functools.partial(trace_kernel, step),
        out_shape=shape(((step + 1) * (place.shape[1] // 128), 128)),
        in_specs=[VMEM] * 3,
        out_specs=VMEM,
        compiler_params=room(4),
        name="traces",
    )(place, cur, surf)


def join_kernel(own, sibling, out, sems):
    slab = out.shape[0]
    _, upper = position()
    pairs = []
    for j in range(slab // 2):
        here = plane_of(upper, j, slab)
        pairs += [(own.at[j], out.at[here]), (sibling.at[j], out.at[slab - 1 - here])]
    run_copies(pairs, sems)


def join(own, sibling):
    half, rows, lanes = own.shape
    return pl.pallas_call(
        join_kernel,
        out_shape=shape((2 * half, rows, lanes)),
        in_specs=[VMEM] * 2,
        out_specs=HBM,
        scratch_shapes=[pltpu.SemaphoreType.DMA((2 * half,))],
        compiler_params=room(2),
        name="join",
    )(own, sibling)


def on_chip(value):
    return pltpu.with_memory_space_constraint(value, pltpu.VMEM)


def table_low(total_x, slab, offset):
    m, _ = position()
    return m * slab - (total_x - 1) + offset


def table_kernel(total_x, slab, spread, head, out):
    lanes = out.shape[1]
    low = table_low(total_x, slab, head[0])
    dy = (lax.broadcasted_iota(jnp.int32, (spread, lanes), 0) - (spread // 2 - 1)).astype(F32)
    dz = (lax.broadcasted_iota(jnp.int32, (spread, lanes), 1) + 1).astype(F32)
    side = dy * dy
    deep = dz * dz

    def one(t, carry):
        dx = (t + low).astype(F32)
        inverse = lax.rsqrt(dx * dx + side + deep)
        value = dz * (inverse * inverse * inverse)
        start = pl.multiple_of(t * spread, spread)
        out[pl.ds(start, spread), :] = value.astype(jnp.bfloat16).astype(F32)
        return carry

    lax.fori_loop(0, out.shape[0] // spread, one, 0)


def gravity_table(total_x, slab, depth, lateral, vertical, head):
    size = depth * 2 * lateral * vertical
    return pl.pallas_call(
        functools.partial(table_kernel, total_x, slab, 2 * lateral),
        out_shape=shape((depth * 2 * lateral, vertical)),
        in_specs=[SMEM],
        out_specs=VMEM,
        cost_estimate=pl.CostEstimate(
            flops=20 * size, bytes_accessed=4 * size, transcendentals=2 * size
        ),
        compiler_params=room(8),
        name="gravity_table",
    )(head)


def forward_kernel(first, guard, total_x, lateral, head, table, dens, out):
    planes, rows, _ = dens.shape
    count = out.shape[0]
    spread = 2 * lateral
    core = lax.axis_index("station") % 2
    lead = total_x - 1 - head[0]
    if guard:
        out[...] = jnp.zeros_like(out)

    def one(s, carry):
        sx, sy = divmod_static(head[1 + first + s], lateral)
        shift = lead - sx
        start = (shift + core * planes) * spread + (lateral - 1 - sy)

        def accumulate():
            acc = None
            for p in range(planes):
                term = table[pl.ds(start + p * spread, rows), :] * dens[p]
                acc = term if acc is None else acc + term
            out[pl.ds(s, 1), :] = jnp.sum(acc, axis=0, keepdims=True)

        if guard:
            pl.when((shift >= 0) & (shift < guard))(accumulate)
        else:
            accumulate()
        return carry

    lax.fori_loop(0, count, one, 0, unroll=8)


def gravity_forward(first, count, guard, total_x, lateral, head, table, dens):
    work = count * dens.size
    return pl.pallas_call(
        functools.partial(forward_kernel, first, guard, total_x, lateral),
        out_shape=shape((count, dens.shape[2])),
        in_specs=[SMEM, VMEM, VMEM],
        out_specs=VMEM,
        cost_estimate=pl.CostEstimate(
            flops=4 * work, bytes_accessed=4 * dens.size, transcendentals=0
        ),
        compiler_params=room(8),
        name="gravity_forward",
    )(head, on_chip(table), dens)


def adjoint_kernel(lines, guard, total_x, lateral, head, weights, table, start_at, out):
    slab, rows, _ = out.shape
    spread = 2 * lateral
    lead = total_x - 1 - head[0]
    row_low = lax.axis_index("station") * rows

    def one(k, i, acc):
        sx, sy = divmod_static(head[1 + 128 * k + i], lateral)
        shift = lead - sx
        weight = weights[k, i]
        if guard:
            keep = (shift >= 0) & (shift < guard)
            shift = jnp.where(keep, shift, 0)
            weight = jnp.where(keep, weight, 0.0)
        start = shift * spread + (lateral - 1 - sy + row_low)
        return tuple(
            acc[x] + weight * table[pl.ds(start + x * spread, rows), :] for x in range(slab)
        )

    acc = tuple(start_at[x] for x in range(slab))
    for k in lines:
        acc = lax.fori_loop(0, 128, functools.partial(one, k), acc, unroll=16)
    for x in range(slab):
        out[x] = acc[x]


def gravity_adjoint(lines, guard, total_x, lateral, head, weights, table, start_at):
    return pl.pallas_call(
        functools.partial(adjoint_kernel, lines, guard, total_x, lateral),
        out_shape=shape(start_at.shape),
        in_specs=[SMEM, SMEM, VMEM, VMEM],
        out_specs=VMEM,
        cost_estimate=pl.CostEstimate(
            flops=256 * len(lines) * start_at.size, bytes_accessed=8 * start_at.size, transcendentals=0
        ),
        compiler_params=room(8),
        name="gravity_adjoint",
    )(head, weights, table, start_at)


def small_call(kernel, outs, *values):
    single = not isinstance(outs, tuple)
    return pl.pallas_call(
        kernel,
        out_shape=outs,
        in_specs=[VMEM] * len(values),
        out_specs=VMEM if single else (VMEM,) * len(outs),
        compiler_params=room(2),
    )(*values)


def sum_kernel(first, second, out):
    out[...] = first[...] + second[...]


def plus(first, second):
    return small_call(sum_kernel, shape(first.shape), first, second)


def unpack_kernel(packed, other, out):
    steps, receivers = out.shape
    for b in range(receivers // 128):
        rows = slice(b * steps, (b + 1) * steps)
        out[:, b * 128 : (b + 1) * 128] = packed[rows, :] + other[rows, :]


def predict_kernel(*refs):
    pieces, out = refs[:-1], refs[-1]
    sums = jnp.concatenate([piece[...] for piece in pieces], 0)
    for k in range(out.shape[0]):
        out[k : k + 1, :] = jnp.sum(sums[k * 128 : (k + 1) * 128, :].T, axis=0, keepdims=True)


def residual_kernel(packed, other, observed, weights, own):
    residual = packed[...] + other[...] - observed[...]
    weights[...] = residual.astype(jnp.bfloat16).astype(F32)
    mine = own.shape[0]
    for k in range(residual.shape[0] // mine):

        @pl.when(lax.axis_index("station") == k)
        def _(k=k):
            own[...] = residual[k * mine : (k + 1) * mine, :]


def cross_kernel(count, velocity, density, outer, inner, out):
    slab, rows, lanes = velocity.shape
    lane = lax.broadcasted_iota(jnp.int32, (rows, lanes), 1)
    row = lax.broadcasted_iota(jnp.int32, (rows, lanes), 0)
    m, flipped = position()
    left_ok = jnp.where(m > 0, 0.5, 0.0)
    right_ok = jnp.where(m < count - 1, 0.5, 0.0)

    def slopes(field, side, x):
        f = field[x]
        if x > 0:
            below = 0.5 * field[x - 1]
        else:
            below = left_ok * jnp.where(flipped, inner[side], outer[side])
        if x < slab - 1:
            above = 0.5 * field[x + 1]
        else:
            above = right_ok * jnp.where(flipped, outer[side], inner[side])
        up = jnp.where(row < rows - 1, pltpu.roll(f, rows - 1, 0), 0.0)
        down = jnp.where(row > 0, pltpu.roll(f, 1, 0), 0.0)
        ahead = jnp.where(lane < lanes - 1, pltpu.roll(f, lanes - 1, 1), 0.0)
        back = jnp.where(lane > 0, pltpu.roll(f, 1, 1), 0.0)
        return above - below, (up - down) * 0.5, (ahead - back) * 0.5

    for x in range(slab):
        v = slopes(velocity, 0, x)
        q = slopes(density, 1, x)
        out[0, x] = v[1] * q[2] - v[2] * q[1]
        out[1, x] = v[2] * q[0] - v[0] * q[2]
        out[2, x] = v[0] * q[1] - v[1] * q[0]


def cross_gradient_of(count, velocity, density, outer, inner):
    return pl.pallas_call(
        functools.partial(cross_kernel, count),
        out_shape=shape((3,) + velocity.shape),
        in_specs=[VMEM] * 4,
        out_specs=VMEM,
        cost_estimate=pl.CostEstimate(
            flops=60 * velocity.size, bytes_accessed=24 * velocity.size, transcendentals=0
        ),
        compiler_params=room(8),
        name="cross_gradient",
    )(velocity, density, outer, inner)


def per_device(
    p_now, p_prev, velocity, density, wavelet, source_cell, receiver_cells, station_cells, observed
):
    slab, lateral, vertical = p_now.shape
    count = lax.axis_size("mp")
    stations = lax.axis_size("station")
    steps = wavelet.shape[0]
    half = slab // 2
    assert half == REACH and count % 2 == 0 and stations % 4 == 0
    total_x = slab * count
    m, upper = position()
    s = lax.axis_index("station")
    block = lateral // stations
    chain = pairs_of(count, stations, chain_partner(count))
    together = lax.optimization_barrier

    def across(value):
        return lax.ppermute(value, AXES, chain)

    def swap(value, slab_bit, station_bit):
        pairs = pairs_of(count, stations, lambda i, k: (i ^ slab_bit, k ^ station_bit))
        return lax.ppermute(value, AXES, pairs)

    cur = first_planes(p_now)
    outer = across(cur)
    inner = swap(cur, 0, 1)
    prev, cour, cour_outer, mask, dens, pulses, known, edges = setup(
        count,
        source_cell,
        wavelet,
        station_cells.reshape(-1, 128),
        observed.reshape(-1, 128),
        p_prev,
        velocity,
        density,
    )

    receiver_x, receiver_y = divmod_static(receiver_cells, lateral)
    receiver_j = receiver_x - m * slab
    receiver_j = jnp.where(upper, slab - 1 - receiver_j, receiver_j)
    inside = (receiver_j >= 0) & (receiver_j < half)
    place = jnp.where(inside, receiver_j * lateral + receiver_y, -1)[None, :]

    reach = min(total_x, 64)
    chunks = -(-total_x // reach)
    span = reach + slab - 1
    own_stations = station_cells.shape[0]
    n_stations = own_stations * stations

    def head_of(offset, cells):
        return jnp.concatenate([jnp.reshape(offset, (1,)).astype(jnp.int32), cells])

    def table_of(head):
        return gravity_table(total_x, slab, span, lateral, vertical, head)

    state = {"known": known, "edges": edges}

    def merged(gate):
        if "pending" not in state:
            return gate(state["known"])
        known, other, bit = state.pop("pending")
        other = gate(other)
        upper = (s // bit) % 2 == 1
        pair = [jnp.where(upper, other, known), jnp.where(upper, known, other)]
        state["known"] = jnp.concatenate(pair, 1)
        return state["known"]

    def exchange(bit):
        def work(gate):
            known = merged(gate)
            state["pending"] = known, swap(known, 0, bit), bit

        return work

    def send_edges(gate):
        state["outer"] = across(gate(state["edges"]))

    def share_edges(gate):
        state["inner"] = swap(gate(state["outer"]), 0, 1)

    def cross(gate):
        state["cross"] = cross_gradient_of(
            count, velocity, density, state["outer"], gate(state["inner"])
        )
        return "cross"

    lines = n_stations // 128

    def build_table(gate):
        known = merged(gate)
        cells = known[0].reshape(-1).astype(jnp.int32)
        head = head_of(0, cells)
        zero, head, observed_all, where = together(
            (jnp.zeros((1,), jnp.int32), head, known[1].reshape(-1, 128), place)
        )
        state.update(head=head, observed=observed_all, place=where)
        state["table"] = table_of(zero)
        return "table"

    pieces = 5
    part = -(-n_stations // (8 * pieces)) * 8

    def forward(i):
        def work(gate):
            size = min(part, n_stations - i * part)
            state[i] = gravity_forward(
                i * part, size, 0, total_x, lateral, gate(state["head"]), state["table"], dens
            )
            return i

        return work

    def predict(gate):
        sums = [state[i] for i in range(pieces)]
        sums[0] = gate(sums[0])
        packed = small_call(predict_kernel, shape((lines, 128)), *sums)
        state["packed"], state["other"] = packed, swap(packed, 0, 1)

    def add_up(bit):
        def work(gate):
            packed = plus(gate(state["packed"]), state["other"])
            state["packed"], state["other"] = packed, swap(packed, bit, 1)

        return work

    def residual(gate):
        state["weights"], state["own"] = small_call(
            residual_kernel,
            (shape((lines, 128)), shape((lines // stations, 128))),
            gate(state["packed"]),
            state["other"],
            state["observed"],
        )
        state["gradient"] = jnp.zeros((slab, block, vertical), F32)
        return "weights"

    def adjoint(half_lines):
        def work(gate):
            state["gradient"] = gravity_adjoint(
                half_lines,
                0,
                total_x,
                lateral,
                state["head"],
                gate(state["weights"]),
                state["table"],
                state["gradient"],
            )
            return "gradient"

        return work

    def both(first, second):
        def work(gate):
            first(gate)
            return second(gate)

        return work

    hidden = chunks == 1 and count & (count - 1) == 0
    jobs = [exchange(1 << b) for b in range(stations.bit_length() - 1)]
    if hidden:
        jobs += [build_table] + [forward(i) for i in range(pieces)] + [both(share_edges, predict)]
        stages = [add_up(1 << b) for b in range(count.bit_length() - 1)]
        jobs += [both(stages[0], cross)] + stages[1:]
        quarter = lines // 4
        jobs += [both(residual, adjoint(range(quarter)))]
        jobs += [adjoint(range(quarter, 3 * quarter)), adjoint(range(3 * quarter, lines))]
    jobs[0] = both(send_edges, jobs[0])
    if not hidden:
        jobs += [share_edges, cross]
    assert len(jobs) < steps

    surf = cour
    for step in range(steps):
        if step:
            outer = across(cur)
            inner = swap(cur, 0, 1)
        base, surf = local_step(step, pulses, mask, cur, prev, cour, surf)

        def gate(value):
            nonlocal base
            base, value = together((base, value))
            return value

        ready = None
        if step and jobs:
            ready = jobs.pop(0)(gate)
        cur, prev = halo_step(base, cour, cour_outer, outer, inner), cur
        if ready is not None:
            cur, state[ready] = together((cur, state[ready]))

    sibling = swap(cur, 0, 1)
    packed = recorded_traces(steps - 1, state.get("place", place), cur, surf)
    other = swap(packed, 0, 1)
    if count & (count - 1) == 0:
        bit = 1
        while bit < count:
            packed = plus(packed, other)
            other = swap(packed, bit, 1)
            if bit == 1:
                wavefield = join(cur, sibling)
            if bit == 2:
                other, wavefield = together((other, wavefield))
            bit *= 2
    else:
        wavefield = join(cur, sibling)
        packed = lax.psum(packed + other, "mp")
        other = jnp.zeros_like(packed)
    traces = small_call(unpack_kernel, shape((steps, receiver_cells.shape[0])), packed, other)
    if hidden:
        gravity_residual = state["own"].reshape(-1)
        density_gradient = state["gradient"]
    else:
        known = merged(lambda value: value)
        cells = known[0].reshape(-1).astype(jnp.int32)

        def add_chunk(i, total):
            head = head_of(i * reach, cells)
            return total + gravity_forward(
                0, n_stations, reach, total_x, lateral, head, table_of(head[:1]), dens
            )

        sums = lax.fori_loop(0, chunks, add_chunk, jnp.zeros((n_stations, vertical), F32))
        predicted = jnp.sum(sums, axis=1)
        predicted = lax.psum(predicted + swap(predicted, 0, 1), "mp")
        difference = predicted - known[1].reshape(-1)
        gravity_residual = lax.dynamic_slice(difference, (s * own_stations,), (own_stations,))
        weights = difference.astype(jnp.bfloat16).astype(F32).reshape(-1, 128)

        def back_chunk(i, total):
            head = head_of(i * reach, cells)
            return gravity_adjoint(
                range(lines), reach, total_x, lateral, head, weights, table_of(head[:1]), total
            )

        density_gradient = lax.fori_loop(
            0, chunks, back_chunk, jnp.zeros((slab, block, vertical), F32)
        )
    return (wavefield, traces, gravity_residual, density_gradient, state["cross"])


def solution(mesh):
    in_specs = (
        P("mp", None, None),
        P("mp", None, None),
        P("mp", None, None),
        P("mp", None, None),
        P(),
        P(),
        P(),
        P("station"),
        P("station"),
    )
    out_specs = (
        P("mp", None, None),
        P(),
        P("station"),
        P("mp", "station", None),
        P(None, "mp", None, None),
    )

    return jax.shard_map(
        per_device, mesh=mesh, in_specs=in_specs, out_specs=out_specs, check_vma=False
    )
```
